32 devices in a mesh: dp: 8 (over y, x, core), tensor: 4 (over z).
Axes of the slice: x: 2, y: 2, z: 4, core: 2. Of those that a mesh axis runs over, the one named last changes fastest.
Arguments:
- tokens_in: bfloat16 [16384, 768], P(('dp', 'tensor')), may hold values from -6 to 6
- ln1_gain: float32 [768], replicated, may hold values from 0.25 to 1.75
- ln1_bias: float32 [768], replicated, may hold values from -1.5 to 1.5
- w_qkv: bfloat16 [768, 3, 768], P(None, None, 'tensor'), may hold values from -0.21875 to 0.21875
- b_qkv: float32 [3, 768], P(None, 'tensor'), may hold values from -0.5 to 0.5
- feat_q: bfloat16 [12, 64, 64], P('tensor'), may hold values from -1.5 to 1.5
- feat_k: bfloat16 [12, 64, 64], P('tensor'), may hold values from -1.5 to 1.5
- w_out: bfloat16 [768, 768], P('tensor'), may hold values from -1.75 to 1.75
- b_out: float32 [768], replicated, may hold values from -1.5 to 1.5
- ln2_gain: float32 [768], replicated, may hold values from 0.25 to 1.75
- ln2_bias: float32 [768], replicated, may hold values from -1.5 to 1.5
- w_fc: bfloat16 [768, 3072], P(None, 'tensor'), may hold values from -0.21875 to 0.21875
- b_fc: float32 [3072], P('tensor'), may hold values from -1.5 to 1.5
- w_proj: bfloat16 [3072, 768], P('tensor'), may hold values from -0.109375 to 0.109375
- b_proj: float32 [768], replicated, may hold values from -1.5 to 1.5
- seq_lengths: int32 [8, 2], P('dp'), may hold values from 0 to 2048, as said below
- cotangent: bfloat16 [16384, 768], P(('dp', 'tensor')), may hold values from -6 to 6
Outputs:
- result: bfloat16 [16384, 768], P(('dp', 'tensor'))
- grad_input: bfloat16 [16384, 768], P(('dp', 'tensor'))
- grad_ln1_gain: float32 [768], replicated
- grad_ln1_bias: float32 [768], replicated
- grad_w_qkv: float32 [768, 3, 768], P(None, None, 'tensor')
- grad_b_qkv: float32 [3, 768], P(None, 'tensor')
- grad_feat_q: float32 [12, 64, 64], P('tensor')
- grad_feat_k: float32 [12, 64, 64], P('tensor')
- grad_w_out: float32 [768, 768], P('tensor')
- grad_b_out: float32 [768], replicated
- grad_ln2_gain: float32 [768], replicated
- grad_ln2_bias: float32 [768], replicated
- grad_w_fc: float32 [768, 3072], P(None, 'tensor')
- grad_b_fc: float32 [3072], P('tensor')
- grad_w_proj: float32 [3072, 768], P('tensor')
- grad_b_proj: float32 [768], replicated
The draws below stay inside these ranges and needn't reach their ends.
Inputs may be any that keep to these rules, and one draw needn't show every extreme that they name: `seq_lengths`: each row is either (1024, 1024) for two sequences or (2048, 0) for one; both kinds occur in every draw.
All inputs are finite; a program needn't handle non-finite values.
Results may differ from the reference program's by a relative error of at most 0.02.
Values may be sent and summed in bfloat16 or wider, within the bound.
A program may use at most 192 MiB of HBM per device.

```python
import jax
import jax.numpy as jnp
from jax import lax

D = 768
H = 12
HD = 64
FF = 3072
SPAN = 64
SHORT = 1024
GROUP_TOK = 2048
TOKENS = 16384
N_DP = 8
N_TENSOR = 4


def draw_seq_lengths(key, part):
    single = jax.random.randint(key, (N_DP,), 0, 2).astype(jnp.int32)
    single = single.at[0].set(1).at[1].set(0)
    first_len = jnp.where(single == 1, 2 * SHORT, SHORT)
    second_len = jnp.where(single == 1, 0, SHORT)
    return jnp.stack([first_len, second_len], axis=1).astype(jnp.int32)


def shard_levels(key, extent, shards, least, high):
    def one(position, parts):
        steps = jax.random.uniform(jax.random.fold_in(jax.random.fold_in(key, 6), position), (parts,), jnp.float32, least / len(shards), high / len(shards))
        return jnp.repeat(jnp.exp(steps), extent[position] // parts).reshape((-1,) + (1,) * (len(extent) - position - 1))

    level = one(*shards[0])
    for cut in shards[1:]:
        level = level * one(*cut)
    return level


def gaussian(own_key, shape, width, most, shards=(), held_as=jnp.bfloat16):
    gain = shard_levels(own_key, shape, shards, -0.22, 0.18) if shards else 1.0
    result = jax.random.normal(own_key, shape, jnp.float32) * width * gain
    return jnp.minimum(jnp.maximum(result, -most), most).astype(held_as)


def setup_inputs(seed: int = 0) -> dict:
    key_of = jax.random.split(jax.random.key(seed), 18)
    return {
        "tokens_in": gaussian(key_of[0], (TOKENS, D), 1.0, 6.0, ((0, 32),)),
        "ln1_gain": jnp.clip(1.0 + 0.15 * jax.random.normal(key_of[1], (D,), jnp.float32), 0.25, 1.75),
        "ln1_bias": gaussian(key_of[2], (D,), 0.3, 1.5, (), jnp.float32),
        "w_qkv": gaussian(key_of[3], (D, 3, D), D ** -0.5, 0.21875, ((2, 4),)),
        "b_qkv": gaussian(key_of[4], (3, D), 0.1, 0.5, ((1, 4),), jnp.float32),
        "feat_q": gaussian(key_of[5], (H, HD, HD), 0.25, 1.5, ((0, 4),)),
        "feat_k": gaussian(key_of[6], (H, HD, HD), 0.25, 1.5, ((0, 4),)),
        "w_out": gaussian(key_of[7], (D, D), (D // 64) ** -0.5, 1.75, ((0, 4),)),
        "b_out": gaussian(key_of[8], (D,), 0.3, 1.5, (), jnp.float32),
        "ln2_gain": jnp.clip(1.0 + 0.15 * jax.random.normal(key_of[9], (D,), jnp.float32), 0.25, 1.75),
        "ln2_bias": gaussian(key_of[10], (D,), 0.3, 1.5, (), jnp.float32),
        "w_fc": gaussian(key_of[11], (D, FF), D ** -0.5, 0.21875, ((1, 4),)),
        "b_fc": gaussian(key_of[12], (FF,), 0.3, 1.5, ((0, 4),), jnp.float32),
        "w_proj": gaussian(key_of[13], (FF, D), FF ** -0.5, 0.109375, ((0, 4),)),
        "b_proj": gaussian(key_of[14], (D,), 0.3, 1.5, (), jnp.float32),
        "seq_lengths": draw_seq_lengths(jax.random.fold_in(key_of[17], 71), 0),
        "cotangent": gaussian(key_of[16], (TOKENS, D), 1.0, 6.0, ((0, 32),)),
    }


NORM_EPS = 1e-05
PRECISE = lax.Precision.HIGHEST

@jax.custom_vjp
def low(v):
    return lax.optimization_barrier(v.astype(jnp.bfloat16)).astype(jnp.float32)

@jax.custom_vjp
def low_back(v):
    return v

def low_keep(v):
    return (low(v), None)

def low_pass(kept, grad):
    return (grad,)

def back_keep(v):
    return (v, None)

def back_low(kept, grad):
    return (low(grad),)
low.defvjp(low_keep, low_pass)
low_back.defvjp(back_keep, back_low)

def layer_norm(inputs, scale_vec, shift_vec):
    average = lax.optimization_barrier(jnp.mean(inputs, axis=-1, keepdims=True))
    centred = inputs - average
    variance = lax.optimization_barrier(jnp.mean(centred * centred, axis=-1, keepdims=True))
    return centred * lax.rsqrt(variance + NORM_EPS) * scale_vec + shift_vec

def feature(logits):
    return jnp.concatenate([jax.nn.softmax(logits, axis=-1), jax.nn.softmax(-logits, axis=-1)], axis=-1)

def gelu_tanh(inputs):
    return jax.nn.gelu(inputs, approximate=True)

def span_links(lengths, span_count):
    first_end = lengths[0].astype(jnp.int32)
    second_end = (lengths[0] + lengths[1]).astype(jnp.int32)
    positions = jnp.arange(span_count, dtype=jnp.int32)
    starts = positions * SPAN
    seq_id = (starts >= first_end).astype(jnp.int32) + (starts >= second_end).astype(jnp.int32)
    linked = (positions[None, :] < positions[:, None]) & (seq_id[None, :] == seq_id[:, None])
    return linked.astype(jnp.float32)

def attention_mix(qkv_all, feat_q, feat_k, linked_mask):
    span_count = qkv_all.shape[0] // SPAN
    blocks = qkv_all.reshape(span_count, SPAN, 3, H, HD)
    query_rows = blocks[:, :, 0]
    key_rows = blocks[:, :, 1]
    value_rows = blocks[:, :, 2]
    query_logits = low_back(jnp.einsum('ncha,hab->nchb', query_rows, feat_q, precision=PRECISE))
    key_logits = low_back(jnp.einsum('ncha,hab->nchb', key_rows, feat_k, precision=PRECISE))
    query_feat = low(feature(query_logits))
    key_feat = low(feature(key_logits))
    causal = jnp.tril(jnp.ones((SPAN, SPAN), jnp.float32))
    scores = low_back(jnp.einsum('nihf,njhf->nhij', query_feat, key_feat, precision=PRECISE) * causal)
    key_value = low_back(jnp.einsum('njhf,njhe->nhfe', key_feat, value_rows, precision=PRECISE))
    key_total = lax.optimization_barrier(jnp.sum(key_feat, axis=1))
    carried = low_back(jnp.einsum('nm,mhfe->nhfe', linked_mask, key_value, precision=PRECISE))
    key_accum = jnp.einsum('nm,mhf->nhf', linked_mask, key_total, precision=PRECISE)
    numerator = low_back(jnp.einsum('nhij,njhe->nihe', low(scores), value_rows, precision=PRECISE) + jnp.einsum('nihf,nhfe->nihe', query_feat, low(carried), precision=PRECISE))
    denominator = jnp.transpose(lax.optimization_barrier(jnp.sum(scores, axis=-1)), (0, 2, 1)) + jnp.einsum('nihf,nhf->nih', query_feat, key_accum, precision=PRECISE)
    mixing = low_back(low(numerator / denominator[..., None]))
    return mixing.reshape(span_count * SPAN, H * HD)

def group_forward(group_rows, weights, linked_mask):
    ln1_gain, ln1_bias, w_qkv, b_qkv, feat_q, feat_k, w_out, b_out, ln2_gain, ln2_bias, w_fc, b_fc, w_proj, b_proj = weights
    head_cols = D // N_TENSOR
    unit_cols = FF // N_TENSOR
    normed_one = low(layer_norm(group_rows, ln1_gain, ln1_bias))
    pieces = []
    for member in range(N_TENSOR):
        copied = low_back(normed_one)
        columns = slice(member * head_cols, (member + 1) * head_cols)
        pieces.append(jnp.einsum('rd,dcw->rcw', copied, w_qkv[:, :, columns], precision=PRECISE) + b_qkv[:, columns])
    qkv_all = low_back(low(jnp.concatenate(pieces, axis=2)))
    mixing = attention_mix(qkv_all, feat_q, feat_k, linked_mask)
    head_total = jnp.zeros_like(group_rows)
    for member in range(N_TENSOR):
        columns = slice(member * head_cols, (member + 1) * head_cols)
        head_total = head_total + low(jnp.dot(mixing[:, columns], w_out[columns], precision=PRECISE))
    mid_res = group_rows + low_back(head_total + b_out)
    normed_two = low(layer_norm(mid_res, ln2_gain, ln2_bias))
    unit_total = jnp.zeros_like(group_rows)
    for member in range(N_TENSOR):
        copied = low_back(normed_two)
        columns = slice(member * unit_cols, (member + 1) * unit_cols)
        pre_act = low_back(jnp.dot(copied, w_fc[:, columns], precision=PRECISE) + b_fc[columns])
        act_low = low(gelu_tanh(pre_act))
        unit_total = unit_total + low(jnp.dot(act_low, w_proj[columns], precision=PRECISE))
    return mid_res + low_back(unit_total + b_proj)

def reference(tokens_in, ln1_gain, ln1_bias, w_qkv, b_qkv, feat_q, feat_k, w_out, b_out, ln2_gain, ln2_bias, w_fc, b_fc, w_proj, b_proj, seq_lengths, cotangent):
    params = tuple((item.astype(jnp.float32) for item in (ln1_gain, ln1_bias, w_qkv, b_qkv, feat_q, feat_k, w_out, b_out, ln2_gain, ln2_bias, w_fc, b_fc, w_proj, b_proj)))
    all_rows = tokens_in.astype(jnp.float32).reshape(N_DP, GROUP_TOK, D)
    all_cots = cotangent.astype(jnp.float32).reshape(N_DP, GROUP_TOK, D)
    span_count = GROUP_TOK // SPAN

    def advance(totals, inputs):
        group_rows, cot_rows, lengths = inputs
        linked_mask = span_links(lengths, span_count)

        def forward(rows_in, weights):
            return group_forward(rows_in, weights, linked_mask)
        outputs, pullback = jax.vjp(forward, group_rows, params)
        grad_rows, grad_params = pullback(cot_rows)
        totals = tuple((first + second for first, second in zip(totals, grad_params)))
        return (totals, (outputs.astype(jnp.bfloat16), grad_rows.astype(jnp.bfloat16)))
    zero_init = tuple((jnp.zeros(item.shape, jnp.float32) for item in params))
    totals, (outputs, grads_in) = lax.scan(advance, zero_init, (all_rows, all_cots, seq_lengths))
    g_ln1_gain, g_ln1_bias, g_w_qkv, g_b_qkv, g_feat_q, g_feat_k, g_w_out, g_b_out, g_ln2_gain, g_ln2_bias, g_w_fc, g_b_fc, g_w_proj, g_b_proj = totals
    return (outputs.reshape(TOKENS, D), grads_in.reshape(TOKENS, D), g_ln1_gain, g_ln1_bias, g_w_qkv, g_b_qkv, g_feat_q, g_feat_k, g_w_out, g_b_out, g_ln2_gain, g_ln2_bias, g_w_fc, g_b_fc, g_w_proj, g_b_proj)
```

```python
import functools
import math

import jax
import jax.numpy as jnp
from jax import lax
from jax.experimental import pallas as pl
from jax.experimental.pallas import tpu as pltpu
from jax.sharding import PartitionSpec as P

NORM_EPS = 1e-05
BF = jnp.bfloat16
F32 = jnp.float32
MESH = pl.DeviceIdType.MESH
NT = 4
D = 768
HD = 64
HPG = 3
HC = HPG * HD
NH = NT * HPG
U = 768
AUG = 80
QKV = 3 * HC
KINDS = 3
R_W = 96
R_G = (112, 96, 96)
ROWS_G = (896, 768, 768)
CB = 256


def dot(a, b, ca=1, cb=0):
    return lax.dot_general(a, b, (((ca,), (cb,)), ((), ())), preferred_element_type=F32)


def mo(value, multiple):
    return pl.multiple_of(value, multiple)


def soft_pair(logits):
    top = jnp.max(logits, axis=0, keepdims=True)
    low = jnp.min(logits, axis=0, keepdims=True)
    e_pos = jnp.exp(logits - top)
    e_neg = jnp.exp(low - logits)
    p = e_pos * (1.0 / jnp.sum(e_pos, axis=0, keepdims=True))
    m = e_neg * (1.0 / jnp.sum(e_neg, axis=0, keepdims=True))
    return jnp.concatenate([p, m], axis=0)


def norm_stats(rows):
    mean = jnp.mean(rows, axis=-1, keepdims=True)
    centred = rows - mean
    var = jnp.mean(centred * centred, axis=-1, keepdims=True)
    inv = lax.rsqrt(var + NORM_EPS)
    return centred * inv, inv


def col(n):
    return pl.ds(mo(n * CB, CB), CB)


def layer_kernel(
    nh,
    seq_ref,
    x_ref,
    cot_ref,
    ln1g_ref,
    ln1b_ref,
    bout_ref,
    ln2g_ref,
    ln2b_ref,
    bproj_ref,
    a_own,
    b_own,
    c_own,
    ft_own,
    bp_own,
    res_ref,
    gin_ref,
    oa_ref,
    ob_ref,
    oc_ref,
    ov_ref,
    WA,
    WB,
    WC,
    FT,
    BP,
    R0A,
    R0B,
    R0C,
    RAA,
    RAB,
    RAC,
    RBA,
    RBB,
    RBC,
    ZRA,
    ZRB,
    ZRC,
    OA,
    OB,
    OC,
    RHA,
    RHB,
    RHC,
    LS,
    LR,
    LZ,
    N1,
    QK,
    VA,
    QF,
    KF,
    NM,
    ST,
    CT,
    CR,
    SQ,
    GR,
    MX,
    DI,
    MID,
    N2,
    N2T,
    UN,
    GN2,
    GML,
    ACT,
    ACTT,
    GP,
    GBF,
    GA,
    GC,
    GQ,
    VS,
    own_s,
    sm_s,
    sm_r,
    wz_s,
    w_s,
    w_r,
    g_s,
    g_r,
    z_r,
    o_s,
    o_r,
    h_s,
    h_r,
    l_s,
    l_r,
    lz_s,
    lz_r,
    c_s,
    c_r,
):
    dp = lax.axis_index("dp")
    z = lax.axis_index("tensor")
    T = x_ref.shape[0]
    NB = T // CB
    core = lax.rem(dp, 2)
    bx = lax.rem(dp // 2, 2)
    by = lax.rem(dp // 4, 2)
    d_core = 1 - 2 * core
    d_x = 2 * (1 - 2 * bx)
    d_y = 4 * (1 - 2 * by)
    slot = core * 4 + by * 2 + bx

    W = (WA, WB, WC)
    OWN = (a_own, b_own, c_own)
    R0 = (R0A, R0B, R0C)
    RA = (RAA, RAB, RAC)
    RB = (RBA, RBB, RBC)
    ZR = (ZRA, ZRB, ZRC)
    O = (OA, OB, OC)
    RH = (RHA, RHB, RHC)

    def order(j):
        return jnp.where(j == 0, z, j - 1 + (j - 1 >= z).astype(jnp.int32))

    def high(i):
        step = 8 * 2**i
        return dp + step * (1 - 2 * lax.rem(dp // step, 2))

    def rcopy(src, dst, ssem, rsem, dev):
        return pltpu.make_async_remote_copy(
            src_ref=src, dst_ref=dst, send_sem=ssem, recv_sem=rsem, device_id=dev, device_id_type=MESH
        )

    def first_is_y(k, g):
        return lax.rem(k + g, 2)

    def step_a(k, g):
        q = first_is_y(k, g)
        return dp + q * d_y + (1 - q) * d_x

    def step_b(k, g):
        q = first_is_y(k, g)
        return dp + q * d_x + (1 - q) * d_y

    def slot_of(k, g, flip_a, flip_b):
        q = first_is_y(k, g)
        sx = bx + (1 - 2 * bx) * (q * flip_b + (1 - q) * flip_a)
        sy = by + (1 - 2 * by) * (q * flip_a + (1 - q) * flip_b)
        return core * 4 + sy * 2 + sx

    def abs_slot(k, g, flip_a, bit_b):
        q = first_is_y(k, g)
        ax = bx + (1 - 2 * bx) * flip_a
        ay = by + (1 - 2 * by) * flip_a
        sx = q * bit_b + (1 - q) * ax
        sy = q * ay + (1 - q) * bit_b
        return core * 4 + sy * 2 + sx

    def my_b_bit(k, g):
        q = first_is_y(k, g)
        return q * bx + (1 - q) * by

    peers = [(dp + d_core, z), (dp + d_x, z), (dp + d_y, z)]
    peers += [(high(i), z) for i in range(nh)]
    peers += [(dp, lax.rem(z + o, NT)) for o in range(1, NT)]
    barrier = pltpu.get_barrier_semaphore()
    for peer in peers:
        pl.semaphore_signal(barrier, inc=1, device_id=peer, device_id_type=MESH)
    pl.semaphore_wait(barrier, len(peers))

    def wrows(k, g, s):
        return W[k].at[g, pl.ds(mo(s * R_W, R_W), R_W), :]

    def wrows4(k, g, c):
        return W[k].at[g, pl.ds(mo(c * 4 * R_W, R_W), 4 * R_W), :]

    def w_z(k):
        for o in range(1, NT):
            rcopy(
                OWN[k].at[pl.ds(mo(slot * R_W, R_W), R_W), :],
                wrows(k, z, slot),
                wz_s.at[k, o - 1],
                w_r.at[0, k, z],
                (dp, lax.rem(z + o, NT)),
            ).start()

    def w_wait(k, g, stage, ref):
        rcopy(ref, ref, w_s.at[0, k, g], w_r.at[stage, k, g], (dp + d_core, z)).wait_recv()

    def w_1(k, i):
        g = order(i)
        w_wait(k, g, 0, wrows(k, g, slot))
        src = wrows(k, g, slot)
        rcopy(src, src, w_s.at[0, k, g], w_r.at[1, k, g], (step_a(k, g), z)).start()

    def w_2(k, i):
        g = order(i)
        w_wait(k, g, 1, wrows(k, g, slot_of(k, g, 1, 0)))
        for f in range(2):
            src = wrows(k, g, slot_of(k, g, f, 0))
            rcopy(src, src, w_s.at[1 + f, k, g], w_r.at[2 + f, k, g], (step_b(k, g), z)).start()

    def w_3(k, i):
        g = order(i)
        for f in range(2):
            w_wait(k, g, 2 + f, wrows(k, g, slot_of(k, g, f, 1)))
        src = wrows4(k, g, core)
        rcopy(src, src, w_s.at[3, k, g], w_r.at[4, k, g], (dp + d_core, z)).start()

    def w_4(k, i):
        g = order(i)
        w_wait(k, g, 4, wrows4(k, g, 1 - core))
        one = wrows(k, g, slot)
        for st in range(3):
            rcopy(one, one, w_s.at[st, k, g], w_r.at[0, k, g], (dp + d_core, z)).wait_send()
        four = wrows4(k, g, core)
        rcopy(four, four, w_s.at[3, k, g], w_r.at[0, k, g], (dp + d_core, z)).wait_send()

    def w_z_done(k):
        one = OWN[k].at[pl.ds(mo(slot * R_W, R_W), R_W), :]
        for o in range(1, NT):
            rcopy(one, one, wz_s.at[k, o - 1], w_r.at[0, k, z], (dp, lax.rem(z + o, NT))).wait_send()

    small = ((ft_own, FT), (bp_own, BP))

    def small_send():
        for i, (own, buf) in enumerate(small):
            for o in range(1, NT):
                rcopy(own, buf.at[z], sm_s.at[i, o - 1], sm_r.at[i, z], (dp, lax.rem(z + o, NT))).start()

    def small_wait(g):
        for i, (own, buf) in enumerate(small):
            rcopy(own, buf.at[g], sm_s.at[i, 0], sm_r.at[i, g], (dp, z)).wait_recv()

    def small_done():
        for i, (own, buf) in enumerate(small):
            for o in range(1, NT):
                rcopy(own, buf.at[z], sm_s.at[i, o - 1], sm_r.at[i, z], (dp, lax.rem(z + o, NT))).wait_send()

    local = [
        pltpu.make_async_copy(ft_own, FT.at[z], own_s.at[0]),
        pltpu.make_async_copy(bp_own, BP.at[z], own_s.at[1]),
        pltpu.make_async_copy(a_own, WA.at[z, pl.ds(0, D), :], own_s.at[2]),
        pltpu.make_async_copy(b_own, WB.at[z], own_s.at[3]),
        pltpu.make_async_copy(c_own, WC.at[z], own_s.at[4]),
    ]
    small_send()
    w_z(0)
    for copy in local:
        copy.start()

    def grows(k, g, s, n=1):
        return W[k].at[g, pl.ds(mo(s * R_G[k], 16), n * R_G[k]), :]

    def add_rows(dst, start, src, n):
        blk = 16 if n % 32 else 32

        def body(i, _):
            at = pl.ds(mo(start + i * blk, 16), blk)
            dst[at, :] = (dst[at, :].astype(F32) + src[pl.ds(mo(i * blk, 16), blk), :].astype(F32)).astype(BF)
            return 0

        lax.fori_loop(0, n // blk, body, 0)

    def g_wait(k, g, stage, ref):
        rcopy(ref, ref, g_s.at[0, k, g], g_r.at[stage, k, g], (dp + d_core, z)).wait_recv()

    def g_core(k, g):
        rcopy(
            grows(k, g, (1 - core) * 4, 4), R0[k].at[g], g_s.at[0, k, g], g_r.at[0, k, g], (dp + d_core, z)
        ).start()

    def g_a(k, g):
        g_wait(k, g, 0, R0[k].at[g])
        add_rows(W[k].at[g], core * 4 * R_G[k], R0[k].at[g], 4 * R_G[k])
        for b in range(2):
            rcopy(
                grows(k, g, abs_slot(k, g, 1, b)),
                RA[k].at[g, b],
                g_s.at[1 + b, k, g],
                g_r.at[1 + b, k, g],
                (step_a(k, g), z),
            ).start()

    def g_b(k, g):
        for b in range(2):
            g_wait(k, g, 1 + b, RA[k].at[g, b])
            add_rows(W[k].at[g], abs_slot(k, g, 0, b) * R_G[k], RA[k].at[g, b], R_G[k])
        rcopy(
            grows(k, g, slot_of(k, g, 0, 1)),
            RB[k].at[g],
            g_s.at[3, k, g],
            g_r.at[3, k, g],
            (step_b(k, g), z),
        ).start()

    def g_z(k, g):
        g_wait(k, g, 3, RB[k].at[g])
        add_rows(W[k].at[g], slot * R_G[k], RB[k].at[g], R_G[k])

        @pl.when(g != z)
        def _():
            rcopy(grows(k, g, slot), ZR[k].at[z], g_s.at[4, k, g], z_r.at[k, z], (dp, g)).start()

    def g_done(k, g):
        four = grows(k, g, 0, 4)
        one = grows(k, g, 0)
        rcopy(four, four, g_s.at[0, k, g], g_r.at[0, k, g], (dp + d_core, z)).wait_send()
        for st in range(1, 4):
            rcopy(one, one, g_s.at[st, k, g], g_r.at[0, k, g], (dp + d_core, z)).wait_send()

        @pl.when(g != z)
        def _():
            rcopy(one, one, g_s.at[4, k, g], g_r.at[0, k, g], (dp + d_core, z)).wait_send()

    def orows(k, s, n=1):
        return O[k].at[pl.ds(mo(s * R_G[k], 16), n * R_G[k]), :]

    def o_wait(k, stage, ref):
        rcopy(ref, ref, o_s.at[stage, k], o_r.at[stage, k], (dp + d_core, z)).wait_recv()

    def g_sum(k):
        for o in range(1, NT):
            zz = lax.rem(z + o, NT)
            ref = ZR[k].at[zz]
            rcopy(ref, ref, g_s.at[0, k, 0], z_r.at[k, zz], (dp, z)).wait_recv()
        blk = 16

        def body(i, _):
            at = pl.ds(mo(i * blk, 16), blk)
            mine = pl.ds(mo(slot * R_G[k] + i * blk, 16), blk)
            acc = W[k][z, mine, :].astype(F32)
            for o in range(1, NT):
                acc = acc + ZR[k][lax.rem(z + o, NT), at, :].astype(F32)
            O[k][mine, :] = acc.astype(BF)
            return 0

        lax.fori_loop(0, R_G[k] // blk, body, 0)
        for i in range(nh):
            rcopy(orows(k, slot), RH[k].at[i], h_s.at[i, k], h_r.at[i, k], (high(i), z)).start()
            rcopy(orows(k, slot), RH[k].at[i], h_s.at[i, k], h_r.at[i, k], (high(i), z)).wait()
            add_rows(O[k], slot * R_G[k], RH[k].at[i], R_G[k])
        src = orows(k, slot)
        rcopy(src, src, o_s.at[0, k], o_r.at[0, k], (step_b(k, z), z)).start()

    def o_2(k):
        o_wait(k, 0, orows(k, slot_of(k, z, 0, 1)))
        for f in range(2):
            src = orows(k, slot_of(k, z, 0, f))
            rcopy(src, src, o_s.at[1 + f, k], o_r.at[1 + f, k], (step_a(k, z), z)).start()

    def o_3(k):
        for f in range(2):
            o_wait(k, 1 + f, orows(k, slot_of(k, z, 1, f)))
        src = orows(k, core * 4, 4)
        rcopy(src, src, o_s.at[3, k], o_r.at[3, k], (dp + d_core, z)).start()

    def o_4(k, out, sem):
        o_wait(k, 3, orows(k, (1 - core) * 4, 4))
        copy = pltpu.make_async_copy(O[k], out, sem)
        copy.start()
        one = orows(k, slot)
        for st in range(3):
            rcopy(one, one, o_s.at[st, k], o_r.at[0, k], (dp + d_core, z)).wait_send()
        four = orows(k, core * 4, 4)
        rcopy(four, four, o_s.at[3, k], o_r.at[0, k], (dp + d_core, z)).wait_send()
        return copy

    def iota(shape, axis):
        return lax.broadcasted_iota(jnp.int32, shape, axis)

    causal = iota((CB, CB), 0) <= iota((CB, CB), 1)
    aug_tail = jnp.where(iota((16, T), 0) < 2, 1.0, 0.0).astype(BF)
    ones_rows = jnp.ones((16, T), BF)
    head_mask = (iota((HC, HC), 0) // HD) == (iota((HC, HC), 1) // HD)

    def pick(which):
        r = iota((2 * HD, HC), 0) - which * HD
        return (r == lax.rem(iota((2 * HD, HC), 1), HD)).astype(BF)

    def pick_back(which):
        r = iota((HC, 2 * HD), 1) - which * HD
        return (r == lax.rem(iota((HC, 2 * HD), 0), HD)).astype(BF)

    def block_diag(g, which):
        return jnp.where(head_mask, dot(FT[g], pick(which)), 0.0).astype(BF)

    first_end = seq_ref[0, 0]
    second_end = seq_ref[0, 0] + seq_ref[0, 1]

    def seq_id(zz):
        start = zz * T
        return (start >= first_end).astype(jnp.int32) + (start >= second_end).astype(jnp.int32)

    from_prev = jnp.logical_and(z > 0, seq_id(z) == seq_id(z - 1))
    from_next = jnp.logical_and(z < NT - 1, seq_id(z) == seq_id(z + 1))

    RB_ = 64

    def p0(i, _):
        at = pl.ds(mo(i * RB_, RB_), RB_)
        xh, _inv = norm_stats(x_ref[at, :].astype(F32))
        N1[at, :] = (xh * ln1g_ref[...] + ln1b_ref[...]).astype(BF)
        return 0

    lax.fori_loop(0, T // RB_, p0, 0)
    for g in range(NT):
        WA[g, pl.ds(D, ROWS_G[0] - D), :] = jnp.zeros((ROWS_G[0] - D, D), BF)
    GQ[pl.ds(QKV, D - QKV), :] = jnp.zeros((D - QKV, T), BF)

    @pl.when(z == 0)
    def _():
        CR[...] = jnp.zeros_like(CR)

    @pl.when(z == NT - 1)
    def _():
        GR[...] = jnp.zeros_like(GR)

    for copy in local[:3]:
        copy.wait()

    def p1(j, _):
        g = order(j)

        @pl.when(j == 1)
        def _():
            small_wait(order(1))
            w_1(0, 1)
            w_1(0, 2)
            w_2(0, 1)
            w_1(0, 3)
            w_z(1)
            w_2(0, 2)
            w_3(0, 1)
            w_2(0, 3)
            w_3(0, 2)
            w_4(0, 1)

        @pl.when(j == 2)
        def _():
            small_wait(order(2))
            w_3(0, 3)
            w_4(0, 2)

        @pl.when(j == 3)
        def _():
            small_wait(order(3))
            w_4(0, 3)
            w_1(1, 1)
            w_1(1, 2)
            w_1(1, 3)
            w_z(2)

        bias = jnp.transpose(BP[g])[:QKV, 0:1]
        qkv = (dot(WA[g, pl.ds(0, QKV), :], N1[...], 1, 1) + bias).astype(BF)
        QK[g] = qkv[: 2 * HC]
        ql = dot(block_diag(g, 0), qkv[:HC])
        kl = dot(block_diag(g, 1), qkv[HC : 2 * HC])
        for h in range(HPG):
            hh = g * HPG + h
            rows = slice(h * HD, (h + 1) * HD)
            qf = soft_pair(ql[rows]).astype(BF)
            kf = soft_pair(kl[rows]).astype(BF)
            va = jnp.concatenate([qkv[2 * HC + h * HD : 2 * HC + (h + 1) * HD], aug_tail], axis=0)
            QF[hh] = qf
            KF[hh] = kf
            VA[hh] = va
            kn = kf.T
            ST[hh] = dot(va, kn)
            for qi in range(NB):
                qs = slice(qi * CB, (qi + 1) * CB)
                acc = None
                for ki in range(qi + 1):
                    ks = slice(ki * CB, (ki + 1) * CB)
                    s = dot(kn[ks], qf[:, qs])
                    if ki == qi:
                        s = jnp.where(causal, s, 0.0)
                    part = dot(va[:, ks], s.astype(BF))
                    acc = part if acc is None else acc + part
                NM[hh, :, qs] = acc[: HD + 8]
        return 0

    lax.fori_loop(0, NT, p1, 0)
    w_2(1, 1)
    w_2(1, 2)
    w_2(1, 3)

    def chain_wait(buf, g, stage):
        rcopy(buf.at[g], buf.at[g], c_s.at[stage, g], c_r.at[stage, g], (dp, z)).wait_recv()

    def p1b(g, _):
        @pl.when(z > 0)
        def _():
            chain_wait(CR, g, 0)

        for h in range(HPG):
            hh = g * HPG + h
            carried = jnp.where(from_prev, CR[g, h].astype(F32), 0.0)
            SQ[g, h] = (ST[hh] + carried).astype(BF)
            CT[hh] = carried.astype(BF)

        @pl.when(z < NT - 1)
        def _():
            rcopy(SQ.at[g], CR.at[g], c_s.at[0, g], c_r.at[0, g], (dp, z + 1)).start()

        for h in range(HPG):
            hh = g * HPG + h
            num = NM[hh] + dot(CT[hh], QF[hh])[: HD + 8]
            inv = 1.0 / num[HD : HD + 1]
            DI[hh] = inv
            MX[g, pl.ds(h * HD, HD), :] = (num[:HD] * inv).astype(BF)
        return 0

    lax.fori_loop(0, NT, p1b, 0)
    w_3(1, 1)
    w_3(1, 2)
    w_3(1, 3)

    def p2(n, _):
        acc = None
        for g in range(NT):
            part = dot(MX[g], WA[g, pl.ds(QKV, HC), col(n)], 0, 0)
            acc = part if acc is None else acc + part
        MID[:, col(n)] = x_ref[:, col(n)].astype(F32) + (acc + bout_ref[:, col(n)])
        return 0

    lax.fori_loop(0, D // CB, p2, 0)

    def p2b(i, _):
        at = pl.ds(mo(i * 128, 128), 128)
        xh, _inv = norm_stats(MID[at, :])
        n2 = (xh * ln2g_ref[...] + ln2b_ref[...]).astype(BF)
        N2[at, :] = n2
        N2T[:, at] = n2.T
        return 0

    lax.fori_loop(0, T // 128, p2b, 0)
    w_1(2, 1)
    w_1(2, 2)
    w_1(2, 3)

    @pl.when(z < NT - 1)
    def _():
        for g in range(NT):
            rcopy(SQ.at[g], SQ.at[g], c_s.at[0, g], c_r.at[0, g], (dp, z)).wait_send()

    UN[...] = jnp.zeros_like(UN)
    GN2[...] = jnp.zeros_like(GN2)
    for copy in local[3:]:
        copy.wait()

    cc = math.sqrt(2.0 / math.pi)

    def p3(j, _):
        g = order(j)

        @pl.when(j == 1)
        def _():
            w_4(1, 1)
            w_2(2, 2)
            w_2(2, 3)
            w_3(2, 1)
            w_3(2, 2)
            w_3(2, 3)
            w_4(2, 1)

        @pl.when(j == 2)
        def _():
            w_4(1, 2)
            w_4(2, 2)

        @pl.when(j == 3)
        def _():
            w_4(1, 3)
            w_4(2, 3)

        def units(u, total):
            pre = dot(N2[...], WB[g, :, col(u)]) + BP[g, pl.ds(1, 1), col(u)]
            sq = pre * pre
            t = jnp.tanh(cc * pre * (1.0 + 0.044715 * sq))
            act = (0.5 * pre * (1.0 + t)).astype(BF)
            slope = 0.5 * (1.0 + t) + (0.5 * cc) * pre * (1.0 - t * t) * (1.0 + (3 * 0.044715) * sq)
            ACT[:, col(u)] = act
            ACTT[col(u), :] = act.T
            gact = dot(cot_ref[...], WC[g, col(u), :], 1, 1)
            gpre = (gact * slope).astype(BF)
            GP[:, col(u)] = gpre
            GBF[g, :, col(u)] = jnp.sum(gpre.astype(F32), axis=0, keepdims=True)
            return total

        lax.fori_loop(0, U // CB, units, 0)

        @pl.when(j == 0)
        def _():
            w_2(2, 1)

        @pl.when(j >= 1)
        def _():
            gp = order(j - 1)
            g_a(1, gp)
            g_a(2, gp)

        def outs(n, _):
            UN[:, col(n)] += dot(ACT[...], WC[g, :, col(n)])
            GN2[:, col(n)] += dot(GP[...], WB[g, col(n), :], 1, 1)
            return 0

        lax.fori_loop(0, D // CB, outs, 0)

        @pl.when(j >= 2)
        def _():
            gp = order(j - 2)
            g_b(1, gp)
            g_b(2, gp)

        def grads(n, _):
            WC[g, col(n), :] = dot(ACTT[col(n), :], cot_ref[...]).astype(BF)
            WB[g, col(n), :] = dot(N2T[col(n), :], GP[...]).astype(BF)
            return 0

        lax.fori_loop(0, D // CB, grads, 0)
        g_core(1, g)
        g_core(2, g)

        @pl.when(j >= 3)
        def _():
            gp = order(j - 3)
            g_z(1, gp)
            g_z(2, gp)

        return 0

    lax.fori_loop(0, NT, p3, 0)

    VS[...] = jnp.zeros_like(VS)

    def p4(i, _):
        at = pl.ds(mo(i * RB_, RB_), RB_)
        mid = MID[at, :]
        res_ref[at, :] = (mid + UN[at, :] + bproj_ref[...]).astype(BF)
        xh, inv = norm_stats(mid)
        gn = GN2[at, :]
        gh = gn * ln2g_ref[...]
        c1 = jnp.mean(gh, axis=-1, keepdims=True)
        c2 = jnp.mean(gh * xh, axis=-1, keepdims=True)
        cot = cot_ref[at, :].astype(F32)
        gm = cot + inv * (gh - c1 - xh * c2)
        GN2[at, :] = gm
        low = gm.astype(BF)
        GML[at, :] = low
        VS[0] += jnp.sum(cot, axis=0, keepdims=True)
        VS[1] += jnp.sum(low.astype(F32), axis=0, keepdims=True)
        VS[2] += jnp.sum(gn * xh, axis=0, keepdims=True)
        VS[3] += jnp.sum(gn, axis=0, keepdims=True)
        return 0

    lax.fori_loop(0, T // RB_, p4, 0)
    g_a(1, order(3))
    g_a(2, order(3))

    tail_row = iota((16, T), 0)

    def p5a(g, _):
        gmix = dot(WA[g, pl.ds(QKV, HC), :], GML[...], 1, 1).astype(BF).astype(F32)
        mix = MX[g]
        WA[g, pl.ds(QKV, HC), :] = dot(mix, GML[...]).astype(BF)
        prod = gmix * mix.astype(F32)
        for h in range(HPG):
            hh = g * HPG + h
            rows = slice(h * HD, (h + 1) * HD)
            inv = DI[hh]
            gden = -jnp.sum(prod[rows], axis=0, keepdims=True) * inv
            hi = gden.astype(BF).astype(F32)
            lo = gden - hi
            tail = jnp.where(tail_row == 0, hi, jnp.where(tail_row == 1, lo, 0.0)).astype(BF)
            ga = jnp.concatenate([(gmix[rows] * inv).astype(BF), tail], axis=0)
            GA[hh] = ga
            gc = dot(ga, QF[hh].T)
            GC[hh] = gc
            SQ[g, h] = gc.astype(BF)

        @pl.when(z == NT - 1)
        def _():
            rcopy(SQ.at[g], GR.at[g], c_s.at[1, g], c_r.at[1, g], (dp, z - 1)).start()

        return 0

    lax.fori_loop(0, NT, p5a, 0)
    g_b(1, order(2))
    g_b(2, order(2))
    g_z(1, order(1))
    g_z(2, order(1))

    def chain_back(g):
        @pl.when(z < NT - 1)
        def _():
            chain_wait(GR, g, 1)
            for h in range(HPG):
                hh = g * HPG + h
                later = jnp.where(from_next, GR[g, h].astype(F32), 0.0)
                SQ[g, h] = (GC[hh] + later).astype(BF)

        @pl.when(jnp.logical_and(z > 0, z < NT - 1))
        def _():
            rcopy(SQ.at[g], GR.at[g], c_s.at[1, g], c_r.at[1, g], (dp, z - 1)).start()

    GN1 = UN
    GN1[...] = jnp.zeros_like(GN1)

    def p5b(g, _):
        chain_back(g)
        gql = []
        gkl = []
        for h in range(HPG):
            hh = g * HPG + h
            qf = QF[hh]
            kf = KF[hh]
            va = VA[hh]
            ga = GA[hh]
            kn = kf.T
            vn = va.T
            ctt = CT[hh].T
            gkc = jnp.where(from_next, GR[g, h], jnp.zeros((AUG, 2 * HD), BF))
            gkt = gkc.T
            gq = [None] * NB
            gk = [None] * NB
            gv = [None] * NB
            for qi in range(NB):
                qs = slice(qi * CB, (qi + 1) * CB)
                gq[qi] = dot(ctt, ga[:, qs])
                for ki in range(qi + 1):
                    ks = slice(ki * CB, (ki + 1) * CB)
                    s = dot(kn[ks], qf[:, qs])
                    gs = dot(vn[ks], ga[:, qs])
                    if ki == qi:
                        s = jnp.where(causal, s, 0.0)
                        gs = jnp.where(causal, gs, 0.0)
                    s = s.astype(BF)
                    gs = gs.astype(BF)
                    gq[qi] = gq[qi] + dot(kf[:, ks], gs)
                    pk = dot(qf[:, qs], gs, 1, 1)
                    pv = dot(ga[:, qs], s, 1, 1)[:HD]
                    gk[ki] = pk if gk[ki] is None else gk[ki] + pk
                    gv[ki] = pv if gv[ki] is None else gv[ki] + pv
            for ki in range(NB):
                ks = slice(ki * CB, (ki + 1) * CB)
                gk[ki] = gk[ki] + dot(gkt, va[:, ks])
                gv[ki] = gv[ki] + dot(gkc[:HD], kf[:, ks])
                GQ[pl.ds(2 * HC + h * HD, HD), ks] = gv[ki].astype(BF)

            def back(feat, grads):
                out = []
                for b in range(NB):
                    bs = slice(b * CB, (b + 1) * CB)
                    p = feat[:HD, bs].astype(F32)
                    m = feat[HD:, bs].astype(F32)
                    g1 = grads[b][:HD]
                    g2 = grads[b][HD:]
                    s1 = jnp.sum(g1 * p, axis=0, keepdims=True)
                    s2 = jnp.sum(g2 * m, axis=0, keepdims=True)
                    out.append((p * (g1 - s1) - m * (g2 - s2)).astype(BF))
                return jnp.concatenate(out, axis=1)

            gql.append(back(qf, gq))
            gkl.append(back(kf, gk))
        comp = None
        for which, parts in ((0, gql), (1, gkl)):
            glog = jnp.concatenate(parts, axis=0)
            own = QK[g, pl.ds(which * HC, HC), :]
            GQ[pl.ds(which * HC, HC), :] = dot(block_diag(g, which), glog, 0, 0).astype(BF)
            gfeat = jnp.where(head_mask, dot(own, glog, 1, 1), 0.0).astype(BF)
            part = dot(gfeat, pick_back(which))
            comp = part if comp is None else comp + part
        comp = comp.astype(BF)
        gq_all = GQ[...]
        gqn = gq_all[:QKV].T
        for n in range(D // CB):
            GN1[:, n * CB : (n + 1) * CB] += dot(gqn, WA[g, pl.ds(0, QKV), n * CB : (n + 1) * CB])
        WA[g, pl.ds(0, QKV), :] = dot(gq_all[:QKV], N1[...]).astype(BF)
        for b in range(HC // 32):
            WA[g, pl.ds(D, 32), b * 128 : (b + 1) * 128] = comp[b * 32 : (b + 1) * 32]
        vec = dot(ones_rows, gq_all, 1, 1)
        row = iota((16, D), 0)
        vec = jnp.where(row == 1, GBF[g], vec)
        for i in range(4):
            vec = jnp.where(row == 2 + i, VS[i], vec)
        WA[g, pl.ds(D + 32, 16), :] = vec.astype(BF)
        g_core(0, g)

        @pl.when(g == 0)
        def _():
            g_b(1, order(3))
            g_b(2, order(3))
            g_z(1, order(2))
            g_z(2, order(2))

        @pl.when(g == 1)
        def _():
            g_z(1, order(3))
            g_z(2, order(3))

        @pl.when(g >= 1)
        def _():
            g_a(0, g - 1)

        @pl.when(g >= 2)
        def _():
            g_b(0, g - 2)

        @pl.when(g >= 3)
        def _():
            g_z(0, g - 3)
            g_sum(1)
            g_sum(2)

        return 0

    lax.fori_loop(0, NT, p5b, 0)
    g_a(0, NT - 1)

    LS[...] = jnp.zeros_like(LS)

    def p6(i, _):
        at = pl.ds(mo(i * RB_, RB_), RB_)
        xh, inv = norm_stats(x_ref[at, :].astype(F32))
        gn = GN1[at, :]
        gh = gn * ln1g_ref[...]
        c1 = jnp.mean(gh, axis=-1, keepdims=True)
        c2 = jnp.mean(gh * xh, axis=-1, keepdims=True)
        gin_ref[at, :] = (GN2[at, :] + inv * (gh - c1 - xh * c2)).astype(BF)
        LS[0, 0:1, :] += jnp.sum(gn * xh, axis=0, keepdims=True)
        LS[0, 1:2, :] += jnp.sum(gn, axis=0, keepdims=True)
        return 0

    lax.fori_loop(0, T // RB_, p6, 0)

    partners = [dp + d_core, dp + d_x, dp + d_y] + [high(i) for i in range(nh)]

    def small_sum(i):
        copy = rcopy(LS.at[i], LR.at[i], l_s.at[i], l_r.at[i], (partners[i], z))
        copy.start()
        copy.wait()
        LS[i + 1] = LS[i] + LR[i]

    g_b(0, NT - 2)
    g_z(0, NT - 3)
    o_2(1)
    o_2(2)
    for i in range(len(partners)):
        small_sum(i)
    last = len(partners)
    g_b(0, NT - 1)
    g_z(0, NT - 2)
    o_3(1)
    o_3(2)
    LZ[z] = LS[last]
    for o in range(1, NT):
        rcopy(LS.at[last], LZ.at[z], lz_s.at[o - 1], lz_r.at[z], (dp, lax.rem(z + o, NT))).start()
    g_z(0, NT - 1)
    outs = [o_4(1, ob_ref, own_s.at[0]), o_4(2, oc_ref, own_s.at[1])]
    g_sum(0)
    for o in range(1, NT):
        zz = lax.rem(z + o, NT)
        rcopy(LZ.at[zz], LZ.at[zz], lz_s.at[o - 1], lz_r.at[zz], (dp, z)).wait_recv()
    total = LZ[0]
    for zz in range(1, NT):
        total = total + LZ[zz]
    ov_ref[...] = total
    o_2(0)
    o_3(0)
    outs.append(o_4(0, oa_ref, own_s.at[2]))
    for copy in outs:
        copy.wait()

    for o in range(1, NT):
        rcopy(LS.at[last], LZ.at[z], lz_s.at[o - 1], lz_r.at[z], (dp, lax.rem(z + o, NT))).wait_send()
    small_done()
    for k in range(KINDS):
        w_z_done(k)
        for g in range(NT):
            g_done(k, g)

    @pl.when(z > 0)
    def _():
        for g in range(NT):
            rcopy(SQ.at[g], SQ.at[g], c_s.at[1, g], c_r.at[1, g], (dp, z)).wait_send()


def layer_call(nh, T, *args):
    def vm(shape, dtype=BF):
        return pltpu.VMEM(shape, dtype)

    dma = pltpu.SemaphoreType.DMA
    nhb = max(nh, 1)
    nst = 3 + nh
    scratch = [
        vm((NT, ROWS_G[0], D)),
        vm((NT, D, U)),
        vm((NT, U, D)),
        vm((NT, HC, 2 * HD)),
        vm((NT, 8, D), F32),
    ]
    scratch += [vm((NT, 4 * r, D)) for r in R_G]
    scratch += [vm((NT, 2, r, D)) for r in R_G]
    scratch += [vm((NT, r, D)) for r in R_G]
    scratch += [vm((NT, r, D)) for r in R_G]
    scratch += [vm((rows, D)) for rows in ROWS_G]
    scratch += [vm((nhb, r if nh else 16, D)) for r in R_G]
    scratch += [vm((nst + 1, 8, D), F32), vm((nst, 8, D), F32), vm((NT, 8, D), F32)]
    scratch += [
        vm((T, D)),
        vm((NT, 2 * HC, T)),
        vm((NH, AUG, T)),
        vm((NH, 2 * HD, T)),
        vm((NH, 2 * HD, T)),
        vm((NH, HD + 8, T), F32),
        vm((NH, AUG, 2 * HD), F32),
        vm((NH, AUG, 2 * HD)),
        vm((NT, HPG, AUG, 2 * HD)),
        vm((NT, HPG, AUG, 2 * HD)),
        vm((NT, HPG, AUG, 2 * HD)),
        vm((NT, HC, T)),
        vm((NH, 1, T), F32),
        vm((T, D), F32),
        vm((T, D)),
        vm((D, T)),
        vm((T, D), F32),
        vm((T, D), F32),
        vm((T, D)),
        vm((T, U)),
        vm((U, T)),
        vm((T, U)),
        vm((NT, 1, U), F32),
        vm((NH, AUG, T)),
        vm((NH, AUG, 2 * HD), F32),
        vm((D, T)),
        vm((4, 1, D), F32),
    ]
    scratch += [
        dma((5,)),
        dma((2, NT - 1)),
        dma((2, NT)),
        dma((KINDS, NT - 1)),
        dma((4, KINDS, NT)),
        dma((5, KINDS, NT)),
        dma((5, KINDS, NT)),
        dma((4, KINDS, NT)),
        dma((KINDS, NT)),
        dma((4, KINDS)),
        dma((4, KINDS)),
        dma((nhb, KINDS)),
        dma((nhb, KINDS)),
        dma((nst,)),
        dma((nst,)),
        dma((NT - 1,)),
        dma((NT,)),
        dma((2, NT)),
        dma((2, NT)),
    ]
    vmem = pl.BlockSpec(memory_space=pltpu.VMEM)
    hbm = pl.BlockSpec(memory_space=pl.ANY)
    return pl.pallas_call(
        functools.partial(layer_kernel, nh),
        out_shape=(
            jax.ShapeDtypeStruct((T, D), BF),
            jax.ShapeDtypeStruct((T, D), BF),
            jax.ShapeDtypeStruct((ROWS_G[0], D), BF),
            jax.ShapeDtypeStruct((D, U), BF),
            jax.ShapeDtypeStruct((U, D), BF),
            jax.ShapeDtypeStruct((8, D), F32),
        ),
        in_specs=[pl.BlockSpec(memory_space=pltpu.SMEM)] + [vmem] * 8 + [hbm] * 5,
        out_specs=(vmem, vmem, hbm, hbm, hbm, vmem),
        scratch_shapes=scratch,
        compiler_params=pltpu.CompilerParams(
            collective_id=0, has_side_effects=True, vmem_limit_bytes=67043328
        ),
    )(*args)


def local(
    nh,
    tokens_in,
    ln1_gain,
    ln1_bias,
    w_qkv,
    b_qkv,
    feat_q,
    feat_k,
    w_out,
    b_out,
    ln2_gain,
    ln2_bias,
    w_fc,
    b_fc,
    w_proj,
    b_proj,
    seq_lengths,
    cotangent,
):
    T = tokens_in.shape[0]
    a_own = jnp.concatenate([jnp.transpose(w_qkv, (1, 2, 0)).reshape(QKV, D), w_out], axis=0)
    ft_own = jnp.concatenate(
        [jnp.transpose(feat_q, (0, 2, 1)).reshape(HC, HD), jnp.transpose(feat_k, (0, 2, 1)).reshape(HC, HD)],
        axis=1,
    )
    bq = jnp.pad(b_qkv.reshape(1, QKV), ((0, 0), (0, D - QKV)))
    bp_own = jnp.concatenate([bq, b_fc.reshape(1, U), jnp.zeros((6, D), F32)], axis=0)

    def row(v):
        return v.reshape(1, D)

    res, gin, oa, ob, oc, ov = layer_call(
        nh,
        T,
        seq_lengths,
        tokens_in,
        cotangent,
        row(ln1_gain),
        row(ln1_bias),
        row(b_out),
        row(ln2_gain),
        row(ln2_bias),
        row(b_proj),
        a_own,
        w_fc,
        w_proj,
        ft_own,
        bp_own,
    )
    g_w_qkv = jnp.transpose(oa[:QKV].reshape(3, HC, D), (2, 0, 1)).astype(F32)
    g_w_out = oa[QKV:D].astype(F32)
    feats = jnp.transpose(oa[D : D + 32].reshape(32, HC // 32, 2 * HD), (1, 0, 2)).reshape(HC, 2 * HD)
    feats = feats.astype(F32).reshape(HPG, HD, 2 * HD)
    vec = oa[D + 32 : D + 48].astype(F32)
    return (
        res,
        gin,
        ov[0],
        ov[1],
        g_w_qkv,
        vec[0, :QKV].reshape(3, HC),
        feats[:, :, :HD],
        feats[:, :, HD:],
        g_w_out,
        vec[3],
        vec[4],
        vec[5],
        ob.astype(F32),
        vec[1],
        oc.astype(F32),
        vec[2],
    )


def solution(mesh):
    n_dp = mesh.shape["dp"]
    nh = max(0, (n_dp // 8).bit_length() - 1)
    return jax.shard_map(
        functools.partial(local, nh),
        mesh=mesh,
        in_specs=(
            P(("dp", "tensor"), None),
            P(),
            P(),
            P(None, None, "tensor"),
            P(None, "tensor"),
            P("tensor", None, None),
            P("tensor", None, None),
            P("tensor", None),
            P(),
            P(),
            P(),
            P(None, "tensor"),
            P("tensor"),
            P("tensor", None),
            P(),
            P("dp", None),
            P(("dp", "tensor"), None),
        ),
        out_specs=(
            P(("dp", "tensor"), None),
            P(("dp", "tensor"), None),
            P(),
            P(),
            P(None, None, "tensor"),
            P(None, "tensor"),
            P("tensor", None, None),
            P("tensor", None, None),
            P("tensor", None),
            P(),
            P(),
            P(),
            P(None, "tensor"),
            P("tensor"),
            P("tensor", None),
            P(),
        ),
        check_vma=False,
    )
```

```python
import functools
import math

import jax
import jax.numpy as jnp
from jax import lax
from jax.experimental import pallas as pl
from jax.experimental.pallas import tpu as pltpu
from jax.sharding import PartitionSpec as P

NORM_EPS = 1e-05
BF = jnp.bfloat16
F32 = jnp.float32
MESH = pl.DeviceIdType.MESH
NT = 4
D = 768
HD = 64
HPG = 3
HC = HPG * HD
NH = NT * HPG
U = 768
AUG = 80
QKV = 3 * HC
KINDS = 3
R_W = 96
R_G = (112, 96, 96)
ROWS_G = (896, 768, 768)
CB = 256
HALF_W = (48, 48)
HALF_G = ((64, 48), (48, 48), (48, 48))


def dot(a, b, ca=1, cb=0):
    return lax.dot_general(a, b, (((ca,), (cb,)), ((), ())), preferred_element_type=F32)


def mo(value, multiple):
    return pl.multiple_of(value, multiple)


def soft_pair(logits):
    top = jnp.max(logits, axis=0, keepdims=True)
    low = jnp.min(logits, axis=0, keepdims=True)
    e_pos = jnp.exp(logits - top)
    e_neg = jnp.exp(low - logits)
    p = e_pos * (1.0 / jnp.sum(e_pos, axis=0, keepdims=True))
    m = e_neg * (1.0 / jnp.sum(e_neg, axis=0, keepdims=True))
    return jnp.concatenate([p, m], axis=0)


def norm_stats(rows):
    mean = jnp.mean(rows, axis=-1, keepdims=True)
    centred = rows - mean
    var = jnp.mean(centred * centred, axis=-1, keepdims=True)
    inv = lax.rsqrt(var + NORM_EPS)
    return centred * inv, inv


def col(n):
    return pl.ds(mo(n * CB, CB), CB)


def layer_kernel(
    nh,
    seq_ref,
    x_ref,
    cot_ref,
    ln1g_ref,
    ln1b_ref,
    bout_ref,
    ln2g_ref,
    ln2b_ref,
    bproj_ref,
    a_own,
    b_own,
    c_own,
    ft_own,
    bp_own,
    res_ref,
    gin_ref,
    oa_ref,
    ob_ref,
    oc_ref,
    ov_ref,
    WA,
    WB,
    WC,
    FT,
    BP,
    R0A,
    R0B,
    R0C,
    RAA,
    RAB,
    RAC,
    RBA,
    RBB,
    RBC,
    ZRA,
    ZRB,
    ZRC,
    OA,
    OB,
    OC,
    RHA,
    RHB,
    RHC,
    LS,
    LR,
    LZ,
    N1,
    QK,
    VA,
    QF,
    KF,
    NM,
    ST,
    CT,
    CR,
    SQ,
    GR,
    MX,
    DI,
    MID,
    N2,
    N2T,
    UN,
    GN2,
    GML,
    ACT,
    ACTT,
    GP,
    GBF,
    GA,
    GC,
    GQ,
    VS,
    own_s,
    sm_s,
    sm_r,
    wz_s,
    w_s,
    w_r,
    g_s,
    g_r,
    z_r,
    o_s,
    o_r,
    h_s,
    h_r,
    l_s,
    l_r,
    lz_s,
    lz_r,
    c_s,
    c_r,
):
    dp = lax.axis_index("dp")
    z = lax.axis_index("tensor")
    T = x_ref.shape[0]
    NB = T // CB
    core = lax.rem(dp, 2)
    bx = lax.rem(dp // 2, 2)
    by = lax.rem(dp // 4, 2)
    d_core = 1 - 2 * core
    d_x = 2 * (1 - 2 * bx)
    d_y = 4 * (1 - 2 * by)
    slot = core * 4 + by * 2 + bx

    W = (WA, WB, WC)
    OWN = (a_own, b_own, c_own)
    R0 = (R0A, R0B, R0C)
    RA = (RAA, RAB, RAC)
    RB = (RBA, RBB, RBC)
    ZR = (ZRA, ZRB, ZRC)
    O = (OA, OB, OC)
    RH = (RHA, RHB, RHC)

    def flip(j):
        return lax.rem(z // 2 + j // 2, 2) * 2 + lax.rem(z + j, 2)

    def ff(j):
        return flip(lax.rem(NT - j, NT))

    def last(t):
        return flip(NT - 1 - t)

    def high(i):
        step = 8 * 2**i
        return dp + step * (1 - 2 * lax.rem(dp // step, 2))

    def rcopy(src, dst, ssem, rsem, dev):
        return pltpu.make_async_remote_copy(
            src_ref=src, dst_ref=dst, send_sem=ssem, recv_sem=rsem, device_id=dev, device_id_type=MESH
        )

    dev_x = (dp + d_x, z)
    dev_y = (dp + d_y, z)
    dev_c = (dp + d_core, z)
    slot_x = core * 4 + by * 2 + (1 - bx)
    slot_y = core * 4 + (1 - by) * 2 + bx
    slot_d = core * 4 + (1 - by) * 2 + (1 - bx)

    peers = [(dp + d_core, z), (dp + d_x, z), (dp + d_y, z)]
    peers += [(high(i), z) for i in range(nh)]
    peers += [(dp, lax.rem(z + o, NT)) for o in range(1, NT)]
    barrier = pltpu.get_barrier_semaphore()
    for peer in peers:
        pl.semaphore_signal(barrier, inc=1, device_id=peer, device_id_type=MESH)
    pl.semaphore_wait(barrier, len(peers))

    def wrows(k, g, s):
        return W[k].at[g, pl.ds(mo(s * R_W, R_W), R_W), :]

    def wrows4(k, g, c):
        return W[k].at[g, pl.ds(mo(c * 4 * R_W, R_W), 4 * R_W), :]

    def whalf(k, g, s, h):
        return W[k].at[g, pl.ds(mo(s * R_W + h * HALF_W[0], 16), HALF_W[h]), :]

    def w_z(k, g):
        rcopy(
            OWN[k].at[pl.ds(mo(slot * R_W, R_W), R_W), :], wrows(k, z, slot), wz_s.at[k, g], w_r.at[0, k, z], (dp, g)
        ).start()

    def w_wait(k, g, stage, ref):
        rcopy(ref, ref, w_s.at[0, k, g], w_r.at[stage, k, g], dev_c).wait_recv()

    def w_send(k, g, s_stage, r_stage, ref, dev):
        rcopy(ref, ref, w_s.at[s_stage, k, g], w_r.at[r_stage, k, g], dev).start()

    def w_1(k, g):
        mine = wrows(k, g, slot)
        w_wait(k, g, 0, mine)
        w_send(k, g, 0, 1, mine, dev_x)
        w_send(k, g, 1, 2, mine, dev_y)

    def w_2(k, g):
        w_wait(k, g, 1, wrows(k, g, slot_x))
        w_send(k, g, 2, 3, whalf(k, g, slot_x, 0), dev_y)
        w_wait(k, g, 2, wrows(k, g, slot_y))
        w_send(k, g, 3, 4, whalf(k, g, slot_y, 1), dev_x)

    def w_3(k, g):
        w_wait(k, g, 3, whalf(k, g, slot_d, 0))
        w_wait(k, g, 4, whalf(k, g, slot_d, 1))
        w_send(k, g, 4, 5, wrows4(k, g, core), dev_c)

    def w_4(k, g):
        w_wait(k, g, 5, wrows4(k, g, 1 - core))
        sent = [wrows(k, g, slot)] * 2 + [whalf(k, g, slot_x, 0), whalf(k, g, slot_y, 1), wrows4(k, g, core)]
        for st, ref in enumerate(sent):
            rcopy(ref, ref, w_s.at[st, k, g], w_r.at[0, k, g], dev_c).wait_send()

    def w_z_done(k):
        one = OWN[k].at[pl.ds(mo(slot * R_W, R_W), R_W), :]
        for i in range(1, NT):
            g = flip(i)
            rcopy(one, wrows(k, z, slot), wz_s.at[k, g], w_r.at[0, k, z], (dp, g)).wait_send()

    small = ((ft_own, FT), (bp_own, BP))

    def small_send():
        for i, (own, buf) in enumerate(small):
            for o in range(1, NT):
                rcopy(own, buf.at[z], sm_s.at[i, o - 1], sm_r.at[i, z], (dp, lax.rem(z + o, NT))).start()

    def small_wait(g):
        for i, (own, buf) in enumerate(small):
            rcopy(own, buf.at[g], sm_s.at[i, 0], sm_r.at[i, g], (dp, z)).wait_recv()

    def small_done():
        for i, (own, buf) in enumerate(small):
            for o in range(1, NT):
                rcopy(own, buf.at[z], sm_s.at[i, o - 1], sm_r.at[i, z], (dp, lax.rem(z + o, NT))).wait_send()

    local = [
        pltpu.make_async_copy(ft_own, FT.at[z], own_s.at[0]),
        pltpu.make_async_copy(bp_own, BP.at[z], own_s.at[1]),
        pltpu.make_async_copy(a_own, WA.at[z, pl.ds(0, D), :], own_s.at[2]),
        pltpu.make_async_copy(b_own, WB.at[z], own_s.at[3]),
        pltpu.make_async_copy(c_own, WC.at[z], own_s.at[4]),
    ]
    small_send()
    for i in range(1, NT):
        w_z(0, flip(i))
    for copy in local:
        copy.start()
    for j in range(1, NT):
        w_z(1, ff(j))
        w_z(2, ff(j))

    def grows(k, g, s, n=1):
        return W[k].at[g, pl.ds(mo(s * R_G[k], 16), n * R_G[k]), :]

    def add_rows(dst, start, src, n):
        blk = 16 if n % 32 else 32

        def body(i, _):
            at = pl.ds(mo(start + i * blk, 16), blk)
            dst[at, :] = (dst[at, :].astype(F32) + src[pl.ds(mo(i * blk, 16), blk), :].astype(F32)).astype(BF)
            return 0

        lax.fori_loop(0, n // blk, body, 0)

    def ghalf(k, g, s, h):
        return W[k].at[g, pl.ds(mo(s * R_G[k] + h * HALF_G[k][0], 16), HALF_G[k][h]), :]

    def ra(k, g, h):
        return RA[k].at[g, pl.ds(h * HALF_G[k][0], HALF_G[k][h]), :]

    def g_wait(k, g, stage, ref):
        rcopy(ref, ref, g_s.at[0, k, g], g_r.at[stage, k, g], dev_c).wait_recv()

    def g_send(k, g, stage, src, dst, dev):
        rcopy(src, dst, g_s.at[stage, k, g], g_r.at[stage, k, g], dev).start()

    def g_core(k, g):
        g_send(k, g, 0, grows(k, g, (1 - core) * 4, 4), R0[k].at[g], dev_c)

    def g_a(k, g):
        g_wait(k, g, 0, R0[k].at[g])
        add_rows(W[k].at[g], core * 4 * R_G[k], R0[k].at[g], 4 * R_G[k])
        g_send(k, g, 1, ghalf(k, g, slot_d, 0), ra(k, g, 0), dev_x)
        g_send(k, g, 2, ghalf(k, g, slot_d, 1), ra(k, g, 1), dev_y)

    def g_b(k, g):
        g_wait(k, g, 1, ra(k, g, 0))
        add_rows(W[k].at[g], slot_y * R_G[k], ra(k, g, 0), HALF_G[k][0])
        g_send(k, g, 4, grows(k, g, slot_y), RB[k].at[g, 1], dev_y)
        g_wait(k, g, 2, ra(k, g, 1))
        add_rows(W[k].at[g], slot_x * R_G[k] + HALF_G[k][0], ra(k, g, 1), HALF_G[k][1])
        g_send(k, g, 3, grows(k, g, slot_x), RB[k].at[g, 0], dev_x)

    def g_z(k, g):
        for i in range(2):
            g_wait(k, g, 3 + i, RB[k].at[g, i])
            add_rows(W[k].at[g], slot * R_G[k], RB[k].at[g, i], R_G[k])

        @pl.when(g != z)
        def _():
            rcopy(grows(k, g, slot), ZR[k].at[z], g_s.at[5, k, g], z_r.at[k, z], (dp, g)).start()

    def g_done(k, g):
        one = grows(k, g, 0)
        sent = [grows(k, g, 0, 4), ghalf(k, g, 0, 0), ghalf(k, g, 0, 1), one, one]
        for st, ref in enumerate(sent):
            rcopy(ref, ref, g_s.at[st, k, g], g_r.at[0, k, g], dev_c).wait_send()

        @pl.when(g != z)
        def _():
            rcopy(one, one, g_s.at[5, k, g], g_r.at[0, k, g], dev_c).wait_send()

    def orows(k, s, n=1):
        return O[k].at[pl.ds(mo(s * R_G[k], 16), n * R_G[k]), :]

    def ohalf(k, s, h):
        return O[k].at[pl.ds(mo(s * R_G[k] + h * HALF_G[k][0], 16), HALF_G[k][h]), :]

    def o_wait(k, stage, ref):
        rcopy(ref, ref, o_s.at[stage, k], o_r.at[stage, k], dev_c).wait_recv()

    def o_send(k, stage, ref, dev):
        rcopy(ref, ref, o_s.at[stage, k], o_r.at[stage, k], dev).start()

    def g_sum(k):
        for o in range(1, NT):
            zz = lax.rem(z + o, NT)
            ref = ZR[k].at[zz]
            rcopy(ref, ref, g_s.at[0, k, 0], z_r.at[k, zz], (dp, z)).wait_recv()
        blk = 16

        def body(i, _):
            at = pl.ds(mo(i * blk, 16), blk)
            mine = pl.ds(mo(slot * R_G[k] + i * blk, 16), blk)
            acc = W[k][z, mine, :].astype(F32)
            for o in range(1, NT):
                acc = acc + ZR[k][lax.rem(z + o, NT), at, :].astype(F32)
            O[k][mine, :] = acc.astype(BF)
            return 0

        lax.fori_loop(0, R_G[k] // blk, body, 0)
        for i in range(nh):
            rcopy(orows(k, slot), RH[k].at[i], h_s.at[i, k], h_r.at[i, k], (high(i), z)).start()
            rcopy(orows(k, slot), RH[k].at[i], h_s.at[i, k], h_r.at[i, k], (high(i), z)).wait()
            add_rows(O[k], slot * R_G[k], RH[k].at[i], R_G[k])
        o_send(k, 0, orows(k, slot), dev_x)
        o_send(k, 1, orows(k, slot), dev_y)

    def o_2(k):
        o_wait(k, 0, orows(k, slot_x))
        o_send(k, 2, ohalf(k, slot_x, 0), dev_y)
        o_wait(k, 1, orows(k, slot_y))
        o_send(k, 3, ohalf(k, slot_y, 1), dev_x)

    def o_3(k):
        o_wait(k, 2, ohalf(k, slot_d, 0))
        o_wait(k, 3, ohalf(k, slot_d, 1))
        o_send(k, 4, orows(k, core * 4, 4), dev_c)

    def o_4(k, out, sem):
        o_wait(k, 4, orows(k, (1 - core) * 4, 4))
        copy = pltpu.make_async_copy(O[k], out, sem)
        copy.start()
        sent = [orows(k, slot)] * 2 + [ohalf(k, slot_x, 0), ohalf(k, slot_y, 1), orows(k, core * 4, 4)]
        for st, ref in enumerate(sent):
            rcopy(ref, ref, o_s.at[st, k], o_r.at[0, k], dev_c).wait_send()
        return copy

    def iota(shape, axis):
        return lax.broadcasted_iota(jnp.int32, shape, axis)

    causal = iota((CB, CB), 0) <= iota((CB, CB), 1)
    aug_tail = jnp.where(iota((16, T), 0) < 2, 1.0, 0.0).astype(BF)
    ones_rows = jnp.ones((16, T), BF)
    head_mask = (iota((HC, HC), 0) // HD) == (iota((HC, HC), 1) // HD)

    def pick(which):
        r = iota((2 * HD, HC), 0) - which * HD
        return (r == lax.rem(iota((2 * HD, HC), 1), HD)).astype(BF)

    def pick_back(which):
        r = iota((HC, 2 * HD), 1) - which * HD
        return (r == lax.rem(iota((HC, 2 * HD), 0), HD)).astype(BF)

    def block_diag(g, which):
        return jnp.where(head_mask, dot(FT[g], pick(which)), 0.0).astype(BF)

    first_end = seq_ref[0, 0]
    second_end = seq_ref[0, 0] + seq_ref[0, 1]

    def seq_id(zz):
        start = zz * T
        return (start >= first_end).astype(jnp.int32) + (start >= second_end).astype(jnp.int32)

    from_prev = jnp.logical_and(z > 0, seq_id(z) == seq_id(z - 1))
    from_next = jnp.logical_and(z < NT - 1, seq_id(z) == seq_id(z + 1))

    RB_ = 64

    def p0(i, _):
        at = pl.ds(mo(i * RB_, RB_), RB_)
        xh, _inv = norm_stats(x_ref[at, :].astype(F32))
        N1[at, :] = (xh * ln1g_ref[...] + ln1b_ref[...]).astype(BF)
        return 0

    lax.fori_loop(0, T // RB_, p0, 0)
    for g in range(NT):
        WA[g, pl.ds(D, ROWS_G[0] - D), :] = jnp.zeros((ROWS_G[0] - D, D), BF)
    GQ[pl.ds(QKV, D - QKV), :] = jnp.zeros((D - QKV, T), BF)

    @pl.when(z == 0)
    def _():
        CR[...] = jnp.zeros_like(CR)

    @pl.when(z == NT - 1)
    def _():
        GR[...] = jnp.zeros_like(GR)

    for copy in local[:3]:
        copy.wait()

    def p1(j, _):
        g = flip(j)

        @pl.when(j == 1)
        def _():
            small_wait(flip(1))
            w_1(0, flip(1))
            w_2(0, flip(1))
            w_1(0, flip(2))
            w_1(0, flip(3))
            w_3(0, flip(1))
            w_2(0, flip(2))
            w_4(0, flip(1))

        @pl.when(j == 2)
        def _():
            small_wait(flip(2))
            w_2(0, flip(3))
            w_3(0, flip(2))
            w_4(0, flip(2))

        @pl.when(j == 3)
        def _():
            small_wait(flip(3))
            w_3(0, flip(3))
            w_4(0, flip(3))

        bias = jnp.transpose(BP[g])[:QKV, 0:1]
        qkv = (dot(WA[g, pl.ds(0, QKV), :], N1[...], 1, 1) + bias).astype(BF)
        QK[g] = qkv[: 2 * HC]
        ql = dot(block_diag(g, 0), qkv[:HC])
        kl = dot(block_diag(g, 1), qkv[HC : 2 * HC])
        for h in range(HPG):
            hh = g * HPG + h
            rows = slice(h * HD, (h + 1) * HD)
            qf = soft_pair(ql[rows]).astype(BF)
            kf = soft_pair(kl[rows]).astype(BF)
            va = jnp.concatenate([qkv[2 * HC + h * HD : 2 * HC + (h + 1) * HD], aug_tail], axis=0)
            QF[hh] = qf
            KF[hh] = kf
            VA[hh] = va
            kn = kf.T
            ST[hh] = dot(va, kn)
            for qi in range(NB):
                qs = slice(qi * CB, (qi + 1) * CB)
                acc = None
                for ki in range(qi + 1):
                    ks = slice(ki * CB, (ki + 1) * CB)
                    s = dot(kn[ks], qf[:, qs])
                    if ki == qi:
                        s = jnp.where(causal, s, 0.0)
                    part = dot(va[:, ks], s.astype(BF))
                    acc = part if acc is None else acc + part
                NM[hh, :, qs] = acc[: HD + 8]

        @pl.when(z == 0)
        def _():
            for h in range(HPG):
                SQ[g, h] = ST[g * HPG + h].astype(BF)
            rcopy(SQ.at[g], CR.at[g], c_s.at[0, g], c_r.at[0, g], (dp, z + 1)).start()

        return 0

    lax.fori_loop(0, NT, p1, 0)
    w_1(1, ff(1))
    w_1(2, ff(1))

    def chain_wait(buf, g, stage):
        rcopy(buf.at[g], buf.at[g], c_s.at[stage, g], c_r.at[stage, g], (dp, z)).wait_recv()

    def p1b(g, _):
        @pl.when(z > 0)
        def _():
            chain_wait(CR, g, 0)

        for h in range(HPG):
            CT[g * HPG + h] = jnp.where(from_prev, CR[g, h], jnp.zeros((AUG, 2 * HD), BF))

        @pl.when(jnp.logical_and(z > 0, z < NT - 1))
        def _():
            for h in range(HPG):
                hh = g * HPG + h
                SQ[g, h] = (ST[hh] + CT[hh].astype(F32)).astype(BF)
            rcopy(SQ.at[g], CR.at[g], c_s.at[0, g], c_r.at[0, g], (dp, z + 1)).start()

        return 0

    lax.fori_loop(0, NT, p1b, 0)
    w_2(1, ff(1))
    w_2(2, ff(1))

    def p1c(g, _):
        for h in range(HPG):
            hh = g * HPG + h
            num = NM[hh] + dot(CT[hh], QF[hh])[: HD + 8]
            inv = 1.0 / num[HD : HD + 1]
            DI[hh] = inv
            MX[g, pl.ds(h * HD, HD), :] = (num[:HD] * inv).astype(BF)
        return 0

    lax.fori_loop(0, NT, p1c, 0)

    def p2(n, _):
        acc = None
        for g in range(NT):
            part = dot(MX[g], WA[g, pl.ds(QKV, HC), col(n)], 0, 0)
            acc = part if acc is None else acc + part
        MID[:, col(n)] = x_ref[:, col(n)].astype(F32) + (acc + bout_ref[:, col(n)])
        return 0

    lax.fori_loop(0, D // CB, p2, 0)

    def p2b(i, _):
        at = pl.ds(mo(i * 128, 128), 128)
        xh, _inv = norm_stats(MID[at, :])
        n2 = (xh * ln2g_ref[...] + ln2b_ref[...]).astype(BF)
        N2[at, :] = n2
        N2T[:, at] = n2.T
        return 0

    lax.fori_loop(0, T // 128, p2b, 0)
    w_3(1, ff(1))
    w_3(2, ff(1))
    w_1(1, ff(2))
    w_1(2, ff(2))

    @pl.when(z < NT - 1)
    def _():
        for g in range(NT):
            rcopy(SQ.at[g], SQ.at[g], c_s.at[0, g], c_r.at[0, g], (dp, z)).wait_send()

    UN[...] = jnp.zeros_like(UN)
    GN2[...] = jnp.zeros_like(GN2)
    for copy in local[3:]:
        copy.wait()

    cc = math.sqrt(2.0 / math.pi)

    def p3(j, _):
        g = ff(j)

        @pl.when(j == 1)
        def _():
            w_4(1, ff(1))
            w_4(2, ff(1))
            w_1(1, ff(3))
            w_1(2, ff(3))

        @pl.when(j == 2)
        def _():
            w_4(1, ff(2))
            w_4(2, ff(2))

        @pl.when(j == 3)
        def _():
            w_4(1, ff(3))
            w_4(2, ff(3))

        def units(u, total):
            pre = dot(N2[...], WB[g, :, col(u)]) + BP[g, pl.ds(1, 1), col(u)]
            sq = pre * pre
            t = jnp.tanh(cc * pre * (1.0 + 0.044715 * sq))
            act = (0.5 * pre * (1.0 + t)).astype(BF)
            slope = 0.5 * (1.0 + t) + (0.5 * cc) * pre * (1.0 - t * t) * (1.0 + (3 * 0.044715) * sq)
            ACT[:, col(u)] = act
            ACTT[col(u), :] = act.T
            gact = dot(cot_ref[...], WC[g, col(u), :], 1, 1)
            gpre = (gact * slope).astype(BF)
            GP[:, col(u)] = gpre
            GBF[g, :, col(u)] = jnp.sum(gpre.astype(F32), axis=0, keepdims=True)
            return total

        lax.fori_loop(0, U // CB, units, 0)

        @pl.when(j == 1)
        def _():
            w_3(1, ff(2))
            w_3(2, ff(2))

        @pl.when(j >= 1)
        def _():
            g_a(1, ff(j - 1))
            g_a(2, ff(j - 1))

        @pl.when(j == 2)
        def _():
            w_3(1, ff(3))
            w_3(2, ff(3))
            g_b(1, ff(0))
            g_b(2, ff(0))

        @pl.when(j == 3)
        def _():
            g_z(1, ff(0))
            g_z(2, ff(0))

        def outs(n, _):
            UN[:, col(n)] += dot(ACT[...], WC[g, :, col(n)])
            GN2[:, col(n)] += dot(GP[...], WB[g, col(n), :], 1, 1)
            return 0

        lax.fori_loop(0, D // CB, outs, 0)

        @pl.when(j == 0)
        def _():
            w_2(1, ff(2))
            w_2(2, ff(2))

        @pl.when(j == 1)
        def _():
            w_2(1, ff(3))
            w_2(2, ff(3))

        def grads(n, _):
            WC[g, col(n), :] = dot(ACTT[col(n), :], cot_ref[...]).astype(BF)
            WB[g, col(n), :] = dot(N2T[col(n), :], GP[...]).astype(BF)
            return 0

        lax.fori_loop(0, D // CB, grads, 0)
        g_core(1, g)
        g_core(2, g)

        return 0

    lax.fori_loop(0, NT, p3, 0)
    g_b(1, ff(1))
    g_b(2, ff(1))

    VS[...] = jnp.zeros_like(VS)

    def p4(i, _):
        at = pl.ds(mo(i * RB_, RB_), RB_)
        mid = MID[at, :]
        res_ref[at, :] = (mid + UN[at, :] + bproj_ref[...]).astype(BF)
        xh, inv = norm_stats(mid)
        gn = GN2[at, :]
        gh = gn * ln2g_ref[...]
        c1 = jnp.mean(gh, axis=-1, keepdims=True)
        c2 = jnp.mean(gh * xh, axis=-1, keepdims=True)
        cot = cot_ref[at, :].astype(F32)
        gm = cot + inv * (gh - c1 - xh * c2)
        GN2[at, :] = gm
        low = gm.astype(BF)
        GML[at, :] = low
        VS[0] += jnp.sum(cot, axis=0, keepdims=True)
        VS[1] += jnp.sum(low.astype(F32), axis=0, keepdims=True)
        VS[2] += jnp.sum(gn * xh, axis=0, keepdims=True)
        VS[3] += jnp.sum(gn, axis=0, keepdims=True)
        return 0

    lax.fori_loop(0, T // RB_, p4, 0)
    g_a(1, ff(3))
    g_a(2, ff(3))

    tail_row = iota((16, T), 0)

    def p5a(g, _):
        gmix = dot(WA[g, pl.ds(QKV, HC), :], GML[...], 1, 1).astype(BF).astype(F32)
        mix = MX[g]
        WA[g, pl.ds(QKV, HC), :] = dot(mix, GML[...]).astype(BF)
        prod = gmix * mix.astype(F32)
        for h in range(HPG):
            hh = g * HPG + h
            rows = slice(h * HD, (h + 1) * HD)
            inv = DI[hh]
            gden = -jnp.sum(prod[rows], axis=0, keepdims=True) * inv
            hi = gden.astype(BF).astype(F32)
            lo = gden - hi
            tail = jnp.where(tail_row == 0, hi, jnp.where(tail_row == 1, lo, 0.0)).astype(BF)
            ga = jnp.concatenate([(gmix[rows] * inv).astype(BF), tail], axis=0)
            GA[hh] = ga
            gc = dot(ga, QF[hh].T)
            GC[hh] = gc
            SQ[g, h] = gc.astype(BF)

        @pl.when(z == NT - 1)
        def _():
            rcopy(SQ.at[g], GR.at[g], c_s.at[1, g], c_r.at[1, g], (dp, z - 1)).start()

        return 0

    lax.fori_loop(0, NT, p5a, 0)
    g_z(1, ff(1))
    g_z(2, ff(1))

    def chain_back(g, _):
        @pl.when(z < NT - 1)
        def _():
            chain_wait(GR, g, 1)
            for h in range(HPG):
                hh = g * HPG + h
                later = jnp.where(from_next, GR[g, h].astype(F32), 0.0)
                SQ[g, h] = (GC[hh] + later).astype(BF)

        @pl.when(jnp.logical_and(z > 0, z < NT - 1))
        def _():
            rcopy(SQ.at[g], GR.at[g], c_s.at[1, g], c_r.at[1, g], (dp, z - 1)).start()

        return 0

    lax.fori_loop(0, NT, chain_back, 0)
    g_b(1, ff(2))
    g_b(2, ff(2))
    GN1 = UN
    GN1[...] = jnp.zeros_like(GN1)

    def p5b(t, _):
        g = last(t)
        gql = []
        gkl = []
        for h in range(HPG):
            hh = g * HPG + h
            qf = QF[hh]
            kf = KF[hh]
            va = VA[hh]
            ga = GA[hh]
            kn = kf.T
            vn = va.T
            ctt = CT[hh].T
            gkc = jnp.where(from_next, GR[g, h], jnp.zeros((AUG, 2 * HD), BF))
            gkt = gkc.T
            gq = [None] * NB
            gk = [None] * NB
            gv = [None] * NB
            for qi in range(NB):
                qs = slice(qi * CB, (qi + 1) * CB)
                gq[qi] = dot(ctt, ga[:, qs])
                for ki in range(qi + 1):
                    ks = slice(ki * CB, (ki + 1) * CB)
                    s = dot(kn[ks], qf[:, qs])
                    gs = dot(vn[ks], ga[:, qs])
                    if ki == qi:
                        s = jnp.where(causal, s, 0.0)
                        gs = jnp.where(causal, gs, 0.0)
                    s = s.astype(BF)
                    gs = gs.astype(BF)
                    gq[qi] = gq[qi] + dot(kf[:, ks], gs)
                    pk = dot(qf[:, qs], gs, 1, 1)
                    pv = dot(ga[:, qs], s, 1, 1)[:HD]
                    gk[ki] = pk if gk[ki] is None else gk[ki] + pk
                    gv[ki] = pv if gv[ki] is None else gv[ki] + pv
            for ki in range(NB):
                ks = slice(ki * CB, (ki + 1) * CB)
                gk[ki] = gk[ki] + dot(gkt, va[:, ks])
                gv[ki] = gv[ki] + dot(gkc[:HD], kf[:, ks])
                GQ[pl.ds(2 * HC + h * HD, HD), ks] = gv[ki].astype(BF)

            def back(feat, grads):
                out = []
                for b in range(NB):
                    bs = slice(b * CB, (b + 1) * CB)
                    p = feat[:HD, bs].astype(F32)
                    m = feat[HD:, bs].astype(F32)
                    g1 = grads[b][:HD]
                    g2 = grads[b][HD:]
                    s1 = jnp.sum(g1 * p, axis=0, keepdims=True)
                    s2 = jnp.sum(g2 * m, axis=0, keepdims=True)
                    out.append((p * (g1 - s1) - m * (g2 - s2)).astype(BF))
                return jnp.concatenate(out, axis=1)

            gql.append(back(qf, gq))
            gkl.append(back(kf, gk))

        @pl.when(t >= 1)
        def _():
            g_a(0, last(t - 1))

        @pl.when(t == 1)
        def _():
            g_b(1, ff(3))
            g_b(2, ff(3))

        @pl.when(t == 2)
        def _():
            g_z(1, ff(3))
            g_z(2, ff(3))

        @pl.when(t >= 2)
        def _():
            g_b(0, last(t - 2))

        @pl.when(t == 3)
        def _():
            g_z(0, last(0))

        comp = None
        for which, parts in ((0, gql), (1, gkl)):
            glog = jnp.concatenate(parts, axis=0)
            own = QK[g, pl.ds(which * HC, HC), :]
            GQ[pl.ds(which * HC, HC), :] = dot(block_diag(g, which), glog, 0, 0).astype(BF)
            gfeat = jnp.where(head_mask, dot(own, glog, 1, 1), 0.0).astype(BF)
            part = dot(gfeat, pick_back(which))
            comp = part if comp is None else comp + part
        comp = comp.astype(BF)
        gq_all = GQ[...]
        gqn = gq_all[:QKV].T
        for n in range(D // CB):
            GN1[:, n * CB : (n + 1) * CB] += dot(gqn, WA[g, pl.ds(0, QKV), n * CB : (n + 1) * CB])
        WA[g, pl.ds(0, QKV), :] = dot(gq_all[:QKV], N1[...]).astype(BF)
        for b in range(HC // 32):
            WA[g, pl.ds(D, 32), b * 128 : (b + 1) * 128] = comp[b * 32 : (b + 1) * 32]
        vec = dot(ones_rows, gq_all, 1, 1)
        row = iota((16, D), 0)
        vec = jnp.where(row == 1, GBF[g], vec)
        for i in range(4):
            vec = jnp.where(row == 2 + i, VS[i], vec)
        WA[g, pl.ds(D + 32, 16), :] = vec.astype(BF)
        g_core(0, g)

        @pl.when(t == 0)
        def _():
            g_z(1, ff(2))
            g_z(2, ff(2))

        return 0

    lax.fori_loop(0, NT, p5b, 0)

    LS[...] = jnp.zeros_like(LS)

    def p6(i, _):
        at = pl.ds(mo(i * RB_, RB_), RB_)
        xh, inv = norm_stats(x_ref[at, :].astype(F32))
        gn = GN1[at, :]
        gh = gn * ln1g_ref[...]
        c1 = jnp.mean(gh, axis=-1, keepdims=True)
        c2 = jnp.mean(gh * xh, axis=-1, keepdims=True)
        gin_ref[at, :] = (GN2[at, :] + inv * (gh - c1 - xh * c2)).astype(BF)
        LS[0, 0:1, :] += jnp.sum(gn * xh, axis=0, keepdims=True)
        LS[0, 1:2, :] += jnp.sum(gn, axis=0, keepdims=True)
        return 0

    lax.fori_loop(0, T // RB_, p6, 0)

    partners = [dp + d_core, dp + d_x, dp + d_y] + [high(i) for i in range(nh)]

    steps = len(partners)

    def small_start(i):
        rcopy(LS.at[i], LR.at[i], l_s.at[i], l_r.at[i], (partners[i], z)).start()

    def small_end(i):
        rcopy(LS.at[i], LR.at[i], l_s.at[i], l_r.at[i], (partners[i], z)).wait()
        LS[i + 1] = LS[i] + LR[i]

    small_start(0)
    g_a(0, last(3))
    g_b(0, last(2))
    small_end(0)
    small_start(1)
    g_z(0, last(1))
    g_sum(1)
    g_sum(2)
    small_end(1)
    small_start(2)
    g_b(0, last(3))
    g_z(0, last(2))
    small_end(2)
    for i in range(3, steps):
        small_start(i)
        small_end(i)
    LZ[z] = LS[steps]
    for o in range(1, NT):
        rcopy(LS.at[steps], LZ.at[z], lz_s.at[o - 1], lz_r.at[z], (dp, lax.rem(z + o, NT))).start()
    o_2(1)
    o_2(2)
    g_z(0, last(3))
    g_sum(0)
    o_3(1)
    o_3(2)
    o_2(0)
    outs = [o_4(1, ob_ref, own_s.at[0]), o_4(2, oc_ref, own_s.at[1])]
    for o in range(1, NT):
        zz = lax.rem(z + o, NT)
        rcopy(LZ.at[zz], LZ.at[zz], lz_s.at[o - 1], lz_r.at[zz], (dp, z)).wait_recv()
    total = LZ[0]
    for zz in range(1, NT):
        total = total + LZ[zz]
    ov_ref[...] = total
    o_3(0)
    outs.append(o_4(0, oa_ref, own_s.at[2]))
    for copy in outs:
        copy.wait()

    for o in range(1, NT):
        rcopy(LS.at[steps], LZ.at[z], lz_s.at[o - 1], lz_r.at[z], (dp, lax.rem(z + o, NT))).wait_send()
    small_done()
    for k in range(KINDS):
        w_z_done(k)
        for g in range(NT):
            g_done(k, g)

    @pl.when(z > 0)
    def _():
        for g in range(NT):
            rcopy(SQ.at[g], SQ.at[g], c_s.at[1, g], c_r.at[1, g], (dp, z)).wait_send()


def layer_call(nh, T, *args):
    def vm(shape, dtype=BF):
        return pltpu.VMEM(shape, dtype)

    dma = pltpu.SemaphoreType.DMA
    nhb = max(nh, 1)
    nst = 3 + nh
    scratch = [
        vm((NT, ROWS_G[0], D)),
        vm((NT, D, U)),
        vm((NT, U, D)),
        vm((NT, HC, 2 * HD)),
        vm((NT, 8, D), F32),
    ]
    scratch += [vm((NT, 4 * r, D)) for r in R_G]
    scratch += [vm((NT, r, D)) for r in R_G]
    scratch += [vm((NT, 2, r, D)) for r in R_G]
    scratch += [vm((NT, r, D)) for r in R_G]
    scratch += [vm((rows, D)) for rows in ROWS_G]
    scratch += [vm((nhb, r if nh else 16, D)) for r in R_G]
    scratch += [vm((nst + 1, 8, D), F32), vm((nst, 8, D), F32), vm((NT, 8, D), F32)]
    scratch += [
        vm((T, D)),
        vm((NT, 2 * HC, T)),
        vm((NH, AUG, T)),
        vm((NH, 2 * HD, T)),
        vm((NH, 2 * HD, T)),
        vm((NH, HD + 8, T), F32),
        vm((NH, AUG, 2 * HD), F32),
        vm((NH, AUG, 2 * HD)),
        vm((NT, HPG, AUG, 2 * HD)),
        vm((NT, HPG, AUG, 2 * HD)),
        vm((NT, HPG, AUG, 2 * HD)),
        vm((NT, HC, T)),
        vm((NH, 1, T), F32),
        vm((T, D), F32),
        vm((T, D)),
        vm((D, T)),
        vm((T, D), F32),
        vm((T, D), F32),
        vm((T, D)),
        vm((T, U)),
        vm((U, T)),
        vm((T, U)),
        vm((NT, 1, U), F32),
        vm((NH, AUG, T)),
        vm((NH, AUG, 2 * HD), F32),
        vm((D, T)),
        vm((4, 1, D), F32),
    ]
    scratch += [
        dma((5,)),
        dma((2, NT - 1)),
        dma((2, NT)),
        dma((KINDS, NT)),
        dma((5, KINDS, NT)),
        dma((6, KINDS, NT)),
        dma((6, KINDS, NT)),
        dma((5, KINDS, NT)),
        dma((KINDS, NT)),
        dma((5, KINDS)),
        dma((5, KINDS)),
        dma((nhb, KINDS)),
        dma((nhb, KINDS)),
        dma((nst,)),
        dma((nst,)),
        dma((NT - 1,)),
        dma((NT,)),
        dma((2, NT)),
        dma((2, NT)),
    ]
    vmem = pl.BlockSpec(memory_space=pltpu.VMEM)
    hbm = pl.BlockSpec(memory_space=pl.ANY)
    return pl.pallas_call(
        functools.partial(layer_kernel, nh),
        out_shape=(
            jax.ShapeDtypeStruct((T, D), BF),
            jax.ShapeDtypeStruct((T, D), BF),
            jax.ShapeDtypeStruct((ROWS_G[0], D), BF),
            jax.ShapeDtypeStruct((D, U), BF),
            jax.ShapeDtypeStruct((U, D), BF),
            jax.ShapeDtypeStruct((8, D), F32),
        ),
        in_specs=[pl.BlockSpec(memory_space=pltpu.SMEM)] + [vmem] * 8 + [hbm] * 5,
        out_specs=(vmem, vmem, hbm, hbm, hbm, vmem),
        scratch_shapes=scratch,
        compiler_params=pltpu.CompilerParams(
            collective_id=0, has_side_effects=True, vmem_limit_bytes=67043328
        ),
    )(*args)


def local(
    nh,
    tokens_in,
    ln1_gain,
    ln1_bias,
    w_qkv,
    b_qkv,
    feat_q,
    feat_k,
    w_out,
    b_out,
    ln2_gain,
    ln2_bias,
    w_fc,
    b_fc,
    w_proj,
    b_proj,
    seq_lengths,
    cotangent,
):
    T = tokens_in.shape[0]
    a_own = jnp.concatenate([jnp.transpose(w_qkv, (1, 2, 0)).reshape(QKV, D), w_out], axis=0)
    ft_own = jnp.concatenate(
        [jnp.transpose(feat_q, (0, 2, 1)).reshape(HC, HD), jnp.transpose(feat_k, (0, 2, 1)).reshape(HC, HD)],
        axis=1,
    )
    bq = jnp.pad(b_qkv.reshape(1, QKV), ((0, 0), (0, D - QKV)))
    bp_own = jnp.concatenate([bq, b_fc.reshape(1, U), jnp.zeros((6, D), F32)], axis=0)

    def row(v):
        return v.reshape(1, D)

    res, gin, oa, ob, oc, ov = layer_call(
        nh,
        T,
        seq_lengths,
        tokens_in,
        cotangent,
        row(ln1_gain),
        row(ln1_bias),
        row(b_out),
        row(ln2_gain),
        row(ln2_bias),
        row(b_proj),
        a_own,
        w_fc,
        w_proj,
        ft_own,
        bp_own,
    )
    g_w_qkv = jnp.transpose(oa[:QKV].reshape(3, HC, D), (2, 0, 1)).astype(F32)
    g_w_out = oa[QKV:D].astype(F32)
    feats = jnp.transpose(oa[D : D + 32].reshape(32, HC // 32, 2 * HD), (1, 0, 2)).reshape(HC, 2 * HD)
    feats = feats.astype(F32).reshape(HPG, HD, 2 * HD)
    vec = oa[D + 32 : D + 48].astype(F32)
    return (
        res,
        gin,
        ov[0],
        ov[1],
        g_w_qkv,
        vec[0, :QKV].reshape(3, HC),
        feats[:, :, :HD],
        feats[:, :, HD:],
        g_w_out,
        vec[3],
        vec[4],
        vec[5],
        ob.astype(F32),
        vec[1],
        oc.astype(F32),
        vec[2],
    )


def solution(mesh):
    n_dp = mesh.shape["dp"]
    nh = max(0, (n_dp // 8).bit_length() - 1)
    return jax.shard_map(
        functools.partial(local, nh),
        mesh=mesh,
        in_specs=(
            P(("dp", "tensor"), None),
            P(),
            P(),
            P(None, None, "tensor"),
            P(None, "tensor"),
            P("tensor", None, None),
            P("tensor", None, None),
            P("tensor", None),
            P(),
            P(),
            P(),
            P(None, "tensor"),
            P("tensor"),
            P("tensor", None),
            P(),
            P("dp", None),
            P(("dp", "tensor"), None),
        ),
        out_specs=(
            P(("dp", "tensor"), None),
            P(("dp", "tensor"), None),
            P(),
            P(),
            P(None, None, "tensor"),
            P(None, "tensor"),
            P("tensor", None, None),
            P("tensor", None, None),
            P("tensor", None),
            P(),
            P(),
            P(),
            P(None, "tensor"),
            P("tensor"),
            P("tensor", None),
            P(),
        ),
        check_vma=False,
    )
```

```python
import functools
import math

import jax
import jax.numpy as jnp
from jax import lax
from jax.experimental import pallas as pl
from jax.experimental.pallas import tpu as pltpu
from jax.sharding import PartitionSpec as P

NORM_EPS = 1e-05
BF = jnp.bfloat16
F32 = jnp.float32
MESH = pl.DeviceIdType.MESH
NT = 4
D = 768
HD = 64
HPG = 3
HC = HPG * HD
NH = NT * HPG
U = 768
AUG = 80
QKV = 3 * HC
KINDS = 3
R_W = 96
R_G = (112, 96, 96)
ROWS_G = (896, 768, 768)
CB = 256
HALF_W = (48, 48)
HALF_G = ((64, 48), (48, 48), (48, 48))


def dot(a, b, ca=1, cb=0):
    return lax.dot_general(a, b, (((ca,), (cb,)), ((), ())), preferred_element_type=F32)


def mo(value, multiple):
    return pl.multiple_of(value, multiple)


def soft_pair(logits):
    top = jnp.max(logits, axis=0, keepdims=True)
    low = jnp.min(logits, axis=0, keepdims=True)
    e_pos = jnp.exp(logits - top)
    e_neg = jnp.exp(low - logits)
    p = e_pos * (1.0 / jnp.sum(e_pos, axis=0, keepdims=True))
    m = e_neg * (1.0 / jnp.sum(e_neg, axis=0, keepdims=True))
    return jnp.concatenate([p, m], axis=0)


def norm_stats(rows):
    mean = jnp.mean(rows, axis=-1, keepdims=True)
    centred = rows - mean
    var = jnp.mean(centred * centred, axis=-1, keepdims=True)
    inv = lax.rsqrt(var + NORM_EPS)
    return centred * inv, inv


def col(n):
    return pl.ds(mo(n * CB, CB), CB)


def layer_kernel(
    nh,
    seq_ref,
    x_ref,
    cot_ref,
    ln1g_ref,
    ln1b_ref,
    bout_ref,
    ln2g_ref,
    ln2b_ref,
    bproj_ref,
    a_own,
    b_own,
    c_own,
    ft_own,
    bp_own,
    res_ref,
    gin_ref,
    oa_ref,
    ob_ref,
    oc_ref,
    ov_ref,
    WA,
    WB,
    WC,
    FT,
    BP,
    R0A,
    R0B,
    R0C,
    RAA,
    RAB,
    RAC,
    RBA,
    RBB,
    RBC,
    ZRA,
    ZRB,
    ZRC,
    OA,
    OB,
    OC,
    RHA,
    RHB,
    RHC,
    LS,
    LR,
    LZ,
    N1,
    QK,
    VA,
    QF,
    KF,
    NM,
    ST,
    CT,
    CR,
    SQ,
    GR,
    MX,
    DI,
    MID,
    N2,
    N2T,
    UN,
    GN2,
    GML,
    ACT,
    ACTT,
    GP,
    GBF,
    GA,
    GC,
    GQ,
    VS,
    own_s,
    sm_s,
    sm_r,
    wz_s,
    w_s,
    w_r,
    g_s,
    g_r,
    z_r,
    o_s,
    o_r,
    h_s,
    h_r,
    l_s,
    l_r,
    lz_s,
    lz_r,
    c_s,
    c_r,
):
    dp = lax.axis_index("dp")
    z = lax.axis_index("tensor")
    T = x_ref.shape[0]
    NB = T // CB
    core = lax.rem(dp, 2)
    bx = lax.rem(dp // 2, 2)
    by = lax.rem(dp // 4, 2)
    d_core = 1 - 2 * core
    d_x = 2 * (1 - 2 * bx)
    d_y = 4 * (1 - 2 * by)
    slot = core * 4 + by * 2 + bx

    W = (WA, WB, WC)
    OWN = (a_own, b_own, c_own)
    R0 = (R0A, R0B, R0C)
    RA = (RAA, RAB, RAC)
    RB = (RBA, RBB, RBC)
    ZR = (ZRA, ZRB, ZRC)
    O = (OA, OB, OC)
    RH = (RHA, RHB, RHC)

    near = z + 1 - 2 * lax.rem(z, 2)
    mid = 2 - z // 2
    far = 3 * (1 - z // 2)
    is_outer = jnp.logical_or(z == 0, z == NT - 1)
    is_inner = jnp.logical_and(z > 0, z < NT - 1)

    def choose(j, groups):
        out = groups[-1]
        for i in range(NT - 2, -1, -1):
            out = jnp.where(j == i, groups[i], out)
        return out

    def wo(j):
        return choose(j, (z, near, mid, far))

    def ff(j):
        return choose(j, (z, far, mid, near))

    def last(t):
        return choose(t, (far, mid, near, z))

    def high(i):
        step = 8 * 2**i
        return dp + step * (1 - 2 * lax.rem(dp // step, 2))

    def rcopy(src, dst, ssem, rsem, dev):
        return pltpu.make_async_remote_copy(
            src_ref=src, dst_ref=dst, send_sem=ssem, recv_sem=rsem, device_id=dev, device_id_type=MESH
        )

    dev_x = (dp + d_x, z)
    dev_y = (dp + d_y, z)
    dev_c = (dp + d_core, z)
    slot_x = core * 4 + by * 2 + (1 - bx)
    slot_y = core * 4 + (1 - by) * 2 + bx
    slot_d = core * 4 + (1 - by) * 2 + (1 - bx)

    peers = [(dp + d_core, z), (dp + d_x, z), (dp + d_y, z)]
    peers += [(high(i), z) for i in range(nh)]
    peers += [(dp, lax.rem(z + o, NT)) for o in range(1, NT)]
    barrier = pltpu.get_barrier_semaphore()
    for peer in peers:
        pl.semaphore_signal(barrier, inc=1, device_id=peer, device_id_type=MESH)
    pl.semaphore_wait(barrier, len(peers))

    def wrows(k, g, s):
        return W[k].at[g, pl.ds(mo(s * R_W, R_W), R_W), :]

    def wrows4(k, g, c):
        return W[k].at[g, pl.ds(mo(c * 4 * R_W, R_W), 4 * R_W), :]

    def whalf(k, g, s, h):
        return W[k].at[g, pl.ds(mo(s * R_W + h * HALF_W[0], 16), HALF_W[h]), :]

    def z_next(g):
        return jnp.where(g < z, z + 1, z - 1)

    def w_z(k):
        src = OWN[k].at[pl.ds(mo(slot * R_W, R_W), R_W), :]

        @pl.when(z < NT - 1)
        def _():
            rcopy(src, wrows(k, z, slot), wz_s.at[k, 0], w_r.at[0, k, z], (dp, z + 1)).start()

        @pl.when(z > 0)
        def _():
            rcopy(src, wrows(k, z, slot), wz_s.at[k, 1], w_r.at[0, k, z], (dp, z - 1)).start()

    def w_wait(k, g, stage, ref):
        rcopy(ref, ref, w_s.at[0, k, g], w_r.at[stage, k, g], dev_c).wait_recv()

    def w_send(k, g, s_stage, r_stage, ref, dev):
        rcopy(ref, ref, w_s.at[s_stage, k, g], w_r.at[r_stage, k, g], dev).start()

    def w_0(k, g):
        mine = wrows(k, g, slot)
        w_wait(k, g, 0, mine)

        @pl.when(is_inner)
        def _():
            w_send(k, g, 5, 0, mine, (dp, z_next(g)))

    def w_1(k, g):
        mine = wrows(k, g, slot)
        w_send(k, g, 0, 1, mine, dev_x)
        w_send(k, g, 1, 2, mine, dev_y)

    def w_2(k, g):
        w_wait(k, g, 1, wrows(k, g, slot_x))
        w_send(k, g, 2, 3, whalf(k, g, slot_x, 0), dev_y)
        w_wait(k, g, 2, wrows(k, g, slot_y))
        w_send(k, g, 3, 4, whalf(k, g, slot_y, 1), dev_x)

    def w_3(k, g):
        w_wait(k, g, 3, whalf(k, g, slot_d, 0))
        w_wait(k, g, 4, whalf(k, g, slot_d, 1))
        w_send(k, g, 4, 5, wrows4(k, g, core), dev_c)

    def w_4(k, g):
        w_wait(k, g, 5, wrows4(k, g, 1 - core))
        sent = [wrows(k, g, slot)] * 2 + [whalf(k, g, slot_x, 0), whalf(k, g, slot_y, 1), wrows4(k, g, core)]
        for st, ref in enumerate(sent):
            rcopy(ref, ref, w_s.at[st, k, g], w_r.at[0, k, g], dev_c).wait_send()

        @pl.when(is_inner)
        def _():
            mine = wrows(k, g, slot)
            rcopy(mine, mine, w_s.at[5, k, g], w_r.at[0, k, g], dev_c).wait_send()

    def w_z_done(k):
        src = OWN[k].at[pl.ds(mo(slot * R_W, R_W), R_W), :]

        @pl.when(z < NT - 1)
        def _():
            rcopy(src, wrows(k, z, slot), wz_s.at[k, 0], w_r.at[0, k, z], (dp, z + 1)).wait_send()

        @pl.when(z > 0)
        def _():
            rcopy(src, wrows(k, z, slot), wz_s.at[k, 1], w_r.at[0, k, z], (dp, z - 1)).wait_send()

    small = ((ft_own, FT), (bp_own, BP))

    def small_send():
        for i, (own, buf) in enumerate(small):
            for o in range(1, NT):
                rcopy(own, buf.at[z], sm_s.at[i, o - 1], sm_r.at[i, z], (dp, lax.rem(z + o, NT))).start()

    def small_wait(g):
        for i, (own, buf) in enumerate(small):
            rcopy(own, buf.at[g], sm_s.at[i, 0], sm_r.at[i, g], (dp, z)).wait_recv()

    def small_done():
        for i, (own, buf) in enumerate(small):
            for o in range(1, NT):
                rcopy(own, buf.at[z], sm_s.at[i, o - 1], sm_r.at[i, z], (dp, lax.rem(z + o, NT))).wait_send()

    local = [
        pltpu.make_async_copy(ft_own, FT.at[z], own_s.at[0]),
        pltpu.make_async_copy(bp_own, BP.at[z], own_s.at[1]),
        pltpu.make_async_copy(a_own, WA.at[z, pl.ds(0, D), :], own_s.at[2]),
        pltpu.make_async_copy(b_own, WB.at[z], own_s.at[3]),
        pltpu.make_async_copy(c_own, WC.at[z], own_s.at[4]),
    ]
    small_send()
    w_z(0)
    for copy in local:
        copy.start()

    def grows(k, g, s, n=1):
        return W[k].at[g, pl.ds(mo(s * R_G[k], 16), n * R_G[k]), :]

    def add_rows(dst, start, src, n):
        blk = 16 if n % 32 else 32

        def body(i, _):
            at = pl.ds(mo(start + i * blk, 16), blk)
            dst[at, :] = (dst[at, :].astype(F32) + src[pl.ds(mo(i * blk, 16), blk), :].astype(F32)).astype(BF)
            return 0

        lax.fori_loop(0, n // blk, body, 0)

    def ghalf(k, g, s, h):
        return W[k].at[g, pl.ds(mo(s * R_G[k] + h * HALF_G[k][0], 16), HALF_G[k][h]), :]

    def ra(k, g, h):
        return RA[k].at[g, pl.ds(h * HALF_G[k][0], HALF_G[k][h]), :]

    def g_wait(k, g, stage, ref):
        rcopy(ref, ref, g_s.at[0, k, g], g_r.at[stage, k, g], dev_c).wait_recv()

    def g_send(k, g, stage, src, dst, dev):
        rcopy(src, dst, g_s.at[stage, k, g], g_r.at[stage, k, g], dev).start()

    def g_core(k, g):
        g_send(k, g, 0, grows(k, g, (1 - core) * 4, 4), R0[k].at[g], dev_c)

    def g_a(k, g):
        g_wait(k, g, 0, R0[k].at[g])
        add_rows(W[k].at[g], core * 4 * R_G[k], R0[k].at[g], 4 * R_G[k])
        g_send(k, g, 1, ghalf(k, g, slot_d, 0), ra(k, g, 0), dev_x)
        g_send(k, g, 2, ghalf(k, g, slot_d, 1), ra(k, g, 1), dev_y)

    def g_b(k, g):
        g_wait(k, g, 1, ra(k, g, 0))
        add_rows(W[k].at[g], slot_y * R_G[k], ra(k, g, 0), HALF_G[k][0])
        g_send(k, g, 4, grows(k, g, slot_y), RB[k].at[g, 1], dev_y)
        g_wait(k, g, 2, ra(k, g, 1))
        add_rows(W[k].at[g], slot_x * R_G[k] + HALF_G[k][0], ra(k, g, 1), HALF_G[k][1])
        g_send(k, g, 3, grows(k, g, slot_x), RB[k].at[g, 0], dev_x)

    def g_y(k, g):
        for i in range(2):
            g_wait(k, g, 3 + i, RB[k].at[g, i])
            add_rows(W[k].at[g], slot * R_G[k], RB[k].at[g, i], R_G[k])

    def z_send(k, g):
        @pl.when(z < g)
        def _():
            rcopy(grows(k, g, slot), ZR[k].at[g], g_s.at[5, k, g], z_r.at[k, g], (dp, z + 1)).start()

        @pl.when(z > g)
        def _():
            at = jnp.where(z - 1 == g, NT, g)
            rcopy(grows(k, g, slot), ZR[k].at[at], g_s.at[5, k, g], z_r.at[k, at], (dp, z - 1)).start()

    def z_add(k, g, at):
        ref = ZR[k].at[at]
        rcopy(ref, ref, g_s.at[0, k, 0], z_r.at[k, at], dev_c).wait_recv()
        add_rows(W[k].at[g], slot * R_G[k], ref, R_G[k])

    def z_out(k, g):
        @pl.when(is_outer)
        def _():
            z_send(k, g)

    def z_in(k, g):
        @pl.when(is_inner)
        def _():
            z_add(k, g, g)
            z_send(k, g)

    def g_done(k, g):
        one = grows(k, g, 0)
        sent = [grows(k, g, 0, 4), ghalf(k, g, 0, 0), ghalf(k, g, 0, 1), one, one]
        for st, ref in enumerate(sent):
            rcopy(ref, ref, g_s.at[st, k, g], g_r.at[0, k, g], dev_c).wait_send()

        @pl.when(g != z)
        def _():
            rcopy(one, one, g_s.at[5, k, g], g_r.at[0, k, g], dev_c).wait_send()

    def orows(k, s, n=1):
        return O[k].at[pl.ds(mo(s * R_G[k], 16), n * R_G[k]), :]

    def ohalf(k, s, h):
        return O[k].at[pl.ds(mo(s * R_G[k] + h * HALF_G[k][0], 16), HALF_G[k][h]), :]

    def o_wait(k, stage, ref):
        rcopy(ref, ref, o_s.at[stage, k], o_r.at[stage, k], dev_c).wait_recv()

    def o_send(k, stage, ref, dev):
        rcopy(ref, ref, o_s.at[stage, k], o_r.at[stage, k], dev).start()

    def g_sum(k):
        @pl.when(z > 0)
        def _():
            z_add(k, z, z)

        @pl.when(z < NT - 1)
        def _():
            z_add(k, z, NT)

        O[k][pl.ds(mo(slot * R_G[k], 16), R_G[k]), :] = W[k][z, pl.ds(mo(slot * R_G[k], 16), R_G[k]), :]
        for i in range(nh):
            rcopy(orows(k, slot), RH[k].at[i], h_s.at[i, k], h_r.at[i, k], (high(i), z)).start()
            rcopy(orows(k, slot), RH[k].at[i], h_s.at[i, k], h_r.at[i, k], (high(i), z)).wait()
            add_rows(O[k], slot * R_G[k], RH[k].at[i], R_G[k])
        o_send(k, 0, orows(k, slot), dev_x)
        o_send(k, 1, orows(k, slot), dev_y)

    def o_2(k):
        o_wait(k, 0, orows(k, slot_x))
        o_send(k, 2, ohalf(k, slot_x, 0), dev_y)
        o_wait(k, 1, orows(k, slot_y))
        o_send(k, 3, ohalf(k, slot_y, 1), dev_x)

    def o_3(k):
        o_wait(k, 2, ohalf(k, slot_d, 0))
        o_wait(k, 3, ohalf(k, slot_d, 1))
        o_send(k, 4, orows(k, core * 4, 4), dev_c)

    def o_4(k, out, sem):
        o_wait(k, 4, orows(k, (1 - core) * 4, 4))
        copy = pltpu.make_async_copy(O[k], out, sem)
        copy.start()
        sent = [orows(k, slot)] * 2 + [ohalf(k, slot_x, 0), ohalf(k, slot_y, 1), orows(k, core * 4, 4)]
        for st, ref in enumerate(sent):
            rcopy(ref, ref, o_s.at[st, k], o_r.at[0, k], dev_c).wait_send()
        return copy

    def iota(shape, axis):
        return lax.broadcasted_iota(jnp.int32, shape, axis)

    causal = iota((CB, CB), 0) <= iota((CB, CB), 1)
    aug_tail = jnp.where(iota((16, T), 0) < 2, 1.0, 0.0).astype(BF)
    ones_rows = jnp.ones((16, T), BF)
    head_mask = (iota((HC, HC), 0) // HD) == (iota((HC, HC), 1) // HD)

    def pick(which):
        r = iota((2 * HD, HC), 0) - which * HD
        return (r == lax.rem(iota((2 * HD, HC), 1), HD)).astype(BF)

    def pick_back(which):
        r = iota((HC, 2 * HD), 1) - which * HD
        return (r == lax.rem(iota((HC, 2 * HD), 0), HD)).astype(BF)

    def block_diag(g, which):
        return jnp.where(head_mask, dot(FT[g], pick(which)), 0.0).astype(BF)

    first_end = seq_ref[0, 0]
    second_end = seq_ref[0, 0] + seq_ref[0, 1]

    def seq_id(zz):
        start = zz * T
        return (start >= first_end).astype(jnp.int32) + (start >= second_end).astype(jnp.int32)

    from_prev = jnp.logical_and(z > 0, seq_id(z) == seq_id(z - 1))
    from_next = jnp.logical_and(z < NT - 1, seq_id(z) == seq_id(z + 1))

    RB_ = 64

    def p0(i, _):
        at = pl.ds(mo(i * RB_, RB_), RB_)
        xh, _inv = norm_stats(x_ref[at, :].astype(F32))
        N1[at, :] = (xh * ln1g_ref[...] + ln1b_ref[...]).astype(BF)
        return 0

    lax.fori_loop(0, T // RB_, p0, 0)
    for g in range(NT):
        WA[g, pl.ds(D, ROWS_G[0] - D), :] = jnp.zeros((ROWS_G[0] - D, D), BF)
    GQ[pl.ds(QKV, D - QKV), :] = jnp.zeros((D - QKV, T), BF)

    @pl.when(z == 0)
    def _():
        CR[...] = jnp.zeros_like(CR)

    @pl.when(z == NT - 1)
    def _():
        GR[...] = jnp.zeros_like(GR)

    for copy in local[:3]:
        copy.wait()

    def chain_wait(buf, g, stage):
        rcopy(buf.at[g], buf.at[g], c_s.at[stage, g], c_r.at[stage, g], (dp, z)).wait_recv()

    def chain_send(g):
        rcopy(SQ.at[g], CR.at[g], c_s.at[0, g], c_r.at[0, g], (dp, z + 1)).start()

    def p1(j, _):
        g = wo(j)

        @pl.when(j == 1)
        def _():
            small_wait(near)
            w_0(0, near)
            w_1(0, near)
            w_z(1)
            w_0(0, mid)
            w_1(0, mid)
            w_z(2)
            w_2(0, near)
            w_3(0, near)
            w_0(0, far)
            w_1(0, far)
            w_2(0, mid)
            w_4(0, near)
            w_0(1, near)

        @pl.when(j == 2)
        def _():
            small_wait(mid)
            w_3(0, mid)
            w_0(2, near)
            w_2(0, far)
            w_4(0, mid)

        @pl.when(j == 3)
        def _():
            small_wait(far)
            w_0(1, mid)
            w_3(0, far)
            w_1(1, near)
            w_1(2, near)
            w_0(2, mid)
            w_4(0, far)

        bias = jnp.transpose(BP[g])[:QKV, 0:1]
        qkv = (dot(WA[g, pl.ds(0, QKV), :], N1[...], 1, 1) + bias).astype(BF)
        QK[g] = qkv[: 2 * HC]
        ql = dot(block_diag(g, 0), qkv[:HC])
        kl = dot(block_diag(g, 1), qkv[HC : 2 * HC])
        for h in range(HPG):
            hh = g * HPG + h
            rows = slice(h * HD, (h + 1) * HD)
            qf = soft_pair(ql[rows]).astype(BF)
            kf = soft_pair(kl[rows]).astype(BF)
            va = jnp.concatenate([qkv[2 * HC + h * HD : 2 * HC + (h + 1) * HD], aug_tail], axis=0)
            QF[hh] = qf
            KF[hh] = kf
            VA[hh] = va
            kn = kf.T
            ST[hh] = dot(va, kn)
            for qi in range(NB):
                qs = slice(qi * CB, (qi + 1) * CB)
                acc = None
                for ki in range(qi + 1):
                    ks = slice(ki * CB, (ki + 1) * CB)
                    s = dot(kn[ks], qf[:, qs])
                    if ki == qi:
                        s = jnp.where(causal, s, 0.0)
                    part = dot(va[:, ks], s.astype(BF))
                    acc = part if acc is None else acc + part
                NM[hh, :, qs] = acc[: HD + 8]

        @pl.when(z == 0)
        def _():
            for h in range(HPG):
                SQ[g, h] = ST[g * HPG + h].astype(BF)
            chain_send(g)

        for zz, jj, ready in ((1, 1, (0, 1)), (1, 2, (2,)), (1, 3, (3,)), (2, 2, (1,)), (2, 3, (0, 2, 3))):

            @pl.when(jnp.logical_and(z == zz, j == jj))
            def _():
                for gg in ready:
                    chain_wait(CR, gg, 0)
                    for h in range(HPG):
                        hh = gg * HPG + h
                        carried = jnp.where(from_prev, CR[gg, h].astype(F32), 0.0)
                        SQ[gg, h] = (ST[hh] + carried).astype(BF)
                    chain_send(gg)

        return 0

    lax.fori_loop(0, NT, p1, 0)
    for k in (1, 2):
        w_0(k, far)
        w_1(k, far)
    w_2(1, near)
    w_2(2, near)

    def p1b(g, _):
        @pl.when(z == NT - 1)
        def _():
            chain_wait(CR, g, 0)

        for h in range(HPG):
            CT[g * HPG + h] = jnp.where(from_prev, CR[g, h], jnp.zeros((AUG, 2 * HD), BF))
        return 0

    lax.fori_loop(0, NT, p1b, 0)

    def p1c(g, _):
        for h in range(HPG):
            hh = g * HPG + h
            num = NM[hh] + dot(CT[hh], QF[hh])[: HD + 8]
            inv = 1.0 / num[HD : HD + 1]
            DI[hh] = inv
            MX[g, pl.ds(h * HD, HD), :] = (num[:HD] * inv).astype(BF)
        return 0

    lax.fori_loop(0, NT, p1c, 0)
    for k in (1, 2):
        w_1(k, mid)
    for k in (1, 2):
        w_3(k, near)
        w_2(k, far)

    def p2(n, _):
        acc = None
        for g in range(NT):
            part = dot(MX[g], WA[g, pl.ds(QKV, HC), col(n)], 0, 0)
            acc = part if acc is None else acc + part
        MID[:, col(n)] = x_ref[:, col(n)].astype(F32) + (acc + bout_ref[:, col(n)])
        return 0

    lax.fori_loop(0, D // CB, p2, 0)

    def p2b(i, _):
        at = pl.ds(mo(i * 128, 128), 128)
        xh, _inv = norm_stats(MID[at, :])
        n2 = (xh * ln2g_ref[...] + ln2b_ref[...]).astype(BF)
        N2[at, :] = n2
        N2T[:, at] = n2.T
        return 0

    lax.fori_loop(0, T // 128, p2b, 0)
    w_3(1, far)
    w_3(2, far)

    @pl.when(z < NT - 1)
    def _():
        for g in range(NT):
            rcopy(SQ.at[g], SQ.at[g], c_s.at[0, g], c_r.at[0, g], (dp, z)).wait_send()

    UN[...] = jnp.zeros_like(UN)
    GN2[...] = jnp.zeros_like(GN2)
    for copy in local[3:]:
        copy.wait()

    cc = math.sqrt(2.0 / math.pi)

    def p3(j, _):
        g = ff(j)

        @pl.when(j > 0)
        def _():
            w_4(1, g)
            w_4(2, g)

        def units(u, total):
            pre = dot(N2[...], WB[g, :, col(u)]) + BP[g, pl.ds(1, 1), col(u)]
            sq = pre * pre
            t = jnp.tanh(cc * pre * (1.0 + 0.044715 * sq))
            act = (0.5 * pre * (1.0 + t)).astype(BF)
            slope = 0.5 * (1.0 + t) + (0.5 * cc) * pre * (1.0 - t * t) * (1.0 + (3 * 0.044715) * sq)
            ACT[:, col(u)] = act
            ACTT[col(u), :] = act.T
            gact = dot(cot_ref[...], WC[g, col(u), :], 1, 1)
            gpre = (gact * slope).astype(BF)
            GP[:, col(u)] = gpre
            GBF[g, :, col(u)] = jnp.sum(gpre.astype(F32), axis=0, keepdims=True)
            return total

        lax.fori_loop(0, U // CB, units, 0)

        @pl.when(j >= 1)
        def _():
            g_a(1, ff(j - 1))
            g_a(2, ff(j - 1))

        @pl.when(j == 1)
        def _():
            w_3(1, mid)
            w_3(2, mid)

        @pl.when(j == 2)
        def _():
            g_b(1, z)
            g_b(2, z)

        def outs(n, _):
            UN[:, col(n)] += dot(ACT[...], WC[g, :, col(n)])
            GN2[:, col(n)] += dot(GP[...], WB[g, col(n), :], 1, 1)
            return 0

        lax.fori_loop(0, D // CB, outs, 0)

        @pl.when(j == 0)
        def _():
            w_2(1, mid)
            w_2(2, mid)

        def grads(n, _):
            WC[g, col(n), :] = dot(ACTT[col(n), :], cot_ref[...]).astype(BF)
            WB[g, col(n), :] = dot(N2T[col(n), :], GP[...]).astype(BF)
            return 0

        lax.fori_loop(0, D // CB, grads, 0)
        g_core(1, g)
        g_core(2, g)

        return 0

    lax.fori_loop(0, NT, p3, 0)
    g_b(1, far)
    g_b(2, far)

    VS[...] = jnp.zeros_like(VS)

    def p4(i, _):
        at = pl.ds(mo(i * RB_, RB_), RB_)
        mid = MID[at, :]
        res_ref[at, :] = (mid + UN[at, :] + bproj_ref[...]).astype(BF)
        xh, inv = norm_stats(mid)
        gn = GN2[at, :]
        gh = gn * ln2g_ref[...]
        c1 = jnp.mean(gh, axis=-1, keepdims=True)
        c2 = jnp.mean(gh * xh, axis=-1, keepdims=True)
        cot = cot_ref[at, :].astype(F32)
        gm = cot + inv * (gh - c1 - xh * c2)
        GN2[at, :] = gm
        low = gm.astype(BF)
        GML[at, :] = low
        VS[0] += jnp.sum(cot, axis=0, keepdims=True)
        VS[1] += jnp.sum(low.astype(F32), axis=0, keepdims=True)
        VS[2] += jnp.sum(gn * xh, axis=0, keepdims=True)
        VS[3] += jnp.sum(gn, axis=0, keepdims=True)
        return 0

    lax.fori_loop(0, T // RB_, p4, 0)
    g_a(1, near)
    g_a(2, near)

    tail_row = iota((16, T), 0)

    def p5a(g, _):
        gmix = dot(WA[g, pl.ds(QKV, HC), :], GML[...], 1, 1).astype(BF).astype(F32)
        mix = MX[g]
        WA[g, pl.ds(QKV, HC), :] = dot(mix, GML[...]).astype(BF)
        prod = gmix * mix.astype(F32)
        for h in range(HPG):
            hh = g * HPG + h
            rows = slice(h * HD, (h + 1) * HD)
            inv = DI[hh]
            gden = -jnp.sum(prod[rows], axis=0, keepdims=True) * inv
            hi = gden.astype(BF).astype(F32)
            lo = gden - hi
            tail = jnp.where(tail_row == 0, hi, jnp.where(tail_row == 1, lo, 0.0)).astype(BF)
            ga = jnp.concatenate([(gmix[rows] * inv).astype(BF), tail], axis=0)
            GA[hh] = ga
            gc = dot(ga, QF[hh].T)
            GC[hh] = gc
            SQ[g, h] = gc.astype(BF)

        @pl.when(z == NT - 1)
        def _():
            rcopy(SQ.at[g], GR.at[g], c_s.at[1, g], c_r.at[1, g], (dp, z - 1)).start()

        return 0

    lax.fori_loop(0, NT, p5a, 0)

    def chain_back(g, _):
        @pl.when(z < NT - 1)
        def _():
            chain_wait(GR, g, 1)
            for h in range(HPG):
                hh = g * HPG + h
                later = jnp.where(from_next, GR[g, h].astype(F32), 0.0)
                SQ[g, h] = (GC[hh] + later).astype(BF)

        @pl.when(jnp.logical_and(z > 0, z < NT - 1))
        def _():
            rcopy(SQ.at[g], GR.at[g], c_s.at[1, g], c_r.at[1, g], (dp, z - 1)).start()

        return 0

    GN1 = UN
    GN1[...] = jnp.zeros_like(GN1)

    def back(feat, grads):
        out = []
        for b in range(NB):
            bs = slice(b * CB, (b + 1) * CB)
            p = feat[:HD, bs].astype(F32)
            m = feat[HD:, bs].astype(F32)
            g1 = grads[b][:HD]
            g2 = grads[b][HD:]
            s1 = jnp.sum(g1 * p, axis=0, keepdims=True)
            s2 = jnp.sum(g2 * m, axis=0, keepdims=True)
            out.append((p * (g1 - s1) - m * (g2 - s2)).astype(BF))
        return jnp.concatenate(out, axis=1)

    def p5b(t, _):
        g = last(t)
        gql = []
        gkl = []
        for h in range(HPG):
            hh = g * HPG + h
            qf = QF[hh]
            kf = KF[hh]
            va = VA[hh]
            ga = GA[hh]
            kn = kf.T
            vn = va.T
            ctt = CT[hh].T
            gq = [None] * NB
            gk = [None] * NB
            gv = [None] * NB
            for qi in range(NB):
                qs = slice(qi * CB, (qi + 1) * CB)
                gq[qi] = dot(ctt, ga[:, qs])
                for ki in range(qi + 1):
                    ks = slice(ki * CB, (ki + 1) * CB)
                    s = dot(kn[ks], qf[:, qs])
                    gs = dot(vn[ks], ga[:, qs])
                    if ki == qi:
                        s = jnp.where(causal, s, 0.0)
                        gs = jnp.where(causal, gs, 0.0)
                    s = s.astype(BF)
                    gs = gs.astype(BF)
                    gq[qi] = gq[qi] + dot(kf[:, ks], gs)
                    pk = dot(qf[:, qs], gs, 1, 1)
                    pv = dot(ga[:, qs], s, 1, 1)[:HD]
                    gk[ki] = pk if gk[ki] is None else gk[ki] + pk
                    gv[ki] = pv if gv[ki] is None else gv[ki] + pv
            for ki in range(NB):
                ks = slice(ki * CB, (ki + 1) * CB)
                NM[3 * h, :HD, ks] = gk[ki][:HD]
                NM[3 * h + 1, :HD, ks] = gk[ki][HD:]
                NM[3 * h + 2, :HD, ks] = gv[ki]
            gql.append(back(qf, gq))

        @pl.when(t == 0)
        def _():
            lax.fori_loop(0, NT, chain_back, 0)
            for k in (1, 2):
                g_b(k, mid)
                g_y(k, z)
                g_y(k, far)

        @pl.when(t >= 1)
        def _():
            g_a(0, last(t - 1))

        @pl.when(t == 1)
        def _():
            g_b(1, near)
            g_b(2, near)

        @pl.when(t >= 2)
        def _():
            g_b(0, last(t - 2))

        for k in (1, 2):

            @pl.when(t == 2)
            def _():
                z_in(k, far)

            @pl.when(t == 3)
            def _():
                z_in(k, mid)

        @pl.when(t == 3)
        def _():
            g_y(0, far)
            z_out(0, far)

        for h in range(HPG):
            hh = g * HPG + h
            kf = KF[hh]
            va = VA[hh]
            gkc = jnp.where(from_next, GR[g, h], jnp.zeros((AUG, 2 * HD), BF))
            gkt = gkc.T
            gk = [None] * NB
            for ki in range(NB):
                ks = slice(ki * CB, (ki + 1) * CB)
                gk[ki] = jnp.concatenate([NM[3 * h, :HD, ks], NM[3 * h + 1, :HD, ks]], axis=0) + dot(gkt, va[:, ks])
                gv = NM[3 * h + 2, :HD, ks] + dot(gkc[:HD], kf[:, ks])
                GQ[pl.ds(2 * HC + h * HD, HD), ks] = gv.astype(BF)
            gkl.append(back(kf, gk))

        comp = None
        for which, parts in ((0, gql), (1, gkl)):
            glog = jnp.concatenate(parts, axis=0)
            own = QK[g, pl.ds(which * HC, HC), :]
            GQ[pl.ds(which * HC, HC), :] = dot(block_diag(g, which), glog, 0, 0).astype(BF)
            gfeat = jnp.where(head_mask, dot(own, glog, 1, 1), 0.0).astype(BF)
            part = dot(gfeat, pick_back(which))
            comp = part if comp is None else comp + part
        comp = comp.astype(BF)
        gq_all = GQ[...]
        gqn = gq_all[:QKV].T
        for n in range(D // CB):
            GN1[:, n * CB : (n + 1) * CB] += dot(gqn, WA[g, pl.ds(0, QKV), n * CB : (n + 1) * CB])
        WA[g, pl.ds(0, QKV), :] = dot(gq_all[:QKV], N1[...]).astype(BF)
        for b in range(HC // 32):
            WA[g, pl.ds(D, 32), b * 128 : (b + 1) * 128] = comp[b * 32 : (b + 1) * 32]
        vec = dot(ones_rows, gq_all, 1, 1)
        row = iota((16, D), 0)
        vec = jnp.where(row == 1, GBF[g], vec)
        for i in range(4):
            vec = jnp.where(row == 2 + i, VS[i], vec)
        WA[g, pl.ds(D + 32, 16), :] = vec.astype(BF)
        g_core(0, g)

        for k in (1, 2):

            @pl.when(t == 0)
            def _():
                z_out(k, far)

            @pl.when(t == 1)
            def _():
                g_y(k, mid)
                z_out(k, mid)

            @pl.when(t == 2)
            def _():
                g_y(k, near)
                z_out(k, near)

            @pl.when(t == 3)
            def _():
                z_in(k, near)

        return 0

    lax.fori_loop(0, NT, p5b, 0)

    LS[...] = jnp.zeros_like(LS)

    def p6(i, _):
        at = pl.ds(mo(i * RB_, RB_), RB_)
        xh, inv = norm_stats(x_ref[at, :].astype(F32))
        gn = GN1[at, :]
        gh = gn * ln1g_ref[...]
        c1 = jnp.mean(gh, axis=-1, keepdims=True)
        c2 = jnp.mean(gh * xh, axis=-1, keepdims=True)
        gin_ref[at, :] = (GN2[at, :] + inv * (gh - c1 - xh * c2)).astype(BF)
        LS[0, 0:1, :] += jnp.sum(gn * xh, axis=0, keepdims=True)
        LS[0, 1:2, :] += jnp.sum(gn, axis=0, keepdims=True)
        return 0

    lax.fori_loop(0, T // RB_, p6, 0)

    partners = [dp + d_core, dp + d_x, dp + d_y] + [high(i) for i in range(nh)]

    steps = len(partners)

    def small_start(i):
        rcopy(LS.at[i], LR.at[i], l_s.at[i], l_r.at[i], (partners[i], z)).start()

    def small_end(i):
        rcopy(LS.at[i], LR.at[i], l_s.at[i], l_r.at[i], (partners[i], z)).wait()
        LS[i + 1] = LS[i] + LR[i]

    small_start(0)
    g_a(0, z)
    g_b(0, near)
    g_y(0, mid)
    z_out(0, mid)
    z_in(0, far)
    small_end(0)
    small_start(1)
    g_b(0, z)
    z_in(0, mid)
    g_y(0, near)
    z_out(0, near)
    z_in(0, near)
    small_end(1)
    small_start(2)
    g_sum(1)
    g_sum(2)
    small_end(2)
    for i in range(3, steps):
        small_start(i)
        small_end(i)
    LZ[z] = LS[steps]
    for o in range(1, NT):
        rcopy(LS.at[steps], LZ.at[z], lz_s.at[o - 1], lz_r.at[z], (dp, lax.rem(z + o, NT))).start()
    o_2(1)
    o_2(2)
    g_y(0, z)
    g_sum(0)
    o_3(1)
    o_3(2)
    o_2(0)
    outs = [o_4(1, ob_ref, own_s.at[0]), o_4(2, oc_ref, own_s.at[1])]
    for o in range(1, NT):
        zz = lax.rem(z + o, NT)
        rcopy(LZ.at[zz], LZ.at[zz], lz_s.at[o - 1], lz_r.at[zz], (dp, z)).wait_recv()
    total = LZ[0]
    for zz in range(1, NT):
        total = total + LZ[zz]
    ov_ref[...] = total
    o_3(0)
    outs.append(o_4(0, oa_ref, own_s.at[2]))
    for copy in outs:
        copy.wait()

    for o in range(1, NT):
        rcopy(LS.at[steps], LZ.at[z], lz_s.at[o - 1], lz_r.at[z], (dp, lax.rem(z + o, NT))).wait_send()
    small_done()
    for k in range(KINDS):
        w_z_done(k)
        for g in range(NT):
            g_done(k, g)

    @pl.when(z > 0)
    def _():
        for g in range(NT):
            rcopy(SQ.at[g], SQ.at[g], c_s.at[1, g], c_r.at[1, g], (dp, z)).wait_send()


def layer_call(nh, T, *args):
    def vm(shape, dtype=BF):
        return pltpu.VMEM(shape, dtype)

    dma = pltpu.SemaphoreType.DMA
    nhb = max(nh, 1)
    nst = 3 + nh
    scratch = [
        vm((NT, ROWS_G[0], D)),
        vm((NT, D, U)),
        vm((NT, U, D)),
        vm((NT, HC, 2 * HD)),
        vm((NT, 8, D), F32),
    ]
    scratch += [vm((NT, 4 * r, D)) for r in R_G]
    scratch += [vm((NT, r, D)) for r in R_G]
    scratch += [vm((NT, 2, r, D)) for r in R_G]
    scratch += [vm((NT + 1, r, D)) for r in R_G]
    scratch += [vm((rows, D)) for rows in ROWS_G]
    scratch += [vm((nhb, r if nh else 16, D)) for r in R_G]
    scratch += [vm((nst + 1, 8, D), F32), vm((nst, 8, D), F32), vm((NT, 8, D), F32)]
    scratch += [
        vm((T, D)),
        vm((NT, 2 * HC, T)),
        vm((NH, AUG, T)),
        vm((NH, 2 * HD, T)),
        vm((NH, 2 * HD, T)),
        vm((NH, HD + 8, T), F32),
        vm((NH, AUG, 2 * HD), F32),
        vm((NH, AUG, 2 * HD)),
        vm((NT, HPG, AUG, 2 * HD)),
        vm((NT, HPG, AUG, 2 * HD)),
        vm((NT, HPG, AUG, 2 * HD)),
        vm((NT, HC, T)),
        vm((NH, 1, T), F32),
        vm((T, D), F32),
        vm((T, D)),
        vm((D, T)),
        vm((T, D), F32),
        vm((T, D), F32),
        vm((T, D)),
        vm((T, U)),
        vm((U, T)),
        vm((T, U)),
        vm((NT, 1, U), F32),
        vm((NH, AUG, T)),
        vm((NH, AUG, 2 * HD), F32),
        vm((D, T)),
        vm((4, 1, D), F32),
    ]
    scratch += [
        dma((5,)),
        dma((2, NT - 1)),
        dma((2, NT)),
        dma((KINDS, 2)),
        dma((6, KINDS, NT)),
        dma((6, KINDS, NT)),
        dma((6, KINDS, NT)),
        dma((5, KINDS, NT)),
        dma((KINDS, NT + 1)),
        dma((5, KINDS)),
        dma((5, KINDS)),
        dma((nhb, KINDS)),
        dma((nhb, KINDS)),
        dma((nst,)),
        dma((nst,)),
        dma((NT - 1,)),
        dma((NT,)),
        dma((2, NT)),
        dma((2, NT)),
    ]
    vmem = pl.BlockSpec(memory_space=pltpu.VMEM)
    hbm = pl.BlockSpec(memory_space=pl.ANY)
    return pl.pallas_call(
        functools.partial(layer_kernel, nh),
        out_shape=(
            jax.ShapeDtypeStruct((T, D), BF),
            jax.ShapeDtypeStruct((T, D), BF),
            jax.ShapeDtypeStruct((ROWS_G[0], D), BF),
            jax.ShapeDtypeStruct((D, U), BF),
            jax.ShapeDtypeStruct((U, D), BF),
            jax.ShapeDtypeStruct((8, D), F32),
        ),
        in_specs=[pl.BlockSpec(memory_space=pltpu.SMEM)] + [vmem] * 8 + [hbm] * 5,
        out_specs=(vmem, vmem, hbm, hbm, hbm, vmem),
        scratch_shapes=scratch,
        compiler_params=pltpu.CompilerParams(
            collective_id=0, has_side_effects=True, vmem_limit_bytes=67043328
        ),
    )(*args)


def local(
    nh,
    tokens_in,
    ln1_gain,
    ln1_bias,
    w_qkv,
    b_qkv,
    feat_q,
    feat_k,
    w_out,
    b_out,
    ln2_gain,
    ln2_bias,
    w_fc,
    b_fc,
    w_proj,
    b_proj,
    seq_lengths,
    cotangent,
):
    T = tokens_in.shape[0]
    a_own = jnp.concatenate([jnp.transpose(w_qkv, (1, 2, 0)).reshape(QKV, D), w_out], axis=0)
    ft_own = jnp.concatenate(
        [jnp.transpose(feat_q, (0, 2, 1)).reshape(HC, HD), jnp.transpose(feat_k, (0, 2, 1)).reshape(HC, HD)],
        axis=1,
    )
    bq = jnp.pad(b_qkv.reshape(1, QKV), ((0, 0), (0, D - QKV)))
    bp_own = jnp.concatenate([bq, b_fc.reshape(1, U), jnp.zeros((6, D), F32)], axis=0)

    def row(v):
        return v.reshape(1, D)

    res, gin, oa, ob, oc, ov = layer_call(
        nh,
        T,
        seq_lengths,
        tokens_in,
        cotangent,
        row(ln1_gain),
        row(ln1_bias),
        row(b_out),
        row(ln2_gain),
        row(ln2_bias),
        row(b_proj),
        a_own,
        w_fc,
        w_proj,
        ft_own,
        bp_own,
    )
    g_w_qkv = jnp.transpose(oa[:QKV].reshape(3, HC, D), (2, 0, 1)).astype(F32)
    g_w_out = oa[QKV:D].astype(F32)
    feats = jnp.transpose(oa[D : D + 32].reshape(32, HC // 32, 2 * HD), (1, 0, 2)).reshape(HC, 2 * HD)
    feats = feats.astype(F32).reshape(HPG, HD, 2 * HD)
    vec = oa[D + 32 : D + 48].astype(F32)
    return (
        res,
        gin,
        ov[0],
        ov[1],
        g_w_qkv,
        vec[0, :QKV].reshape(3, HC),
        feats[:, :, :HD],
        feats[:, :, HD:],
        g_w_out,
        vec[3],
        vec[4],
        vec[5],
        ob.astype(F32),
        vec[1],
        oc.astype(F32),
        vec[2],
    )


def solution(mesh):
    n_dp = mesh.shape["dp"]
    nh = max(0, (n_dp // 8).bit_length() - 1)
    return jax.shard_map(
        functools.partial(local, nh),
        mesh=mesh,
        in_specs=(
            P(("dp", "tensor"), None),
            P(),
            P(),
            P(None, None, "tensor"),
            P(None, "tensor"),
            P("tensor", None, None),
            P("tensor", None, None),
            P("tensor", None),
            P(),
            P(),
            P(),
            P(None, "tensor"),
            P("tensor"),
            P("tensor", None),
            P(),
            P("dp", None),
            P(("dp", "tensor"), None),
        ),
        out_specs=(
            P(("dp", "tensor"), None),
            P(("dp", "tensor"), None),
            P(),
            P(),
            P(None, None, "tensor"),
            P(None, "tensor"),
            P("tensor", None, None),
            P("tensor", None, None),
            P("tensor", None),
            P(),
            P(),
            P(),
            P(None, "tensor"),
            P("tensor"),
            P("tensor", None),
            P(),
        ),
        check_vma=False,
    )
```

```python
import functools
import math

import jax
import jax.numpy as jnp
from jax import lax
from jax.experimental import pallas as pl
from jax.experimental.pallas import tpu as pltpu
from jax.sharding import PartitionSpec as P

NORM_EPS = 1e-05
BF = jnp.bfloat16
F32 = jnp.float32
MESH = pl.DeviceIdType.MESH
NT = 4
D = 768
HD = 64
HPG = 3
HC = HPG * HD
NH = NT * HPG
U = 768
AUG = 80
QKV = 3 * HC
KINDS = 3
R_W = 96
R_G = (112, 96, 96)
ROWS_G = (896, 768, 768)
CB = 256
HALF_W = (48, 48)
HALF_G = ((64, 48), (48, 48), (48, 48))


def dot(a, b, ca=1, cb=0):
    return lax.dot_general(a, b, (((ca,), (cb,)), ((), ())), preferred_element_type=F32)


def mo(value, multiple):
    return pl.multiple_of(value, multiple)


def soft_pair(logits):
    top = jnp.max(logits, axis=0, keepdims=True)
    low = jnp.min(logits, axis=0, keepdims=True)
    e_pos = jnp.exp(logits - top)
    e_neg = jnp.exp(low - logits)
    p = e_pos * (1.0 / jnp.sum(e_pos, axis=0, keepdims=True))
    m = e_neg * (1.0 / jnp.sum(e_neg, axis=0, keepdims=True))
    return jnp.concatenate([p, m], axis=0)


def norm_stats(rows):
    mean = jnp.mean(rows, axis=-1, keepdims=True)
    centred = rows - mean
    var = jnp.mean(centred * centred, axis=-1, keepdims=True)
    inv = lax.rsqrt(var + NORM_EPS)
    return centred * inv, inv


def col(n):
    return pl.ds(mo(n * CB, CB), CB)


def layer_kernel(
    nh,
    seq_ref,
    x_ref,
    cot_ref,
    ln1g_in,
    ln1b_in,
    bout_in,
    ln2g_in,
    ln2b_in,
    bproj_in,
    bfc_in,
    bqkv_in,
    fq_in,
    fk_in,
    a_own,
    a_out,
    b_own,
    c_own,
    res_ref,
    gin_ref,
    oa_ref,
    oo_ref,
    ob_ref,
    oc_ref,
    gfq_ref,
    gfk_ref,
    gbqkv_ref,
    gbfc_ref,
    gbproj_ref,
    gbout_ref,
    gln2g_ref,
    gln2b_ref,
    gln1g_ref,
    gln1b_ref,
    WA,
    WB,
    WC,
    FT,
    BP,
    R0A,
    R0B,
    R0C,
    RAA,
    RAB,
    RAC,
    RBA,
    RBB,
    RBC,
    ZRA,
    ZRB,
    ZRC,
    OA,
    OB,
    OC,
    RHA,
    RHB,
    RHC,
    LS,
    LR,
    LZ,
    N1,
    QK,
    VA,
    QF,
    KF,
    NM,
    ST,
    CT,
    CR,
    SQ,
    GR,
    MX,
    DI,
    MID,
    N2,
    N2T,
    UN,
    GN2,
    GML,
    ACT,
    ACTT,
    GP,
    GBF,
    GA,
    GC,
    GQ,
    VS,
    PV,
    ft_own,
    bp_own,
    WO,
    own_s,
    sm_s,
    sm_r,
    wz_s,
    w_s,
    w_r,
    g_s,
    g_r,
    z_r,
    o_s,
    o_r,
    h_s,
    h_r,
    l_s,
    l_r,
    lz_s,
    lz_r,
    c_s,
    c_r,
):
    dp = lax.axis_index("dp")
    z = lax.axis_index("tensor")
    T = x_ref.shape[0]
    NB = T // CB
    core = lax.rem(dp, 2)
    bx = lax.rem(dp // 2, 2)
    by = lax.rem(dp // 4, 2)
    d_core = 1 - 2 * core
    d_x = 2 * (1 - 2 * bx)
    d_y = 4 * (1 - 2 * by)
    slot = core * 4 + by * 2 + bx

    W = (WA, WB, WC)
    OWN = (a_own, b_own, c_own)
    R0 = (R0A, R0B, R0C)
    RA = (RAA, RAB, RAC)
    RB = (RBA, RBB, RBC)
    ZR = (ZRA, ZRB, ZRC)
    O = (OA, OB, OC)
    RH = (RHA, RHB, RHC)

    near = z + 1 - 2 * lax.rem(z, 2)
    mid = 2 - z // 2
    far = 3 * (1 - z // 2)
    is_outer = jnp.logical_or(z == 0, z == NT - 1)
    is_inner = jnp.logical_and(z > 0, z < NT - 1)

    def choose(j, groups):
        out = groups[-1]
        for i in range(NT - 2, -1, -1):
            out = jnp.where(j == i, groups[i], out)
        return out

    def wo(j):
        return choose(j, (z, near, mid, far))

    def ff(j):
        return choose(j, (z, far, mid, near))

    def last(t):
        return choose(t, (far, mid, near, z))

    def high(i):
        step = 8 * 2**i
        return dp + step * (1 - 2 * lax.rem(dp // step, 2))

    def rcopy(src, dst, ssem, rsem, dev):
        return pltpu.make_async_remote_copy(
            src_ref=src, dst_ref=dst, send_sem=ssem, recv_sem=rsem, device_id=dev, device_id_type=MESH
        )

    dev_x = (dp + d_x, z)
    dev_y = (dp + d_y, z)
    dev_c = (dp + d_core, z)
    slot_x = core * 4 + by * 2 + (1 - bx)
    slot_y = core * 4 + (1 - by) * 2 + bx
    slot_d = core * 4 + (1 - by) * 2 + (1 - bx)

    for i, ref in enumerate((ln1g_in, ln1b_in, bout_in, ln2g_in, ln2b_in, bproj_in)):
        PV[i] = ref[...].reshape(1, D)
    ln1g_ref, ln1b_ref, bout_ref, ln2g_ref, ln2b_ref, bproj_ref = (PV.at[i] for i in range(6))
    bp_own[...] = jnp.zeros_like(bp_own)
    bp_own[0:3, 0:HC] = bqkv_in[...]
    bp_own[3:4, :] = bfc_in[...].reshape(1, D)
    for h in range(HPG):
        ft_own[h * HD : (h + 1) * HD, :] = jnp.concatenate([fq_in[h], fk_in[h]], axis=1)

    peers = [(dp + d_core, z), (dp + d_x, z), (dp + d_y, z)]
    peers += [(high(i), z) for i in range(nh)]
    peers += [(dp, lax.rem(z + o, NT)) for o in range(1, NT)]
    barrier = pltpu.get_barrier_semaphore()
    for peer in peers:
        pl.semaphore_signal(barrier, inc=1, device_id=peer, device_id_type=MESH)
    pl.semaphore_wait(barrier, len(peers))

    def wrows(k, g, s):
        return W[k].at[g, pl.ds(mo(s * R_W, R_W), R_W), :]

    def wrows4(k, g, c):
        return W[k].at[g, pl.ds(mo(c * 4 * R_W, R_W), 4 * R_W), :]

    def whalf(k, g, s, h):
        return W[k].at[g, pl.ds(mo(s * R_W + h * HALF_W[0], 16), HALF_W[h]), :]

    def z_next(g):
        return jnp.where(g < z, z + 1, z - 1)

    def own_rows(k):
        at = pl.ds(mo(slot * R_W, R_W), R_W)
        if k:
            return ((slot >= 0, OWN[k].at[at, :]),)
        split = QKV // R_W
        low = jnp.where(slot < split, slot, 0)
        high = jnp.where(slot < split, 0, slot - split)
        return (
            (slot < split, a_own.at[pl.ds(mo(low * R_W, R_W), R_W), :]),
            (slot >= split, a_out.at[pl.ds(mo(high * R_W, R_W), R_W), :]),
        )

    def w_z(k):
        for here, src in own_rows(k):

            @pl.when(jnp.logical_and(here, z < NT - 1))
            def _():
                rcopy(src, wrows(k, z, slot), wz_s.at[k, 0], w_r.at[0, k, z], (dp, z + 1)).start()

            @pl.when(jnp.logical_and(here, z > 0))
            def _():
                rcopy(src, wrows(k, z, slot), wz_s.at[k, 1], w_r.at[0, k, z], (dp, z - 1)).start()

    def w_wait(k, g, stage, ref):
        rcopy(ref, ref, w_s.at[0, k, g], w_r.at[stage, k, g], dev_c).wait_recv()

    def w_send(k, g, s_stage, r_stage, ref, dev):
        rcopy(ref, ref, w_s.at[s_stage, k, g], w_r.at[r_stage, k, g], dev).start()

    def w_0(k, g):
        mine = wrows(k, g, slot)
        w_wait(k, g, 0, mine)

        @pl.when(is_inner)
        def _():
            w_send(k, g, 5, 0, mine, (dp, z_next(g)))

    def w_1(k, g):
        mine = wrows(k, g, slot)
        w_send(k, g, 0, 1, mine, dev_x)
        w_send(k, g, 1, 2, mine, dev_y)

    def w_2(k, g):
        w_wait(k, g, 1, wrows(k, g, slot_x))
        w_send(k, g, 2, 3, whalf(k, g, slot_x, 0), dev_y)
        w_wait(k, g, 2, wrows(k, g, slot_y))
        w_send(k, g, 3, 4, whalf(k, g, slot_y, 1), dev_x)

    def w_3(k, g):
        w_wait(k, g, 3, whalf(k, g, slot_d, 0))
        w_wait(k, g, 4, whalf(k, g, slot_d, 1))
        w_send(k, g, 4, 5, wrows4(k, g, core), dev_c)

    def w_4(k, g):
        w_wait(k, g, 5, wrows4(k, g, 1 - core))
        sent = [wrows(k, g, slot)] * 2 + [whalf(k, g, slot_x, 0), whalf(k, g, slot_y, 1), wrows4(k, g, core)]
        for st, ref in enumerate(sent):
            rcopy(ref, ref, w_s.at[st, k, g], w_r.at[0, k, g], dev_c).wait_send()

        @pl.when(is_inner)
        def _():
            mine = wrows(k, g, slot)
            rcopy(mine, mine, w_s.at[5, k, g], w_r.at[0, k, g], dev_c).wait_send()

    def w_z_done(k):
        src = own_rows(k)[0][1]

        @pl.when(z < NT - 1)
        def _():
            rcopy(src, wrows(k, z, slot), wz_s.at[k, 0], w_r.at[0, k, z], (dp, z + 1)).wait_send()

        @pl.when(z > 0)
        def _():
            rcopy(src, wrows(k, z, slot), wz_s.at[k, 1], w_r.at[0, k, z], (dp, z - 1)).wait_send()

    small = ((ft_own, FT), (bp_own, BP))

    def small_send():
        for i, (own, buf) in enumerate(small):
            for o in range(1, NT):
                rcopy(own, buf.at[z], sm_s.at[i, o - 1], sm_r.at[i, z], (dp, lax.rem(z + o, NT))).start()

    def small_wait(g):
        for i, (own, buf) in enumerate(small):
            rcopy(own, buf.at[g], sm_s.at[i, 0], sm_r.at[i, g], (dp, z)).wait_recv()

    def small_done():
        for i, (own, buf) in enumerate(small):
            for o in range(1, NT):
                rcopy(own, buf.at[z], sm_s.at[i, o - 1], sm_r.at[i, z], (dp, lax.rem(z + o, NT))).wait_send()

    local = [
        pltpu.make_async_copy(ft_own, FT.at[z], own_s.at[0]),
        pltpu.make_async_copy(bp_own, BP.at[z], own_s.at[1]),
        pltpu.make_async_copy(a_own, WA.at[z, pl.ds(0, QKV), :], own_s.at[2]),
        pltpu.make_async_copy(a_out, WA.at[z, pl.ds(QKV, HC), :], own_s.at[5]),
        pltpu.make_async_copy(b_own, WB.at[z], own_s.at[3]),
        pltpu.make_async_copy(c_own, WC.at[z], own_s.at[4]),
    ]
    small_send()
    w_z(0)

    @pl.when(is_outer)
    def _():
        w_z(1)
        w_z(2)

    for copy in local:
        copy.start()

    def grows(k, g, s, n=1):
        return W[k].at[g, pl.ds(mo(s * R_G[k], 16), n * R_G[k]), :]

    def add_rows(dst, start, src, n):
        blk = 16 if n % 32 else 32

        def body(i, _):
            at = pl.ds(mo(start + i * blk, 16), blk)
            dst[at, :] = (dst[at, :].astype(F32) + src[pl.ds(mo(i * blk, 16), blk), :].astype(F32)).astype(BF)
            return 0

        lax.fori_loop(0, n // blk, body, 0)

    def ghalf(k, g, s, h):
        return W[k].at[g, pl.ds(mo(s * R_G[k] + h * HALF_G[k][0], 16), HALF_G[k][h]), :]

    def ra(k, g, h):
        return RA[k].at[g, pl.ds(h * HALF_G[k][0], HALF_G[k][h]), :]

    def g_wait(k, g, stage, ref):
        rcopy(ref, ref, g_s.at[0, k, g], g_r.at[stage, k, g], dev_c).wait_recv()

    def g_send(k, g, stage, src, dst, dev):
        rcopy(src, dst, g_s.at[stage, k, g], g_r.at[stage, k, g], dev).start()

    def g_core(k, g):
        g_send(k, g, 0, grows(k, g, (1 - core) * 4, 4), R0[k].at[g], dev_c)

    def g_a(k, g):
        g_wait(k, g, 0, R0[k].at[g])
        add_rows(W[k].at[g], core * 4 * R_G[k], R0[k].at[g], 4 * R_G[k])
        g_send(k, g, 1, ghalf(k, g, slot_d, 0), ra(k, g, 0), dev_x)
        g_send(k, g, 2, ghalf(k, g, slot_d, 1), ra(k, g, 1), dev_y)

    def g_b(k, g):
        g_wait(k, g, 1, ra(k, g, 0))
        add_rows(W[k].at[g], slot_y * R_G[k], ra(k, g, 0), HALF_G[k][0])
        g_send(k, g, 4, grows(k, g, slot_y), RB[k].at[g, 1], dev_y)
        g_wait(k, g, 2, ra(k, g, 1))
        add_rows(W[k].at[g], slot_x * R_G[k] + HALF_G[k][0], ra(k, g, 1), HALF_G[k][1])
        g_send(k, g, 3, grows(k, g, slot_x), RB[k].at[g, 0], dev_x)

    def g_y(k, g):
        for i in range(2):
            g_wait(k, g, 3 + i, RB[k].at[g, i])
            add_rows(W[k].at[g], slot * R_G[k], RB[k].at[g, i], R_G[k])

    def z_send(k, g):
        @pl.when(z < g)
        def _():
            rcopy(grows(k, g, slot), ZR[k].at[g], g_s.at[5, k, g], z_r.at[k, g], (dp, z + 1)).start()

        @pl.when(z > g)
        def _():
            at = jnp.where(z - 1 == g, NT, g)
            rcopy(grows(k, g, slot), ZR[k].at[at], g_s.at[5, k, g], z_r.at[k, at], (dp, z - 1)).start()

    def z_add(k, g, at):
        ref = ZR[k].at[at]
        rcopy(ref, ref, g_s.at[0, k, 0], z_r.at[k, at], dev_c).wait_recv()
        add_rows(W[k].at[g], slot * R_G[k], ref, R_G[k])

    def z_out(k, g):
        @pl.when(is_outer)
        def _():
            z_send(k, g)

    def z_in(k, g):
        @pl.when(is_inner)
        def _():
            z_add(k, g, g)
            z_send(k, g)

    def g_done(k, g):
        one = grows(k, g, 0)
        sent = [grows(k, g, 0, 4), ghalf(k, g, 0, 0), ghalf(k, g, 0, 1), one, one]
        for st, ref in enumerate(sent):
            rcopy(ref, ref, g_s.at[st, k, g], g_r.at[0, k, g], dev_c).wait_send()

        @pl.when(g != z)
        def _():
            rcopy(one, one, g_s.at[5, k, g], g_r.at[0, k, g], dev_c).wait_send()

    def orows(k, s, n=1):
        return O[k].at[pl.ds(mo(s * R_G[k], 16), n * R_G[k]), :]

    def ohalf(k, s, h):
        return O[k].at[pl.ds(mo(s * R_G[k] + h * HALF_G[k][0], 16), HALF_G[k][h]), :]

    def o_wait(k, stage, ref):
        rcopy(ref, ref, o_s.at[stage, k], o_r.at[stage, k], dev_c).wait_recv()

    def o_send(k, stage, ref, dev):
        rcopy(ref, ref, o_s.at[stage, k], o_r.at[stage, k], dev).start()

    def g_sum(k):
        @pl.when(z > 0)
        def _():
            z_add(k, z, z)

        @pl.when(z < NT - 1)
        def _():
            z_add(k, z, NT)

        O[k][pl.ds(mo(slot * R_G[k], 16), R_G[k]), :] = W[k][z, pl.ds(mo(slot * R_G[k], 16), R_G[k]), :]
        for i in range(nh):
            rcopy(orows(k, slot), RH[k].at[i], h_s.at[i, k], h_r.at[i, k], (high(i), z)).start()
            rcopy(orows(k, slot), RH[k].at[i], h_s.at[i, k], h_r.at[i, k], (high(i), z)).wait()
            add_rows(O[k], slot * R_G[k], RH[k].at[i], R_G[k])
        o_send(k, 0, orows(k, slot), dev_x)
        o_send(k, 1, orows(k, slot), dev_y)

    def o_2(k):
        o_wait(k, 0, orows(k, slot_x))
        o_send(k, 2, ohalf(k, slot_x, 0), dev_y)
        o_wait(k, 1, orows(k, slot_y))
        o_send(k, 3, ohalf(k, slot_y, 1), dev_x)

    def o_3(k):
        o_wait(k, 2, ohalf(k, slot_d, 0))
        o_wait(k, 3, ohalf(k, slot_d, 1))
        o_send(k, 4, orows(k, core * 4, 4), dev_c)

    def o_4(k):
        o_wait(k, 4, orows(k, (1 - core) * 4, 4))
        sent = [orows(k, slot)] * 2 + [ohalf(k, slot_x, 0), ohalf(k, slot_y, 1), orows(k, core * 4, 4)]
        for st, ref in enumerate(sent):
            rcopy(ref, ref, o_s.at[st, k], o_r.at[0, k], dev_c).wait_send()

    def widen(src, start, dst, first, n):
        def body(i, _):
            dst[pl.ds(mo(first + i * 64, 64), 64), :] = src[pl.ds(mo(start + i * 64, 64), 64), :].astype(F32)
            return 0

        lax.fori_loop(0, n // 64, body, 0)

    def write(src, dst, sem):
        copy = pltpu.make_async_copy(src, dst, sem)
        copy.start()
        return copy

    def out_ff(k, big, part, out, sem):
        widen(O[k], 0, big, 0, T)
        first = write(big, out.at[pl.ds(0, T), :], own_s.at[sem])
        widen(O[k], T, GN2, part * (D - T), D - T)
        return first, write(GN2.at[pl.ds(part * (D - T), D - T), :], out.at[pl.ds(T, D - T), :], own_s.at[sem + 1])

    def iota(shape, axis):
        return lax.broadcasted_iota(jnp.int32, shape, axis)

    causal = iota((CB, CB), 0) <= iota((CB, CB), 1)
    aug_tail = jnp.where(iota((16, T), 0) < 2, 1.0, 0.0).astype(BF)
    ones_rows = jnp.ones((16, T), BF)
    head_mask = (iota((HC, HC), 0) // HD) == (iota((HC, HC), 1) // HD)

    def pick(which):
        r = iota((2 * HD, HC), 0) - which * HD
        return (r == lax.rem(iota((2 * HD, HC), 1), HD)).astype(BF)

    def pick_back(which):
        r = iota((HC, 2 * HD), 1) - which * HD
        return (r == lax.rem(iota((HC, 2 * HD), 0), HD)).astype(BF)

    def block_diag(g, which):
        return jnp.where(head_mask, dot(FT[g], pick(which)), 0.0).astype(BF)

    first_end = seq_ref[0, 0]
    second_end = seq_ref[0, 0] + seq_ref[0, 1]

    def seq_id(zz):
        start = zz * T
        return (start >= first_end).astype(jnp.int32) + (start >= second_end).astype(jnp.int32)

    from_prev = jnp.logical_and(z > 0, seq_id(z) == seq_id(z - 1))
    from_next = jnp.logical_and(z < NT - 1, seq_id(z) == seq_id(z + 1))

    RB_ = 64

    def p0(i, _):
        at = pl.ds(mo(i * RB_, RB_), RB_)
        xh, _inv = norm_stats(x_ref[at, :].astype(F32))
        N1[at, :] = (xh * ln1g_ref[...] + ln1b_ref[...]).astype(BF)
        return 0

    lax.fori_loop(0, T // RB_, p0, 0)
    for g in range(NT):
        WA[g, pl.ds(D, ROWS_G[0] - D), :] = jnp.zeros((ROWS_G[0] - D, D), BF)
    GQ[pl.ds(QKV, D - QKV), :] = jnp.zeros((D - QKV, T), BF)

    @pl.when(z == 0)
    def _():
        CR[...] = jnp.zeros_like(CR)

    @pl.when(z == NT - 1)
    def _():
        GR[...] = jnp.zeros_like(GR)

    for copy in local[:4]:
        copy.wait()

    def chain_wait(buf, g, stage):
        rcopy(buf.at[g], buf.at[g], c_s.at[stage, g], c_r.at[stage, g], (dp, z)).wait_recv()

    def chain_send(g):
        rcopy(SQ.at[g], CR.at[g], c_s.at[0, g], c_r.at[0, g], (dp, z + 1)).start()

    def chain_pass(g):
        chain_wait(CR, g, 0)
        for h in range(HPG):
            carried = jnp.where(from_prev, CR[g, h].astype(F32), 0.0)
            SQ[g, h] = (ST[g * HPG + h] + carried).astype(BF)
        chain_send(g)

    def p1(j, _):
        g = wo(j)

        @pl.when(j == 1)
        def _():
            w_0(0, near)
            w_1(0, near)
            small_wait(near)

            @pl.when(is_inner)
            def _():
                w_0(0, mid)
                w_1(0, mid)
                w_0(1, near)
                w_2(0, near)
                w_0(0, far)
                w_1(0, far)
                w_0(2, near)
                w_0(1, far)
                w_2(0, mid)
                w_3(0, near)

            @pl.when(is_outer)
            def _():
                w_2(0, near)
                w_0(0, mid)
                w_1(0, mid)
                w_3(0, near)
                w_0(0, far)
                w_1(0, far)

            w_4(0, near)

        @pl.when(j == 2)
        def _():
            small_wait(mid)

            @pl.when(is_inner)
            def _():
                w_0(2, far)
                w_z(1)
                w_z(2)
                w_2(0, far)
                w_3(0, mid)
                w_1(1, far)
                w_1(2, far)

            @pl.when(is_outer)
            def _():
                w_2(0, mid)
                w_0(1, far)
                w_2(0, far)
                w_1(1, far)
                w_3(0, mid)
                w_0(2, far)
                w_1(2, far)

            w_4(0, mid)

        @pl.when(j == 3)
        def _():
            small_wait(far)
            w_3(0, far)

            @pl.when(is_inner)
            def _():
                w_0(1, mid)

            w_4(0, far)

        bias = jnp.transpose(BP[g, :, 0:256])
        bias = jnp.concatenate([bias[:HC, i : i + 1] for i in range(3)], axis=0)
        qkv = (dot(WA[g, pl.ds(0, QKV), :], N1[...], 1, 1) + bias).astype(BF)
        QK[g] = qkv[: 2 * HC]
        ql = dot(block_diag(g, 0), qkv[:HC], 0, 0)
        kl = dot(block_diag(g, 1), qkv[HC : 2 * HC], 0, 0)
        for h in range(HPG):
            hh = g * HPG + h
            rows = slice(h * HD, (h + 1) * HD)
            qf = soft_pair(ql[rows]).astype(BF)
            kf = soft_pair(kl[rows]).astype(BF)
            va = jnp.concatenate([qkv[2 * HC + h * HD : 2 * HC + (h + 1) * HD], aug_tail], axis=0)
            QF[hh] = qf
            KF[hh] = kf
            VA[hh] = va
            kn = kf.T
            ST[hh] = dot(va, kn)
            for qi in range(NB):
                qs = slice(qi * CB, (qi + 1) * CB)
                acc = None
                for ki in range(qi + 1):
                    ks = slice(ki * CB, (ki + 1) * CB)
                    s = dot(kn[ks], qf[:, qs])
                    if ki == qi:
                        s = jnp.where(causal, s, 0.0)
                    part = dot(va[:, ks], s.astype(BF))
                    acc = part if acc is None else acc + part
                NM[hh, :, qs] = acc[: HD + 8]

        @pl.when(z == 0)
        def _():
            for h in range(HPG):
                SQ[g, h] = ST[g * HPG + h].astype(BF)
            chain_send(g)

        for zz, jj, ready in ((1, 1, (0, 1)), (1, 2, (2,)), (2, 2, (1,))):

            @pl.when(jnp.logical_and(z == zz, j == jj))
            def _():
                for gg in ready:
                    chain_pass(gg)

        return 0

    lax.fori_loop(0, NT, p1, 0)
    w_2(1, far)

    @pl.when(z == 1)
    def _():
        chain_pass(3)

    @pl.when(z == 2)
    def _():
        chain_pass(0)
        chain_pass(2)

    @pl.when(is_inner)
    def _():
        w_0(2, mid)

    @pl.when(is_outer)
    def _():
        w_0(1, near)

    w_2(2, far)
    w_1(1, near)

    @pl.when(is_outer)
    def _():
        w_0(2, near)

    w_1(2, near)

    @pl.when(z == 2)
    def _():
        chain_pass(3)

    w_3(1, far)
    w_3(2, far)

    @pl.when(is_outer)
    def _():
        w_0(1, mid)

    w_1(1, mid)

    @pl.when(is_outer)
    def _():
        w_0(2, mid)

    w_1(2, mid)

    def p1b(g, _):
        @pl.when(z == NT - 1)
        def _():
            chain_wait(CR, g, 0)

        for h in range(HPG):
            CT[g * HPG + h] = jnp.where(from_prev, CR[g, h], jnp.zeros((AUG, 2 * HD), BF))
        return 0

    lax.fori_loop(0, NT, p1b, 0)

    def p1c(g, _):
        for h in range(HPG):
            hh = g * HPG + h
            num = NM[hh] + dot(CT[hh], QF[hh])[: HD + 8]
            inv = 1.0 / num[HD : HD + 1]
            DI[hh] = inv
            MX[g, pl.ds(h * HD, HD), :] = (num[:HD] * inv).astype(BF)
        return 0

    lax.fori_loop(0, NT, p1c, 0)
    w_2(1, near)
    w_2(2, near)

    def p2(n, _):
        acc = None
        for g in range(NT):
            part = dot(MX[g], WA[g, pl.ds(QKV, HC), col(n)], 0, 0)
            acc = part if acc is None else acc + part
        MID[:, col(n)] = x_ref[:, col(n)].astype(F32) + (acc + bout_ref[:, col(n)])
        return 0

    lax.fori_loop(0, D // CB, p2, 0)

    def p2b(i, _):
        at = pl.ds(mo(i * 128, 128), 128)
        xh, _inv = norm_stats(MID[at, :])
        n2 = (xh * ln2g_ref[...] + ln2b_ref[...]).astype(BF)
        N2[at, :] = n2
        N2T[:, at] = n2.T
        return 0

    lax.fori_loop(0, T // 128, p2b, 0)
    w_3(1, near)
    w_3(2, near)

    @pl.when(z < NT - 1)
    def _():
        for g in range(NT):
            rcopy(SQ.at[g], SQ.at[g], c_s.at[0, g], c_r.at[0, g], (dp, z)).wait_send()

    UN[...] = jnp.zeros_like(UN)
    GN2[...] = jnp.zeros_like(GN2)
    for copy in local[4:]:
        copy.wait()

    cc = math.sqrt(2.0 / math.pi)

    def p3(j, _):
        g = ff(j)

        @pl.when(j > 0)
        def _():
            w_4(1, g)
            w_4(2, g)

        def units(u, total):
            pre = dot(N2[...], WB[g, :, col(u)]) + BP[g, pl.ds(3, 1), col(u)]
            sq = pre * pre
            t = jnp.tanh(cc * pre * (1.0 + 0.044715 * sq))
            act = (0.5 * pre * (1.0 + t)).astype(BF)
            slope = 0.5 * (1.0 + t) + (0.5 * cc) * pre * (1.0 - t * t) * (1.0 + (3 * 0.044715) * sq)
            ACT[:, col(u)] = act
            ACTT[col(u), :] = act.T
            gact = dot(cot_ref[...], WC[g, col(u), :], 1, 1)
            gpre = (gact * slope).astype(BF)
            GP[:, col(u)] = gpre
            GBF[g, :, col(u)] = jnp.sum(gpre.astype(F32), axis=0, keepdims=True)
            return total

        lax.fori_loop(0, U // CB, units, 0)

        @pl.when(j >= 1)
        def _():
            g_a(1, ff(j - 1))
            g_a(2, ff(j - 1))

        @pl.when(j == 1)
        def _():
            w_3(1, mid)
            w_3(2, mid)

        @pl.when(j == 2)
        def _():
            g_b(1, z)
            g_b(2, z)

        def outs(n, _):
            UN[:, col(n)] += dot(ACT[...], WC[g, :, col(n)])
            GN2[:, col(n)] += dot(GP[...], WB[g, col(n), :], 1, 1)
            return 0

        lax.fori_loop(0, D // CB, outs, 0)

        @pl.when(j == 0)
        def _():
            w_2(1, mid)
            w_2(2, mid)

        def grads(n, _):
            WC[g, col(n), :] = dot(ACTT[col(n), :], cot_ref[...]).astype(BF)
            WB[g, col(n), :] = dot(N2T[col(n), :], GP[...]).astype(BF)
            return 0

        lax.fori_loop(0, D // CB, grads, 0)
        g_core(1, g)
        g_core(2, g)

        return 0

    lax.fori_loop(0, NT, p3, 0)
    g_b(1, far)
    g_b(2, far)

    VS[...] = jnp.zeros_like(VS)

    def p4(i, _):
        at = pl.ds(mo(i * RB_, RB_), RB_)
        mid = MID[at, :]
        res_ref[at, :] = (mid + UN[at, :] + bproj_ref[...]).astype(BF)
        xh, inv = norm_stats(mid)
        gn = GN2[at, :]
        gh = gn * ln2g_ref[...]
        c1 = jnp.mean(gh, axis=-1, keepdims=True)
        c2 = jnp.mean(gh * xh, axis=-1, keepdims=True)
        cot = cot_ref[at, :].astype(F32)
        gm = cot + inv * (gh - c1 - xh * c2)
        GN2[at, :] = gm
        low = gm.astype(BF)
        GML[at, :] = low
        VS[0] += jnp.sum(cot, axis=0, keepdims=True)
        VS[1] += jnp.sum(low.astype(F32), axis=0, keepdims=True)
        VS[2] += jnp.sum(gn * xh, axis=0, keepdims=True)
        VS[3] += jnp.sum(gn, axis=0, keepdims=True)
        return 0

    lax.fori_loop(0, T // RB_, p4, 0)
    g_a(1, near)
    g_a(2, near)

    tail_row = iota((16, T), 0)

    def p5a(g, _):
        gmix = dot(WA[g, pl.ds(QKV, HC), :], GML[...], 1, 1).astype(BF).astype(F32)
        mix = MX[g]
        WA[g, pl.ds(QKV, HC), :] = dot(mix, GML[...]).astype(BF)
        prod = gmix * mix.astype(F32)
        for h in range(HPG):
            hh = g * HPG + h
            rows = slice(h * HD, (h + 1) * HD)
            inv = DI[hh]
            gden = -jnp.sum(prod[rows], axis=0, keepdims=True) * inv
            hi = gden.astype(BF).astype(F32)
            lo = gden - hi
            tail = jnp.where(tail_row == 0, hi, jnp.where(tail_row == 1, lo, 0.0)).astype(BF)
            ga = jnp.concatenate([(gmix[rows] * inv).astype(BF), tail], axis=0)
            GA[hh] = ga
            gc = dot(ga, QF[hh].T)
            GC[hh] = gc
            SQ[g, h] = gc.astype(BF)

        @pl.when(z == NT - 1)
        def _():
            rcopy(SQ.at[g], GR.at[g], c_s.at[1, g], c_r.at[1, g], (dp, z - 1)).start()

        return 0

    lax.fori_loop(0, NT, p5a, 0)

    def chain_back(g, _):
        @pl.when(z < NT - 1)
        def _():
            chain_wait(GR, g, 1)
            for h in range(HPG):
                hh = g * HPG + h
                later = jnp.where(from_next, GR[g, h].astype(F32), 0.0)
                SQ[g, h] = (GC[hh] + later).astype(BF)

        @pl.when(jnp.logical_and(z > 0, z < NT - 1))
        def _():
            rcopy(SQ.at[g], GR.at[g], c_s.at[1, g], c_r.at[1, g], (dp, z - 1)).start()

        return 0

    GN1 = UN
    GN1[...] = jnp.zeros_like(GN1)

    def back(feat, grads):
        out = []
        for b in range(NB):
            bs = slice(b * CB, (b + 1) * CB)
            p = feat[:HD, bs].astype(F32)
            m = feat[HD:, bs].astype(F32)
            g1 = grads[b][:HD]
            g2 = grads[b][HD:]
            s1 = jnp.sum(g1 * p, axis=0, keepdims=True)
            s2 = jnp.sum(g2 * m, axis=0, keepdims=True)
            out.append((p * (g1 - s1) - m * (g2 - s2)).astype(BF))
        return jnp.concatenate(out, axis=1)

    def p5b(t, _):
        g = last(t)
        gql = []
        gkl = []
        for h in range(HPG):
            hh = g * HPG + h
            qf = QF[hh]
            kf = KF[hh]
            va = VA[hh]
            ga = GA[hh]
            kn = kf.T
            vn = va.T
            ctt = CT[hh].T
            gq = [None] * NB
            gk = [None] * NB
            gv = [None] * NB
            for qi in range(NB):
                qs = slice(qi * CB, (qi + 1) * CB)
                gq[qi] = dot(ctt, ga[:, qs])
                for ki in range(qi + 1):
                    ks = slice(ki * CB, (ki + 1) * CB)
                    s = dot(kn[ks], qf[:, qs])
                    gs = dot(vn[ks], ga[:, qs])
                    if ki == qi:
                        s = jnp.where(causal, s, 0.0)
                        gs = jnp.where(causal, gs, 0.0)
                    s = s.astype(BF)
                    gs = gs.astype(BF)
                    gq[qi] = gq[qi] + dot(kf[:, ks], gs)
                    pk = dot(qf[:, qs], gs, 1, 1)
                    pv = dot(ga[:, qs], s, 1, 1)[:HD]
                    gk[ki] = pk if gk[ki] is None else gk[ki] + pk
                    gv[ki] = pv if gv[ki] is None else gv[ki] + pv
            for ki in range(NB):
                ks = slice(ki * CB, (ki + 1) * CB)
                NM[3 * h, :HD, ks] = gk[ki][:HD]
                NM[3 * h + 1, :HD, ks] = gk[ki][HD:]
                NM[3 * h + 2, :HD, ks] = gv[ki]
            gql.append(back(qf, gq))

        @pl.when(t == 0)
        def _():
            lax.fori_loop(0, NT, chain_back, 0)
            for k in (1, 2):
                g_b(k, mid)
                g_y(k, z)
                g_y(k, far)

        @pl.when(t >= 1)
        def _():
            g_a(0, last(t - 1))

        @pl.when(t == 1)
        def _():
            g_b(1, near)
            g_b(2, near)

        @pl.when(t >= 2)
        def _():
            g_b(0, last(t - 2))

        for k in (1, 2):

            @pl.when(t == 2)
            def _():
                z_in(k, far)

            @pl.when(t == 3)
            def _():
                z_in(k, mid)

        @pl.when(t == 3)
        def _():
            g_y(0, far)
            z_out(0, far)

        for h in range(HPG):
            hh = g * HPG + h
            kf = KF[hh]
            va = VA[hh]
            gkc = jnp.where(from_next, GR[g, h], jnp.zeros((AUG, 2 * HD), BF))
            gkt = gkc.T
            gk = [None] * NB
            for ki in range(NB):
                ks = slice(ki * CB, (ki + 1) * CB)
                gk[ki] = jnp.concatenate([NM[3 * h, :HD, ks], NM[3 * h + 1, :HD, ks]], axis=0) + dot(gkt, va[:, ks])
                gv = NM[3 * h + 2, :HD, ks] + dot(gkc[:HD], kf[:, ks])
                GQ[pl.ds(2 * HC + h * HD, HD), ks] = gv.astype(BF)
            gkl.append(back(kf, gk))

        comp = None
        for which, parts in ((0, gql), (1, gkl)):
            glog = jnp.concatenate(parts, axis=0)
            own = QK[g, pl.ds(which * HC, HC), :]
            GQ[pl.ds(which * HC, HC), :] = dot(block_diag(g, which), glog).astype(BF)
            gfeat = jnp.where(head_mask, dot(own, glog, 1, 1), 0.0).astype(BF)
            part = dot(gfeat, pick_back(which))
            comp = part if comp is None else comp + part
        comp = comp.astype(BF)
        gq_all = GQ[...]
        gqn = gq_all[:QKV].T
        for n in range(D // CB):
            GN1[:, n * CB : (n + 1) * CB] += dot(gqn, WA[g, pl.ds(0, QKV), n * CB : (n + 1) * CB])
        WA[g, pl.ds(0, QKV), :] = dot(gq_all[:QKV], N1[...]).astype(BF)
        for b in range(HC // 32):
            WA[g, pl.ds(D, 32), b * 128 : (b + 1) * 128] = comp[b * 32 : (b + 1) * 32]
        vec = dot(ones_rows, gq_all, 1, 1)
        row = iota((16, D), 0)
        vec = jnp.where(row == 1, GBF[g], vec)
        for i in range(4):
            vec = jnp.where(row == 2 + i, VS[i], vec)
        WA[g, pl.ds(D + 32, 16), :] = vec.astype(BF)
        g_core(0, g)

        for k in (1, 2):

            @pl.when(t == 0)
            def _():
                z_out(k, far)

            @pl.when(t == 1)
            def _():
                g_y(k, mid)
                z_out(k, mid)

            @pl.when(t == 2)
            def _():
                g_y(k, near)
                z_out(k, near)

            @pl.when(t == 3)
            def _():
                z_in(k, near)

        return 0

    lax.fori_loop(0, NT, p5b, 0)

    LS[...] = jnp.zeros_like(LS)

    def p6(i, _):
        at = pl.ds(mo(i * RB_, RB_), RB_)
        xh, inv = norm_stats(x_ref[at, :].astype(F32))
        gn = GN1[at, :]
        gh = gn * ln1g_ref[...]
        c1 = jnp.mean(gh, axis=-1, keepdims=True)
        c2 = jnp.mean(gh * xh, axis=-1, keepdims=True)
        gin_ref[at, :] = (GN2[at, :] + inv * (gh - c1 - xh * c2)).astype(BF)
        LS[0, 0:1, :] += jnp.sum(gn * xh, axis=0, keepdims=True)
        LS[0, 1:2, :] += jnp.sum(gn, axis=0, keepdims=True)
        return 0

    lax.fori_loop(0, T // RB_, p6, 0)

    partners = [dp + d_core, dp + d_x, dp + d_y] + [high(i) for i in range(nh)]

    steps = len(partners)

    def small_start(i):
        rcopy(LS.at[i], LR.at[i], l_s.at[i], l_r.at[i], (partners[i], z)).start()

    def small_end(i):
        rcopy(LS.at[i], LR.at[i], l_s.at[i], l_r.at[i], (partners[i], z)).wait()
        LS[i + 1] = LS[i] + LR[i]

    small_start(0)
    g_a(0, z)
    g_b(0, near)
    g_y(0, mid)
    z_out(0, mid)
    z_in(0, far)
    small_end(0)
    small_start(1)
    g_b(0, z)
    z_in(0, mid)
    g_y(0, near)
    z_out(0, near)
    z_in(0, near)
    small_end(1)
    small_start(2)
    g_sum(1)
    g_sum(2)
    small_end(2)
    for i in range(3, steps):
        small_start(i)
        small_end(i)
    LZ[z] = LS[steps]
    for o in range(1, NT):
        rcopy(LS.at[steps], LZ.at[z], lz_s.at[o - 1], lz_r.at[z], (dp, lax.rem(z + o, NT))).start()
    o_2(1)
    o_2(2)
    g_y(0, z)
    g_sum(0)
    o_3(1)
    o_3(2)
    o_2(0)
    o_4(1)
    outs = [*out_ff(1, MID, 0, ob_ref, 0)]
    o_4(2)
    outs += [*out_ff(2, UN, 1, oc_ref, 2)]
    for o in range(1, NT):
        zz = lax.rem(z + o, NT)
        rcopy(LZ.at[zz], LZ.at[zz], lz_s.at[o - 1], lz_r.at[zz], (dp, z)).wait_recv()
    total = LZ[0]
    for zz in range(1, NT):
        total = total + LZ[zz]
    gln1g_ref[...] = total[0:1].reshape(D)
    gln1b_ref[...] = total[1:2].reshape(D)
    o_3(0)
    o_4(0)
    widen(OA, 0, WO, 0, QKV)
    outs.append(write(WO.at[pl.ds(0, QKV), :], oa_ref, own_s.at[4]))
    widen(OA, QKV, WO, QKV, HC)
    outs.append(write(WO.at[pl.ds(QKV, HC), :], oo_ref, own_s.at[5]))
    for b in range(HC // 32):
        block = OA[D : D + 32, b * 128 : (b + 1) * 128].astype(F32)
        rows = slice(b % 2 * 32, b % 2 * 32 + 32)
        gfq_ref[b // 2, rows, :] = block[:, :HD]
        gfk_ref[b // 2, rows, :] = block[:, HD:]
    vec = OA[D + 32 : D + 48, :].astype(F32)
    for i in range(3):
        gbqkv_ref[i : i + 1, :] = vec[0:1, i * HC : (i + 1) * HC]
    for i, ref in enumerate((gbfc_ref, gbproj_ref, gbout_ref, gln2g_ref, gln2b_ref)):
        ref[...] = vec[i + 1 : i + 2].reshape(D)
    for copy in outs:
        copy.wait()

    for o in range(1, NT):
        rcopy(LS.at[steps], LZ.at[z], lz_s.at[o - 1], lz_r.at[z], (dp, lax.rem(z + o, NT))).wait_send()
    small_done()
    for k in range(KINDS):
        w_z_done(k)
        for g in range(NT):
            g_done(k, g)

    @pl.when(z > 0)
    def _():
        for g in range(NT):
            rcopy(SQ.at[g], SQ.at[g], c_s.at[1, g], c_r.at[1, g], (dp, z)).wait_send()


def layer_call(nh, T, *args):
    def vm(shape, dtype=BF):
        return pltpu.VMEM(shape, dtype)

    dma = pltpu.SemaphoreType.DMA
    nhb = max(nh, 1)
    nst = 3 + nh
    scratch = [
        vm((NT, ROWS_G[0], D)),
        vm((NT, D, U)),
        vm((NT, U, D)),
        vm((NT, HC, 2 * HD)),
        vm((NT, 8, D), F32),
    ]
    scratch += [vm((NT, 4 * r, D)) for r in R_G]
    scratch += [vm((NT, r, D)) for r in R_G]
    scratch += [vm((NT, 2, r, D)) for r in R_G]
    scratch += [vm((NT + 1, r, D)) for r in R_G]
    scratch += [vm((rows, D)) for rows in ROWS_G]
    scratch += [vm((nhb, r if nh else 16, D)) for r in R_G]
    scratch += [vm((nst + 1, 8, D), F32), vm((nst, 8, D), F32), vm((NT, 8, D), F32)]
    scratch += [
        vm((T, D)),
        vm((NT, 2 * HC, T)),
        vm((NH, AUG, T)),
        vm((NH, 2 * HD, T)),
        vm((NH, 2 * HD, T)),
        vm((NH, HD + 8, T), F32),
        vm((NH, AUG, 2 * HD), F32),
        vm((NH, AUG, 2 * HD)),
        vm((NT, HPG, AUG, 2 * HD)),
        vm((NT, HPG, AUG, 2 * HD)),
        vm((NT, HPG, AUG, 2 * HD)),
        vm((NT, HC, T)),
        vm((NH, 1, T), F32),
        vm((T, D), F32),
        vm((T, D)),
        vm((D, T)),
        vm((T, D), F32),
        vm((T, D), F32),
        vm((T, D)),
        vm((T, U)),
        vm((U, T)),
        vm((T, U)),
        vm((NT, 1, U), F32),
        vm((NH, AUG, T)),
        vm((NH, AUG, 2 * HD), F32),
        vm((D, T)),
        vm((4, 1, D), F32),
        vm((6, 1, D), F32),
        vm((HC, 2 * HD)),
        vm((8, D), F32),
        vm((D, D), F32),
    ]
    scratch += [
        dma((6,)),
        dma((2, NT - 1)),
        dma((2, NT)),
        dma((KINDS, 2)),
        dma((6, KINDS, NT)),
        dma((6, KINDS, NT)),
        dma((6, KINDS, NT)),
        dma((5, KINDS, NT)),
        dma((KINDS, NT + 1)),
        dma((5, KINDS)),
        dma((5, KINDS)),
        dma((nhb, KINDS)),
        dma((nhb, KINDS)),
        dma((nst,)),
        dma((nst,)),
        dma((NT - 1,)),
        dma((NT,)),
        dma((2, NT)),
        dma((2, NT)),
    ]
    vmem = pl.BlockSpec(memory_space=pltpu.VMEM)
    hbm = pl.BlockSpec(memory_space=pl.ANY)
    return pl.pallas_call(
        functools.partial(layer_kernel, nh),
        out_shape=(
            jax.ShapeDtypeStruct((T, D), BF),
            jax.ShapeDtypeStruct((T, D), BF),
            jax.ShapeDtypeStruct((QKV, D), F32),
            jax.ShapeDtypeStruct((HC, D), F32),
            jax.ShapeDtypeStruct((D, U), F32),
            jax.ShapeDtypeStruct((U, D), F32),
            jax.ShapeDtypeStruct((HPG, HD, HD), F32),
            jax.ShapeDtypeStruct((HPG, HD, HD), F32),
            jax.ShapeDtypeStruct((3, HC), F32),
            *[jax.ShapeDtypeStruct((D,), F32)] * 7,
        ),
        in_specs=[pl.BlockSpec(memory_space=pltpu.SMEM)] + [vmem] * 12 + [hbm] * 4,
        out_specs=(vmem, vmem, hbm, hbm, hbm, hbm, *[vmem] * 10),
        scratch_shapes=scratch,
        compiler_params=pltpu.CompilerParams(
            collective_id=0, has_side_effects=True, vmem_limit_bytes=67043328
        ),
    )(*args)


def local(
    nh,
    tokens_in,
    ln1_gain,
    ln1_bias,
    w_qkv,
    b_qkv,
    feat_q,
    feat_k,
    w_out,
    b_out,
    ln2_gain,
    ln2_bias,
    w_fc,
    b_fc,
    w_proj,
    b_proj,
    seq_lengths,
    cotangent,
):
    T = tokens_in.shape[0]
    w_qkv_t = jnp.transpose(w_qkv, (1, 2, 0)).reshape(QKV, D)
    res, gin, g_w_qkv, g_w_out, g_w_fc, g_w_proj, g_fq, g_fk, g_bqkv, g_bfc, g_bproj, g_bout, *g_ln = layer_call(
        nh,
        T,
        seq_lengths,
        tokens_in,
        cotangent,
        ln1_gain,
        ln1_bias,
        b_out,
        ln2_gain,
        ln2_bias,
        b_proj,
        b_fc,
        b_qkv,
        feat_q,
        feat_k,
        w_qkv_t,
        w_out,
        w_fc,
        w_proj,
    )
    g_w_qkv = jnp.transpose(g_w_qkv.reshape(3, HC, D), (2, 0, 1))
    g_ln2g, g_ln2b, g_ln1g, g_ln1b = g_ln
    return (
        res,
        gin,
        g_ln1g,
        g_ln1b,
        g_w_qkv,
        g_bqkv,
        g_fq,
        g_fk,
        g_w_out,
        g_bout,
        g_ln2g,
        g_ln2b,
        g_w_fc,
        g_bfc,
        g_w_proj,
        g_bproj,
    )


def solution(mesh):
    n_dp = mesh.shape["dp"]
    nh = max(0, (n_dp // 8).bit_length() - 1)
    return jax.shard_map(
        functools.partial(local, nh),
        mesh=mesh,
        in_specs=(
            P(("dp", "tensor"), None),
            P(),
            P(),
            P(None, None, "tensor"),
            P(None, "tensor"),
            P("tensor", None, None),
            P("tensor", None, None),
            P("tensor", None),
            P(),
            P(),
            P(),
            P(None, "tensor"),
            P("tensor"),
            P("tensor", None),
            P(),
            P("dp", None),
            P(("dp", "tensor"), None),
        ),
        out_specs=(
            P(("dp", "tensor"), None),
            P(("dp", "tensor"), None),
            P(),
            P(),
            P(None, None, "tensor"),
            P(None, "tensor"),
            P("tensor", None, None),
            P("tensor", None, None),
            P("tensor", None),
            P(),
            P(),
            P(),
            P(None, "tensor"),
            P("tensor"),
            P("tensor", None),
            P(),
        ),
        check_vma=False,
    )
```

```python
import functools
import math

import jax
import jax.numpy as jnp
from jax import lax
from jax.experimental import pallas as pl
from jax.experimental.pallas import tpu as pltpu
from jax.sharding import PartitionSpec as P

NORM_EPS = 1e-05
BF = jnp.bfloat16
F32 = jnp.float32
MESH = pl.DeviceIdType.MESH
NT = 4
D = 768
HD = 64
HPG = 3
HC = HPG * HD
NH = NT * HPG
U = 768
AUG = 80
QKV = 3 * HC
KINDS = 3
R_W = 96
R_G = (112, 96, 96)
ROWS_G = (896, 768, 768)
CB = 256
HALF_W = (48, 48)
HALF_G = ((64, 48), (48, 48), (48, 48))


def dot(a, b, ca=1, cb=0):
    return lax.dot_general(a, b, (((ca,), (cb,)), ((), ())), preferred_element_type=F32)


def mo(value, multiple):
    return pl.multiple_of(value, multiple)


def soft_pair(logits):
    top = jnp.max(logits, axis=0, keepdims=True)
    low = jnp.min(logits, axis=0, keepdims=True)
    e_pos = jnp.exp(logits - top)
    e_neg = jnp.exp(low - logits)
    p = e_pos * (1.0 / jnp.sum(e_pos, axis=0, keepdims=True))
    m = e_neg * (1.0 / jnp.sum(e_neg, axis=0, keepdims=True))
    return jnp.concatenate([p, m], axis=0)


def norm_stats(rows):
    mean = jnp.mean(rows, axis=-1, keepdims=True)
    centred = rows - mean
    var = jnp.mean(centred * centred, axis=-1, keepdims=True)
    inv = lax.rsqrt(var + NORM_EPS)
    return centred * inv, inv


def col(n):
    return pl.ds(mo(n * CB, CB), CB)


def layer_kernel(
    nh,
    seq_ref,
    x_ref,
    cot_ref,
    ln1g_in,
    ln1b_in,
    bout_in,
    ln2g_in,
    ln2b_in,
    bproj_in,
    bfc_in,
    bqkv_in,
    fq_in,
    fk_in,
    a_own,
    a_out,
    b_own,
    c_own,
    res_ref,
    gin_ref,
    oa_ref,
    oo_ref,
    ob_ref,
    oc_ref,
    gfq_ref,
    gfk_ref,
    gbqkv_ref,
    gbfc_ref,
    gbproj_ref,
    gbout_ref,
    gln2g_ref,
    gln2b_ref,
    gln1g_ref,
    gln1b_ref,
    WA,
    WB,
    WC,
    FT,
    BP,
    R0A,
    R0B,
    R0C,
    RAA,
    RAB,
    RAC,
    RBA,
    RBB,
    RBC,
    ZRA,
    ZRB,
    ZRC,
    OA,
    OB,
    OC,
    RHA,
    RHB,
    RHC,
    LS,
    LR,
    LZ,
    N1,
    QK,
    VA,
    QF,
    KF,
    NM,
    ST,
    CT,
    CR,
    SQ,
    GR,
    MX,
    DI,
    MID,
    N2,
    N2T,
    UN,
    GN2,
    GML,
    ACT,
    ACTT,
    GP,
    GBF,
    GA,
    GC,
    GQ,
    VS,
    PV,
    ft_own,
    bp_own,
    WO,
    own_s,
    sm_s,
    sm_r,
    wz_s,
    w_s,
    w_r,
    g_s,
    g_r,
    z_r,
    o_s,
    o_r,
    h_s,
    h_r,
    l_s,
    l_r,
    lz_s,
    lz_r,
    c_s,
    c_r,
):
    dp = lax.axis_index("dp")
    z = lax.axis_index("tensor")
    T = x_ref.shape[0]
    NB = T // CB
    core = lax.rem(dp, 2)
    bx = lax.rem(dp // 2, 2)
    by = lax.rem(dp // 4, 2)
    d_core = 1 - 2 * core
    d_x = 2 * (1 - 2 * bx)
    d_y = 4 * (1 - 2 * by)
    slot = core * 4 + by * 2 + bx

    W = (WA, WB, WC)
    OWN = (a_own, b_own, c_own)
    R0 = (R0A, R0B, R0C)
    RA = (RAA, RAB, RAC)
    RB = (RBA, RBB, RBC)
    ZR = (ZRA, ZRB, ZRC)
    O = (OA, OB, OC)
    RH = (RHA, RHB, RHC)

    near = z + 1 - 2 * lax.rem(z, 2)
    mid = 2 - z // 2
    far = 3 * (1 - z // 2)
    is_outer = jnp.logical_or(z == 0, z == NT - 1)
    is_inner = jnp.logical_and(z > 0, z < NT - 1)

    def choose(j, groups):
        out = groups[-1]
        for i in range(NT - 2, -1, -1):
            out = jnp.where(j == i, groups[i], out)
        return out

    def wo(j):
        return choose(j, (z, near, mid, far))

    def ff(j):
        return choose(j, (z, far, mid, near))

    def last(t):
        return choose(t, (far, mid, near, z))

    def high(i):
        step = 8 * 2**i
        return dp + step * (1 - 2 * lax.rem(dp // step, 2))

    def rcopy(src, dst, ssem, rsem, dev):
        return pltpu.make_async_remote_copy(
            src_ref=src, dst_ref=dst, send_sem=ssem, recv_sem=rsem, device_id=dev, device_id_type=MESH
        )

    dev_x = (dp + d_x, z)
    dev_y = (dp + d_y, z)
    dev_c = (dp + d_core, z)
    slot_x = core * 4 + by * 2 + (1 - bx)
    slot_y = core * 4 + (1 - by) * 2 + bx
    slot_d = core * 4 + (1 - by) * 2 + (1 - bx)

    for i, ref in enumerate((ln1g_in, ln1b_in, bout_in, ln2g_in, ln2b_in, bproj_in)):
        PV[i] = ref[...].reshape(1, D)
    ln1g_ref, ln1b_ref, bout_ref, ln2g_ref, ln2b_ref, bproj_ref = (PV.at[i] for i in range(6))
    bp_own[...] = jnp.zeros_like(bp_own)
    bp_own[0:3, 0:HC] = bqkv_in[...]
    bp_own[3:4, :] = bfc_in[...].reshape(1, D)
    for h in range(HPG):
        ft_own[h * HD : (h + 1) * HD, :] = jnp.concatenate([fq_in[h], fk_in[h]], axis=1)

    peers = [(dp + d_core, z), (dp + d_x, z), (dp + d_y, z)]
    peers += [(high(i), z) for i in range(nh)]
    peers += [(dp, lax.rem(z + o, NT)) for o in range(1, NT)]
    barrier = pltpu.get_barrier_semaphore()
    for peer in peers:
        pl.semaphore_signal(barrier, inc=1, device_id=peer, device_id_type=MESH)
    pl.semaphore_wait(barrier, len(peers))

    def wrows(k, g, s):
        return W[k].at[g, pl.ds(mo(s * R_W, R_W), R_W), :]

    def wrows4(k, g, c):
        return W[k].at[g, pl.ds(mo(c * 4 * R_W, R_W), 4 * R_W), :]

    def whalf(k, g, s, h):
        return W[k].at[g, pl.ds(mo(s * R_W + h * HALF_W[0], 16), HALF_W[h]), :]

    def z_next(g):
        return jnp.where(g < z, z + 1, z - 1)

    def own_rows(k):
        at = pl.ds(mo(slot * R_W, R_W), R_W)
        if k:
            return ((slot >= 0, OWN[k].at[at, :]),)
        split = QKV // R_W
        low = jnp.where(slot < split, slot, 0)
        high = jnp.where(slot < split, 0, slot - split)
        return (
            (slot < split, a_own.at[pl.ds(mo(low * R_W, R_W), R_W), :]),
            (slot >= split, a_out.at[pl.ds(mo(high * R_W, R_W), R_W), :]),
        )

    def w_z(k):
        for here, src in own_rows(k):

            @pl.when(jnp.logical_and(here, z < NT - 1))
            def _():
                rcopy(src, wrows(k, z, slot), wz_s.at[k, 0], w_r.at[0, k, z], (dp, z + 1)).start()

            @pl.when(jnp.logical_and(here, z > 0))
            def _():
                rcopy(src, wrows(k, z, slot), wz_s.at[k, 1], w_r.at[0, k, z], (dp, z - 1)).start()

    def w_wait(k, g, stage, ref):
        rcopy(ref, ref, w_s.at[0, k, g], w_r.at[stage, k, g], dev_c).wait_recv()

    def w_send(k, g, s_stage, r_stage, ref, dev):
        rcopy(ref, ref, w_s.at[s_stage, k, g], w_r.at[r_stage, k, g], dev).start()

    def w_0(k, g):
        mine = wrows(k, g, slot)
        w_wait(k, g, 0, mine)

        @pl.when(is_inner)
        def _():
            w_send(k, g, 5, 0, mine, (dp, z_next(g)))

    def w_1(k, g):
        mine = wrows(k, g, slot)
        w_send(k, g, 0, 1, mine, dev_x)
        w_send(k, g, 1, 2, mine, dev_y)

    def w_2(k, g):
        w_wait(k, g, 1, wrows(k, g, slot_x))
        w_send(k, g, 2, 3, whalf(k, g, slot_x, 0), dev_y)
        w_wait(k, g, 2, wrows(k, g, slot_y))
        w_send(k, g, 3, 4, whalf(k, g, slot_y, 1), dev_x)

    def w_3(k, g):
        w_wait(k, g, 3, whalf(k, g, slot_d, 0))
        w_wait(k, g, 4, whalf(k, g, slot_d, 1))
        w_send(k, g, 4, 5, wrows4(k, g, core), dev_c)

    def w_4(k, g):
        w_wait(k, g, 5, wrows4(k, g, 1 - core))
        sent = [wrows(k, g, slot)] * 2 + [whalf(k, g, slot_x, 0), whalf(k, g, slot_y, 1), wrows4(k, g, core)]
        for st, ref in enumerate(sent):
            rcopy(ref, ref, w_s.at[st, k, g], w_r.at[0, k, g], dev_c).wait_send()

        @pl.when(is_inner)
        def _():
            mine = wrows(k, g, slot)
            rcopy(mine, mine, w_s.at[5, k, g], w_r.at[0, k, g], dev_c).wait_send()

    def w_z_done(k):
        src = own_rows(k)[0][1]

        @pl.when(z < NT - 1)
        def _():
            rcopy(src, wrows(k, z, slot), wz_s.at[k, 0], w_r.at[0, k, z], (dp, z + 1)).wait_send()

        @pl.when(z > 0)
        def _():
            rcopy(src, wrows(k, z, slot), wz_s.at[k, 1], w_r.at[0, k, z], (dp, z - 1)).wait_send()

    small = ((ft_own, FT), (bp_own, BP))

    def small_send():
        for i, (own, buf) in enumerate(small):
            for o in range(1, NT):
                rcopy(own, buf.at[z], sm_s.at[i, o - 1], sm_r.at[i, z], (dp, lax.rem(z + o, NT))).start()

    def small_wait(g):
        for i, (own, buf) in enumerate(small):
            rcopy(own, buf.at[g], sm_s.at[i, 0], sm_r.at[i, g], (dp, z)).wait_recv()

    def small_done():
        for i, (own, buf) in enumerate(small):
            for o in range(1, NT):
                rcopy(own, buf.at[z], sm_s.at[i, o - 1], sm_r.at[i, z], (dp, lax.rem(z + o, NT))).wait_send()

    local = [
        pltpu.make_async_copy(ft_own, FT.at[z], own_s.at[0]),
        pltpu.make_async_copy(bp_own, BP.at[z], own_s.at[1]),
        pltpu.make_async_copy(a_own, WA.at[z, pl.ds(0, QKV), :], own_s.at[2]),
        pltpu.make_async_copy(a_out, WA.at[z, pl.ds(QKV, HC), :], own_s.at[5]),
        pltpu.make_async_copy(b_own, WB.at[z], own_s.at[3]),
        pltpu.make_async_copy(c_own, WC.at[z], own_s.at[4]),
    ]
    small_send()
    w_z(0)

    @pl.when(is_outer)
    def _():
        w_z(1)
        w_z(2)

    for copy in local:
        copy.start()

    def grows(k, g, s, n=1):
        return W[k].at[g, pl.ds(mo(s * R_G[k], 16), n * R_G[k]), :]

    def add_rows(dst, start, src, n):
        blk = 16 if n % 32 else 32

        def body(i, _):
            at = pl.ds(mo(start + i * blk, 16), blk)
            dst[at, :] = (dst[at, :].astype(F32) + src[pl.ds(mo(i * blk, 16), blk), :].astype(F32)).astype(BF)
            return 0

        lax.fori_loop(0, n // blk, body, 0)

    def ghalf(k, g, s, h):
        return W[k].at[g, pl.ds(mo(s * R_G[k] + h * HALF_G[k][0], 16), HALF_G[k][h]), :]

    def ra(k, g, h):
        return RA[k].at[g, pl.ds(h * HALF_G[k][0], HALF_G[k][h]), :]

    def g_wait(k, g, stage, ref):
        rcopy(ref, ref, g_s.at[0, k, g], g_r.at[stage, k, g], dev_c).wait_recv()

    def g_send(k, g, stage, src, dst, dev):
        rcopy(src, dst, g_s.at[stage, k, g], g_r.at[stage, k, g], dev).start()

    def g_core(k, g):
        g_send(k, g, 0, grows(k, g, (1 - core) * 4, 4), R0[k].at[g], dev_c)

    def g_a(k, g):
        g_wait(k, g, 0, R0[k].at[g])
        add_rows(W[k].at[g], core * 4 * R_G[k], R0[k].at[g], 4 * R_G[k])
        g_send(k, g, 1, ghalf(k, g, slot_d, 0), ra(k, g, 0), dev_x)
        g_send(k, g, 2, ghalf(k, g, slot_d, 1), ra(k, g, 1), dev_y)

    def g_b(k, g):
        g_wait(k, g, 1, ra(k, g, 0))
        add_rows(W[k].at[g], slot_y * R_G[k], ra(k, g, 0), HALF_G[k][0])
        g_send(k, g, 4, grows(k, g, slot_y), RB[k].at[g, 1], dev_y)
        g_wait(k, g, 2, ra(k, g, 1))
        add_rows(W[k].at[g], slot_x * R_G[k] + HALF_G[k][0], ra(k, g, 1), HALF_G[k][1])
        g_send(k, g, 3, grows(k, g, slot_x), RB[k].at[g, 0], dev_x)

    def g_y(k, g):
        for i in range(2):
            g_wait(k, g, 3 + i, RB[k].at[g, i])
            add_rows(W[k].at[g], slot * R_G[k], RB[k].at[g, i], R_G[k])

    def z_send(k, g):
        @pl.when(z < g)
        def _():
            rcopy(grows(k, g, slot), ZR[k].at[g], g_s.at[5, k, g], z_r.at[k, g], (dp, z + 1)).start()

        @pl.when(z > g)
        def _():
            at = jnp.where(z - 1 == g, NT, g)
            rcopy(grows(k, g, slot), ZR[k].at[at], g_s.at[5, k, g], z_r.at[k, at], (dp, z - 1)).start()

    def z_add(k, g, at):
        ref = ZR[k].at[at]
        rcopy(ref, ref, g_s.at[0, k, 0], z_r.at[k, at], dev_c).wait_recv()
        add_rows(W[k].at[g], slot * R_G[k], ref, R_G[k])

    def z_out(k, g):
        @pl.when(is_outer)
        def _():
            z_send(k, g)

    def z_in(k, g):
        @pl.when(is_inner)
        def _():
            z_add(k, g, g)
            z_send(k, g)

    def g_done(k, g):
        one = grows(k, g, 0)
        sent = [grows(k, g, 0, 4), ghalf(k, g, 0, 0), ghalf(k, g, 0, 1), one, one]
        for st, ref in enumerate(sent):
            rcopy(ref, ref, g_s.at[st, k, g], g_r.at[0, k, g], dev_c).wait_send()

        @pl.when(g != z)
        def _():
            rcopy(one, one, g_s.at[5, k, g], g_r.at[0, k, g], dev_c).wait_send()

    def orows(k, s, n=1):
        return O[k].at[pl.ds(mo(s * R_G[k], 16), n * R_G[k]), :]

    def ohalf(k, s, h):
        return O[k].at[pl.ds(mo(s * R_G[k] + h * HALF_G[k][0], 16), HALF_G[k][h]), :]

    def o_wait(k, stage, ref):
        rcopy(ref, ref, o_s.at[stage, k], o_r.at[stage, k], dev_c).wait_recv()

    def o_send(k, stage, ref, dev):
        rcopy(ref, ref, o_s.at[stage, k], o_r.at[stage, k], dev).start()

    def g_sum(k):
        @pl.when(z > 0)
        def _():
            z_add(k, z, z)

        @pl.when(z < NT - 1)
        def _():
            z_add(k, z, NT)

        O[k][pl.ds(mo(slot * R_G[k], 16), R_G[k]), :] = W[k][z, pl.ds(mo(slot * R_G[k], 16), R_G[k]), :]
        for i in range(nh):
            rcopy(orows(k, slot), RH[k].at[i], h_s.at[i, k], h_r.at[i, k], (high(i), z)).start()
            rcopy(orows(k, slot), RH[k].at[i], h_s.at[i, k], h_r.at[i, k], (high(i), z)).wait()
            add_rows(O[k], slot * R_G[k], RH[k].at[i], R_G[k])
        o_send(k, 0, orows(k, slot), dev_x)
        o_send(k, 1, orows(k, slot), dev_y)

    def o_2(k):
        o_wait(k, 0, orows(k, slot_x))
        o_send(k, 2, ohalf(k, slot_x, 0), dev_y)
        o_wait(k, 1, orows(k, slot_y))
        o_send(k, 3, ohalf(k, slot_y, 1), dev_x)

    def o_3(k):
        o_wait(k, 2, ohalf(k, slot_d, 0))
        o_wait(k, 3, ohalf(k, slot_d, 1))
        o_send(k, 4, orows(k, core * 4, 4), dev_c)

    def o_4(k):
        o_wait(k, 4, orows(k, (1 - core) * 4, 4))
        sent = [orows(k, slot)] * 2 + [ohalf(k, slot_x, 0), ohalf(k, slot_y, 1), orows(k, core * 4, 4)]
        for st, ref in enumerate(sent):
            rcopy(ref, ref, o_s.at[st, k], o_r.at[0, k], dev_c).wait_send()

    def widen(src, start, dst, first, n):
        def body(i, _):
            dst[pl.ds(mo(first + i * 64, 64), 64), :] = src[pl.ds(mo(start + i * 64, 64), 64), :].astype(F32)
            return 0

        lax.fori_loop(0, n // 64, body, 0)

    def write(src, dst, sem):
        copy = pltpu.make_async_copy(src, dst, sem)
        copy.start()
        return copy

    def out_ff(k, big, part, out, sem):
        widen(O[k], 0, big, 0, T)
        first = write(big, out.at[pl.ds(0, T), :], own_s.at[sem])
        widen(O[k], T, GN2, part * (D - T), D - T)
        return first, write(GN2.at[pl.ds(part * (D - T), D - T), :], out.at[pl.ds(T, D - T), :], own_s.at[sem + 1])

    def iota(shape, axis):
        return lax.broadcasted_iota(jnp.int32, shape, axis)

    causal = iota((CB, CB), 0) <= iota((CB, CB), 1)
    aug_tail = jnp.where(iota((16, T), 0) < 2, 1.0, 0.0).astype(BF)
    ones_rows = jnp.ones((16, T), BF)
    head_mask = (iota((HC, HC), 0) // HD) == (iota((HC, HC), 1) // HD)

    def pick(which):
        r = iota((2 * HD, HC), 0) - which * HD
        return (r == lax.rem(iota((2 * HD, HC), 1), HD)).astype(BF)

    def pick_back(which):
        r = iota((HC, 2 * HD), 1) - which * HD
        return (r == lax.rem(iota((HC, 2 * HD), 0), HD)).astype(BF)

    def block_diag(g, which):
        return jnp.where(head_mask, dot(FT[g], pick(which)), 0.0).astype(BF)

    first_end = seq_ref[0, 0]
    second_end = seq_ref[0, 0] + seq_ref[0, 1]

    def seq_id(zz):
        start = zz * T
        return (start >= first_end).astype(jnp.int32) + (start >= second_end).astype(jnp.int32)

    from_prev = jnp.logical_and(z > 0, seq_id(z) == seq_id(z - 1))
    from_next = jnp.logical_and(z < NT - 1, seq_id(z) == seq_id(z + 1))

    RB_ = 64

    def p0(i, _):
        at = pl.ds(mo(i * RB_, RB_), RB_)
        xh, _inv = norm_stats(x_ref[at, :].astype(F32))
        N1[at, :] = (xh * ln1g_ref[...] + ln1b_ref[...]).astype(BF)
        return 0

    lax.fori_loop(0, T // RB_, p0, 0)
    for g in range(NT):
        WA[g, pl.ds(D, ROWS_G[0] - D), :] = jnp.zeros((ROWS_G[0] - D, D), BF)
    GQ[pl.ds(QKV, D - QKV), :] = jnp.zeros((D - QKV, T), BF)

    @pl.when(z == 0)
    def _():
        CR[...] = jnp.zeros_like(CR)

    @pl.when(z == NT - 1)
    def _():
        GR[...] = jnp.zeros_like(GR)

    for copy in local[:4]:
        copy.wait()

    def chain_wait(buf, g, stage):
        rcopy(buf.at[g], buf.at[g], c_s.at[stage, g], c_r.at[stage, g], (dp, z)).wait_recv()

    def chain_send(g):
        rcopy(SQ.at[g], CR.at[g], c_s.at[0, g], c_r.at[0, g], (dp, z + 1)).start()

    def chain_pass(g):
        chain_wait(CR, g, 0)
        for h in range(HPG):
            carried = jnp.where(from_prev, CR[g, h].astype(F32), 0.0)
            SQ[g, h] = (ST[g * HPG + h] + carried).astype(BF)
        chain_send(g)

    def p1(j, _):
        g = wo(j)

        @pl.when(j == 1)
        def _():
            w_0(0, near)
            w_1(0, near)
            small_wait(near)

            @pl.when(is_inner)
            def _():
                w_0(0, mid)
                w_1(0, mid)
                w_0(1, near)
                w_2(0, near)
                w_0(0, far)
                w_1(0, far)
                w_0(2, near)
                w_0(1, far)
                w_2(0, mid)
                w_3(0, near)

            @pl.when(is_outer)
            def _():
                w_2(0, near)
                w_0(0, mid)
                w_1(0, mid)
                w_3(0, near)
                w_0(0, far)
                w_1(0, far)

            w_4(0, near)

        @pl.when(j == 2)
        def _():
            small_wait(mid)

            @pl.when(is_inner)
            def _():
                w_0(2, far)
                w_z(1)
                w_z(2)
                w_2(0, far)
                w_3(0, mid)
                w_1(1, far)
                w_1(2, far)

            @pl.when(is_outer)
            def _():
                w_2(0, mid)
                w_0(1, far)
                w_2(0, far)
                w_1(1, far)
                w_3(0, mid)
                w_0(2, far)
                w_1(2, far)

            w_4(0, mid)

        @pl.when(j == 3)
        def _():
            small_wait(far)
            w_3(0, far)

            @pl.when(is_inner)
            def _():
                w_0(1, mid)

            w_4(0, far)

        bias = jnp.transpose(BP[g, :, 0:256])
        bias = jnp.concatenate([bias[:HC, i : i + 1] for i in range(3)], axis=0)
        qkv = (dot(WA[g, pl.ds(0, QKV), :], N1[...], 1, 1) + bias).astype(BF)
        QK[g] = qkv[: 2 * HC]
        ql = dot(block_diag(g, 0), qkv[:HC], 0, 0)
        kl = dot(block_diag(g, 1), qkv[HC : 2 * HC], 0, 0)
        for h in range(HPG):
            hh = g * HPG + h
            rows = slice(h * HD, (h + 1) * HD)
            qf = soft_pair(ql[rows]).astype(BF)
            kf = soft_pair(kl[rows]).astype(BF)
            va = jnp.concatenate([qkv[2 * HC + h * HD : 2 * HC + (h + 1) * HD], aug_tail], axis=0)
            QF[hh] = qf
            KF[hh] = kf
            VA[hh] = va
            kn = kf.T
            ST[hh] = dot(va, kn)
            for qi in range(NB):
                qs = slice(qi * CB, (qi + 1) * CB)
                acc = None
                for ki in range(qi + 1):
                    ks = slice(ki * CB, (ki + 1) * CB)
                    s = dot(kn[ks], qf[:, qs])
                    if ki == qi:
                        s = jnp.where(causal, s, 0.0)
                    part = dot(va[:, ks], s.astype(BF))
                    acc = part if acc is None else acc + part
                NM[hh, :, qs] = acc[: HD + 8]

        @pl.when(z == 0)
        def _():
            for h in range(HPG):
                SQ[g, h] = ST[g * HPG + h].astype(BF)
            chain_send(g)

        for zz, jj, ready in ((1, 1, (0, 1)), (1, 2, (2,)), (2, 2, (1,))):

            @pl.when(jnp.logical_and(z == zz, j == jj))
            def _():
                for gg in ready:
                    chain_pass(gg)

        return 0

    lax.fori_loop(0, NT, p1, 0)
    w_2(1, far)

    @pl.when(z == 1)
    def _():
        chain_pass(3)

    @pl.when(z == 2)
    def _():
        chain_pass(0)
        chain_pass(2)

    @pl.when(is_inner)
    def _():
        w_0(2, mid)

    @pl.when(is_outer)
    def _():
        w_0(1, near)

    w_2(2, far)
    w_1(1, near)

    @pl.when(is_outer)
    def _():
        w_0(2, near)

    w_1(2, near)

    @pl.when(z == 2)
    def _():
        chain_pass(3)

    w_3(1, far)
    w_3(2, far)

    @pl.when(is_outer)
    def _():
        w_0(1, mid)

    w_1(1, mid)

    @pl.when(is_outer)
    def _():
        w_0(2, mid)

    w_1(2, mid)

    def p1b(g, _):
        @pl.when(z == NT - 1)
        def _():
            chain_wait(CR, g, 0)

        for h in range(HPG):
            CT[g * HPG + h] = jnp.where(from_prev, CR[g, h], jnp.zeros((AUG, 2 * HD), BF))
        return 0

    lax.fori_loop(0, NT, p1b, 0)

    def p1c(g, _):
        for h in range(HPG):
            hh = g * HPG + h
            num = NM[hh] + dot(CT[hh], QF[hh])[: HD + 8]
            inv = 1.0 / num[HD : HD + 1]
            DI[hh] = inv
            MX[g, pl.ds(h * HD, HD), :] = (num[:HD] * inv).astype(BF)
        return 0

    lax.fori_loop(0, NT, p1c, 0)
    w_2(1, near)
    w_2(2, near)

    def p2(n, _):
        acc = None
        for g in range(NT):
            part = dot(MX[g], WA[g, pl.ds(QKV, HC), col(n)], 0, 0)
            acc = part if acc is None else acc + part
        MID[:, col(n)] = x_ref[:, col(n)].astype(F32) + (acc + bout_ref[:, col(n)])
        return 0

    lax.fori_loop(0, D // CB, p2, 0)

    def p2b(i, _):
        at = pl.ds(mo(i * 128, 128), 128)
        xh, _inv = norm_stats(MID[at, :])
        n2 = (xh * ln2g_ref[...] + ln2b_ref[...]).astype(BF)
        N2[at, :] = n2
        N2T[:, at] = n2.T
        return 0

    lax.fori_loop(0, T // 128, p2b, 0)
    w_3(1, near)
    w_3(2, near)

    @pl.when(z < NT - 1)
    def _():
        for g in range(NT):
            rcopy(SQ.at[g], SQ.at[g], c_s.at[0, g], c_r.at[0, g], (dp, z)).wait_send()

    UN[...] = jnp.zeros_like(UN)
    GN2[...] = jnp.zeros_like(GN2)
    for copy in local[4:]:
        copy.wait()

    cc = math.sqrt(2.0 / math.pi)

    def p3(j, _):
        g = ff(j)

        @pl.when(j > 0)
        def _():
            w_4(1, g)
            w_4(2, g)

        def units(u, total):
            pre = dot(N2[...], WB[g, :, col(u)]) + BP[g, pl.ds(3, 1), col(u)]
            sq = pre * pre
            t = jnp.tanh(cc * pre * (1.0 + 0.044715 * sq))
            act = (0.5 * pre * (1.0 + t)).astype(BF)
            slope = 0.5 * (1.0 + t) + (0.5 * cc) * pre * (1.0 - t * t) * (1.0 + (3 * 0.044715) * sq)
            ACT[:, col(u)] = act
            ACTT[col(u), :] = act.T
            gact = dot(cot_ref[...], WC[g, col(u), :], 1, 1)
            gpre = (gact * slope).astype(BF)
            GP[:, col(u)] = gpre
            GBF[g, :, col(u)] = jnp.sum(gpre.astype(F32), axis=0, keepdims=True)
            return total

        lax.fori_loop(0, U // CB, units, 0)

        @pl.when(j >= 1)
        def _():
            g_a(1, ff(j - 1))
            g_a(2, ff(j - 1))

        @pl.when(j == 1)
        def _():
            w_3(1, mid)
            w_3(2, mid)

        @pl.when(j == 2)
        def _():
            g_b(1, z)
            g_b(2, z)

        def outs(n, _):
            UN[:, col(n)] += dot(ACT[...], WC[g, :, col(n)])
            GN2[:, col(n)] += dot(GP[...], WB[g, col(n), :], 1, 1)
            return 0

        lax.fori_loop(0, D // CB, outs, 0)

        @pl.when(j == 0)
        def _():
            w_2(1, mid)
            w_2(2, mid)

        def grads(n, _):
            WC[g, col(n), :] = dot(ACTT[col(n), :], cot_ref[...]).astype(BF)
            WB[g, col(n), :] = dot(N2T[col(n), :], GP[...]).astype(BF)
            return 0

        lax.fori_loop(0, D // CB, grads, 0)
        g_core(1, g)
        g_core(2, g)

        return 0

    lax.fori_loop(0, NT, p3, 0)
    g_b(1, far)
    g_b(2, far)

    VS[...] = jnp.zeros_like(VS)

    def p4(i, _):
        at = pl.ds(mo(i * RB_, RB_), RB_)
        mid = MID[at, :]
        res_ref[at, :] = (mid + UN[at, :] + bproj_ref[...]).astype(BF)
        xh, inv = norm_stats(mid)
        gn = GN2[at, :]
        gh = gn * ln2g_ref[...]
        c1 = jnp.mean(gh, axis=-1, keepdims=True)
        c2 = jnp.mean(gh * xh, axis=-1, keepdims=True)
        cot = cot_ref[at, :].astype(F32)
        gm = cot + inv * (gh - c1 - xh * c2)
        GN2[at, :] = gm
        low = gm.astype(BF)
        GML[at, :] = low
        VS[0] += jnp.sum(cot, axis=0, keepdims=True)
        VS[1] += jnp.sum(low.astype(F32), axis=0, keepdims=True)
        VS[2] += jnp.sum(gn * xh, axis=0, keepdims=True)
        VS[3] += jnp.sum(gn, axis=0, keepdims=True)
        return 0

    lax.fori_loop(0, T // RB_, p4, 0)
    g_a(1, near)
    g_a(2, near)

    tail_row = iota((16, T), 0)

    def p5a(g, _):
        gmix = dot(WA[g, pl.ds(QKV, HC), :], GML[...], 1, 1).astype(BF).astype(F32)
        mix = MX[g]
        WA[g, pl.ds(QKV, HC), :] = dot(mix, GML[...]).astype(BF)
        prod = gmix * mix.astype(F32)
        for h in range(HPG):
            hh = g * HPG + h
            rows = slice(h * HD, (h + 1) * HD)
            inv = DI[hh]
            gden = -jnp.sum(prod[rows], axis=0, keepdims=True) * inv
            hi = gden.astype(BF).astype(F32)
            lo = gden - hi
            tail = jnp.where(tail_row == 0, hi, jnp.where(tail_row == 1, lo, 0.0)).astype(BF)
            ga = jnp.concatenate([(gmix[rows] * inv).astype(BF), tail], axis=0)
            GA[hh] = ga
            gc = dot(ga, QF[hh].T)
            GC[hh] = gc
            SQ[g, h] = gc.astype(BF)

        @pl.when(z == NT - 1)
        def _():
            rcopy(SQ.at[g], GR.at[g], c_s.at[1, g], c_r.at[1, g], (dp, z - 1)).start()

        return 0

    lax.fori_loop(0, NT, p5a, 0)

    def chain_back(g, _):
        @pl.when(z < NT - 1)
        def _():
            chain_wait(GR, g, 1)
            for h in range(HPG):
                hh = g * HPG + h
                later = jnp.where(from_next, GR[g, h].astype(F32), 0.0)
                SQ[g, h] = (GC[hh] + later).astype(BF)

        @pl.when(jnp.logical_and(z > 0, z < NT - 1))
        def _():
            rcopy(SQ.at[g], GR.at[g], c_s.at[1, g], c_r.at[1, g], (dp, z - 1)).start()

        return 0

    GN1 = UN
    GN1[...] = jnp.zeros_like(GN1)

    def back(feat, grads):
        out = []
        for b in range(NB):
            bs = slice(b * CB, (b + 1) * CB)
            p = feat[:HD, bs].astype(F32)
            m = feat[HD:, bs].astype(F32)
            g1 = grads[b][:HD]
            g2 = grads[b][HD:]
            s1 = jnp.sum(g1 * p, axis=0, keepdims=True)
            s2 = jnp.sum(g2 * m, axis=0, keepdims=True)
            out.append((p * (g1 - s1) - m * (g2 - s2)).astype(BF))
        return jnp.concatenate(out, axis=1)

    def p5b(t, _):
        g = last(t)
        gql = []
        gkl = []
        for h in range(HPG):
            hh = g * HPG + h
            qf = QF[hh]
            kf = KF[hh]
            va = VA[hh]
            ga = GA[hh]
            kn = kf.T
            vn = va.T
            ctt = CT[hh].T
            gq = [None] * NB
            gk = [None] * NB
            gv = [None] * NB
            for qi in range(NB):
                qs = slice(qi * CB, (qi + 1) * CB)
                gq[qi] = dot(ctt, ga[:, qs])
                for ki in range(qi + 1):
                    ks = slice(ki * CB, (ki + 1) * CB)
                    s = dot(kn[ks], qf[:, qs])
                    gs = dot(vn[ks], ga[:, qs])
                    if ki == qi:
                        s = jnp.where(causal, s, 0.0)
                        gs = jnp.where(causal, gs, 0.0)
                    s = s.astype(BF)
                    gs = gs.astype(BF)
                    gq[qi] = gq[qi] + dot(kf[:, ks], gs)
                    pk = dot(qf[:, qs], gs, 1, 1)
                    pv = dot(ga[:, qs], s, 1, 1)[:HD]
                    gk[ki] = pk if gk[ki] is None else gk[ki] + pk
                    gv[ki] = pv if gv[ki] is None else gv[ki] + pv
            for ki in range(NB):
                ks = slice(ki * CB, (ki + 1) * CB)
                NM[3 * h, :HD, ks] = gk[ki][:HD]
                NM[3 * h + 1, :HD, ks] = gk[ki][HD:]
                NM[3 * h + 2, :HD, ks] = gv[ki]
            gql.append(back(qf, gq))

        @pl.when(t == 0)
        def _():
            lax.fori_loop(0, NT, chain_back, 0)
            for k in (1, 2):
                g_b(k, mid)
                g_y(k, z)
                g_y(k, far)

        @pl.when(t >= 1)
        def _():
            g_a(0, last(t - 1))

        @pl.when(t == 1)
        def _():
            g_b(1, near)
            g_b(2, near)

        @pl.when(t >= 2)
        def _():
            g_b(0, last(t - 2))

        for k in (1, 2):

            @pl.when(t == 2)
            def _():
                z_in(k, far)

            @pl.when(t == 3)
            def _():
                z_in(k, mid)

        @pl.when(t == 3)
        def _():
            g_y(0, far)
            z_out(0, far)

        for h in range(HPG):
            hh = g * HPG + h
            kf = KF[hh]
            va = VA[hh]
            gkc = jnp.where(from_next, GR[g, h], jnp.zeros((AUG, 2 * HD), BF))
            gkt = gkc.T
            gk = [None] * NB
            for ki in range(NB):
                ks = slice(ki * CB, (ki + 1) * CB)
                gk[ki] = jnp.concatenate([NM[3 * h, :HD, ks], NM[3 * h + 1, :HD, ks]], axis=0) + dot(gkt, va[:, ks])
                gv = NM[3 * h + 2, :HD, ks] + dot(gkc[:HD], kf[:, ks])
                GQ[pl.ds(2 * HC + h * HD, HD), ks] = gv.astype(BF)
            gkl.append(back(kf, gk))

        comp = None
        for which, parts in ((0, gql), (1, gkl)):
            glog = jnp.concatenate(parts, axis=0)
            own = QK[g, pl.ds(which * HC, HC), :]
            GQ[pl.ds(which * HC, HC), :] = dot(block_diag(g, which), glog).astype(BF)
            gfeat = jnp.where(head_mask, dot(own, glog, 1, 1), 0.0).astype(BF)
            part = dot(gfeat, pick_back(which))
            comp = part if comp is None else comp + part
        comp = comp.astype(BF)
        gq_all = GQ[...]
        gqn = gq_all[:QKV].T
        for n in range(D // CB):
            GN1[:, n * CB : (n + 1) * CB] += dot(gqn, WA[g, pl.ds(0, QKV), n * CB : (n + 1) * CB])
        WA[g, pl.ds(0, QKV), :] = dot(gq_all[:QKV], N1[...]).astype(BF)
        for b in range(HC // 32):
            WA[g, pl.ds(D, 32), b * 128 : (b + 1) * 128] = comp[b * 32 : (b + 1) * 32]
        vec = dot(ones_rows, gq_all, 1, 1)
        row = iota((16, D), 0)
        vec = jnp.where(row == 1, GBF[g], vec)
        for i in range(4):
            vec = jnp.where(row == 2 + i, VS[i], vec)
        WA[g, pl.ds(D + 32, 16), :] = vec.astype(BF)
        g_core(0, g)

        for k in (1, 2):

            @pl.when(t == 0)
            def _():
                z_out(k, far)

            @pl.when(t == 1)
            def _():
                g_y(k, mid)
                z_out(k, mid)

            @pl.when(t == 2)
            def _():
                g_y(k, near)
                z_out(k, near)

            @pl.when(t == 3)
            def _():
                z_in(k, near)

        return 0

    lax.fori_loop(0, NT, p5b, 0)

    LS[...] = jnp.zeros_like(LS)

    def p6(i, _):
        at = pl.ds(mo(i * RB_, RB_), RB_)
        xh, inv = norm_stats(x_ref[at, :].astype(F32))
        gn = GN1[at, :]
        gh = gn * ln1g_ref[...]
        c1 = jnp.mean(gh, axis=-1, keepdims=True)
        c2 = jnp.mean(gh * xh, axis=-1, keepdims=True)
        gin_ref[at, :] = (GN2[at, :] + inv * (gh - c1 - xh * c2)).astype(BF)
        LS[0, 0:1, :] += jnp.sum(gn * xh, axis=0, keepdims=True)
        LS[0, 1:2, :] += jnp.sum(gn, axis=0, keepdims=True)
        return 0

    lax.fori_loop(0, T // RB_, p6, 0)

    partners = [dp + d_core, dp + d_x, dp + d_y] + [high(i) for i in range(nh)]

    steps = len(partners)

    def small_start(i):
        rcopy(LS.at[i], LR.at[i], l_s.at[i], l_r.at[i], (partners[i], z)).start()

    def small_end(i):
        rcopy(LS.at[i], LR.at[i], l_s.at[i], l_r.at[i], (partners[i], z)).wait()
        LS[i + 1] = LS[i] + LR[i]

    small_start(0)
    g_a(0, z)
    g_b(0, near)
    g_y(0, mid)
    z_out(0, mid)
    z_in(0, far)
    small_end(0)
    small_start(1)
    g_b(0, z)
    z_in(0, mid)
    g_y(0, near)
    z_out(0, near)
    z_in(0, near)
    small_end(1)
    small_start(2)
    g_sum(1)
    g_sum(2)
    small_end(2)
    for i in range(3, steps):
        small_start(i)
        small_end(i)
    LZ[z] = LS[steps]
    for o in range(1, NT):
        rcopy(LS.at[steps], LZ.at[z], lz_s.at[o - 1], lz_r.at[z], (dp, lax.rem(z + o, NT))).start()
    o_2(1)
    o_2(2)
    g_y(0, z)
    g_sum(0)
    o_3(1)
    o_3(2)
    o_2(0)
    o_4(1)
    outs = [*out_ff(1, MID, 0, ob_ref, 0)]
    o_4(2)
    outs += [*out_ff(2, UN, 1, oc_ref, 2)]
    for o in range(1, NT):
        zz = lax.rem(z + o, NT)
        rcopy(LZ.at[zz], LZ.at[zz], lz_s.at[o - 1], lz_r.at[zz], (dp, z)).wait_recv()
    total = LZ[0]
    for zz in range(1, NT):
        total = total + LZ[zz]
    gln1g_ref[...] = total[0:1].reshape(D)
    gln1b_ref[...] = total[1:2].reshape(D)
    o_3(0)
    o_4(0)
    widen(OA, 0, WO, 0, QKV)
    outs.append(write(WO.at[pl.ds(0, QKV), :], oa_ref, own_s.at[4]))
    widen(OA, QKV, WO, QKV, HC)
    outs.append(write(WO.at[pl.ds(QKV, HC), :], oo_ref, own_s.at[5]))
    for b in range(HC // 32):
        block = OA[D : D + 32, b * 128 : (b + 1) * 128].astype(F32)
        rows = slice(b % 2 * 32, b % 2 * 32 + 32)
        gfq_ref[b // 2, rows, :] = block[:, :HD]
        gfk_ref[b // 2, rows, :] = block[:, HD:]
    vec = OA[D + 32 : D + 48, :].astype(F32)
    for i in range(3):
        gbqkv_ref[i : i + 1, :] = vec[0:1, i * HC : (i + 1) * HC]
    for i, ref in enumerate((gbfc_ref, gbproj_ref, gbout_ref, gln2g_ref, gln2b_ref)):
        ref[...] = vec[i + 1 : i + 2].reshape(D)
    for copy in outs:
        copy.wait()

    for o in range(1, NT):
        rcopy(LS.at[steps], LZ.at[z], lz_s.at[o - 1], lz_r.at[z], (dp, lax.rem(z + o, NT))).wait_send()
    small_done()
    for k in range(KINDS):
        w_z_done(k)
        for g in range(NT):
            g_done(k, g)

    @pl.when(z > 0)
    def _():
        for g in range(NT):
            rcopy(SQ.at[g], SQ.at[g], c_s.at[1, g], c_r.at[1, g], (dp, z)).wait_send()


def layer_call(nh, T, *args):
    def vm(shape, dtype=BF):
        return pltpu.VMEM(shape, dtype)

    dma = pltpu.SemaphoreType.DMA
    nhb = max(nh, 1)
    nst = 3 + nh
    scratch = [
        vm((NT, ROWS_G[0], D)),
        vm((NT, D, U)),
        vm((NT, U, D)),
        vm((NT, HC, 2 * HD)),
        vm((NT, 8, D), F32),
    ]
    scratch += [vm((NT, 4 * r, D)) for r in R_G]
    scratch += [vm((NT, r, D)) for r in R_G]
    scratch += [vm((NT, 2, r, D)) for r in R_G]
    scratch += [vm((NT + 1, r, D)) for r in R_G]
    scratch += [vm((rows, D)) for rows in ROWS_G]
    scratch += [vm((nhb, r if nh else 16, D)) for r in R_G]
    scratch += [vm((nst + 1, 8, D), F32), vm((nst, 8, D), F32), vm((NT, 8, D), F32)]
    scratch += [
        vm((T, D)),
        vm((NT, 2 * HC, T)),
        vm((NH, AUG, T)),
        vm((NH, 2 * HD, T)),
        vm((NH, 2 * HD, T)),
        vm((NH, HD + 8, T), F32),
        vm((NH, AUG, 2 * HD), F32),
        vm((NH, AUG, 2 * HD)),
        vm((NT, HPG, AUG, 2 * HD)),
        vm((NT, HPG, AUG, 2 * HD)),
        vm((NT, HPG, AUG, 2 * HD)),
        vm((NT, HC, T)),
        vm((NH, 1, T), F32),
        vm((T, D), F32),
        vm((T, D)),
        vm((D, T)),
        vm((T, D), F32),
        vm((T, D), F32),
        vm((T, D)),
        vm((T, U)),
        vm((U, T)),
        vm((T, U)),
        vm((NT, 1, U), F32),
        vm((NH, AUG, T)),
        vm((NH, AUG, 2 * HD), F32),
        vm((D, T)),
        vm((4, 1, D), F32),
        vm((6, 1, D), F32),
        vm((HC, 2 * HD)),
        vm((8, D), F32),
        vm((D, D), F32),
    ]
    scratch += [
        dma((6,)),
        dma((2, NT - 1)),
        dma((2, NT)),
        dma((KINDS, 2)),
        dma((6, KINDS, NT)),
        dma((6, KINDS, NT)),
        dma((6, KINDS, NT)),
        dma((5, KINDS, NT)),
        dma((KINDS, NT + 1)),
        dma((5, KINDS)),
        dma((5, KINDS)),
        dma((nhb, KINDS)),
        dma((nhb, KINDS)),
        dma((nst,)),
        dma((nst,)),
        dma((NT - 1,)),
        dma((NT,)),
        dma((2, NT)),
        dma((2, NT)),
    ]
    vmem = pl.BlockSpec(memory_space=pltpu.VMEM)
    hbm = pl.BlockSpec(memory_space=pl.ANY)
    return pl.pallas_call(
        functools.partial(layer_kernel, nh),
        out_shape=(
            jax.ShapeDtypeStruct((T, D), BF),
            jax.ShapeDtypeStruct((T, D), BF),
            jax.ShapeDtypeStruct((QKV, D), F32),
            jax.ShapeDtypeStruct((HC, D), F32),
            jax.ShapeDtypeStruct((D, U), F32),
            jax.ShapeDtypeStruct((U, D), F32),
            jax.ShapeDtypeStruct((HPG, HD, HD), F32),
            jax.ShapeDtypeStruct((HPG, HD, HD), F32),
            jax.ShapeDtypeStruct((3, HC), F32),
            *[jax.ShapeDtypeStruct((D,), F32)] * 7,
        ),
        in_specs=[pl.BlockSpec(memory_space=pltpu.SMEM)] + [vmem] * 12 + [hbm] * 4,
        out_specs=(vmem, vmem, hbm, hbm, hbm, hbm, *[vmem] * 10),
        scratch_shapes=scratch,
        compiler_params=pltpu.CompilerParams(
            collective_id=0, has_side_effects=True, vmem_limit_bytes=67043328
        ),
    )(*args)


def hand_over(arrays):
    n = len(arrays)

    def body(*refs):
        sems = refs[3 * n]

        def move(a, b, i):
            return pltpu.make_async_copy(refs[a * n + i], refs[b * n + i], sems.at[b % 2, i])

        for i in range(n):
            move(0, 2, i).start()
        for i in range(n):
            move(0, 2, i).wait()
            move(2, 1, i).start()
        for i in range(n):
            move(2, 1, i).wait()

    hbm = pl.BlockSpec(memory_space=pl.ANY)
    return pl.pallas_call(
        body,
        out_shape=tuple(jax.ShapeDtypeStruct(a.shape, a.dtype) for a in arrays),
        in_specs=[hbm] * len(arrays),
        out_specs=(hbm,) * len(arrays),
        scratch_shapes=[*[pltpu.VMEM(a.shape, a.dtype) for a in arrays], pltpu.SemaphoreType.DMA((2, n))],
    )(*arrays)


def local(
    nh,
    tokens_in,
    ln1_gain,
    ln1_bias,
    w_qkv,
    b_qkv,
    feat_q,
    feat_k,
    w_out,
    b_out,
    ln2_gain,
    ln2_bias,
    w_fc,
    b_fc,
    w_proj,
    b_proj,
    seq_lengths,
    cotangent,
):
    T = tokens_in.shape[0]
    w_qkv_t = jnp.transpose(w_qkv, (1, 2, 0)).reshape(QKV, D)
    out = layer_call(
        nh,
        T,
        seq_lengths,
        tokens_in,
        cotangent,
        ln1_gain,
        ln1_bias,
        b_out,
        ln2_gain,
        ln2_bias,
        b_proj,
        b_fc,
        b_qkv,
        feat_q,
        feat_k,
        w_qkv_t,
        w_out,
        w_fc,
        w_proj,
    )
    res, gin, g_w_qkv, g_w_out, g_w_fc, g_w_proj, g_fq, g_fk, g_bqkv, g_bfc, g_bproj, g_bout, *g_ln = hand_over(out)
    g_w_qkv = jnp.transpose(g_w_qkv.reshape(3, HC, D), (2, 0, 1))
    g_ln2g, g_ln2b, g_ln1g, g_ln1b = g_ln
    return (
        res,
        gin,
        g_ln1g,
        g_ln1b,
        g_w_qkv,
        g_bqkv,
        g_fq,
        g_fk,
        g_w_out,
        g_bout,
        g_ln2g,
        g_ln2b,
        g_w_fc,
        g_bfc,
        g_w_proj,
        g_bproj,
    )


def solution(mesh):
    n_dp = mesh.shape["dp"]
    nh = max(0, (n_dp // 8).bit_length() - 1)
    return jax.shard_map(
        functools.partial(local, nh),
        mesh=mesh,
        in_specs=(
            P(("dp", "tensor"), None),
            P(),
            P(),
            P(None, None, "tensor"),
            P(None, "tensor"),
            P("tensor", None, None),
            P("tensor", None, None),
            P("tensor", None),
            P(),
            P(),
            P(),
            P(None, "tensor"),
            P("tensor"),
            P("tensor", None),
            P(),
            P("dp", None),
            P(("dp", "tensor"), None),
        ),
        out_specs=(
            P(("dp", "tensor"), None),
            P(("dp", "tensor"), None),
            P(),
            P(),
            P(None, None, "tensor"),
            P(None, "tensor"),
            P("tensor", None, None),
            P("tensor", None, None),
            P("tensor", None),
            P(),
            P(),
            P(),
            P(None, "tensor"),
            P("tensor"),
            P("tensor", None),
            P(),
        ),
        check_vma=False,
    )
```

```python
import functools
import math

import jax
import jax.numpy as jnp
from jax import lax
from jax.experimental import pallas as pl
from jax.experimental.pallas import tpu as pltpu
from jax.sharding import PartitionSpec as P

NORM_EPS = 1e-05
BF = jnp.bfloat16
F32 = jnp.float32
MESH = pl.DeviceIdType.MESH
NT = 4
D = 768
HD = 64
HPG = 3
HC = HPG * HD
NH = NT * HPG
U = 768
AUG = 80
QKV = 3 * HC
KINDS = 3
R_W = 96
R_G = (112, 96, 96)
ROWS_G = (896, 768, 768)
CB = 256
HALF_W = (48, 48)
HALF_G = ((64, 48), (48, 48), (48, 48))


def dot(a, b, ca=1, cb=0):
    return lax.dot_general(a, b, (((ca,), (cb,)), ((), ())), preferred_element_type=F32)


def mo(value, multiple):
    return pl.multiple_of(value, multiple)


def soft_pair(logits):
    top = jnp.max(logits, axis=0, keepdims=True)
    low = jnp.min(logits, axis=0, keepdims=True)
    e_pos = jnp.exp(logits - top)
    e_neg = jnp.exp(low - logits)
    p = e_pos * (1.0 / jnp.sum(e_pos, axis=0, keepdims=True))
    m = e_neg * (1.0 / jnp.sum(e_neg, axis=0, keepdims=True))
    return jnp.concatenate([p, m], axis=0)


def norm_stats(rows):
    mean = jnp.mean(rows, axis=-1, keepdims=True)
    centred = rows - mean
    var = jnp.mean(centred * centred, axis=-1, keepdims=True)
    inv = lax.rsqrt(var + NORM_EPS)
    return centred * inv, inv


def col(n):
    return pl.ds(mo(n * CB, CB), CB)


def layer_kernel(
    nh,
    seq_ref,
    x_ref,
    cot_ref,
    ln1g_in,
    ln1b_in,
    bout_in,
    ln2g_in,
    ln2b_in,
    bproj_in,
    bfc_in,
    bqkv_in,
    fq_in,
    fk_in,
    a_own,
    a_out,
    b_own,
    c_own,
    res_ref,
    gin_ref,
    oa_ref,
    oo_ref,
    ob_ref,
    oc_ref,
    gfq_ref,
    gfk_ref,
    gbqkv_ref,
    gbfc_ref,
    gbproj_ref,
    gbout_ref,
    gln2g_ref,
    gln2b_ref,
    gln1g_ref,
    gln1b_ref,
    WA,
    WB,
    WC,
    FT,
    BP,
    R0A,
    R0B,
    R0C,
    RAA,
    RAB,
    RAC,
    RBA,
    RBB,
    RBC,
    ZRA,
    ZRB,
    ZRC,
    OA,
    OB,
    OC,
    RHA,
    RHB,
    RHC,
    LS,
    LR,
    LZ,
    N1,
    QK,
    VA,
    QF,
    KF,
    NM,
    ST,
    CT,
    CR,
    SQ,
    GR,
    MX,
    DI,
    MID,
    N2,
    N2T,
    UN,
    GN2,
    GML,
    ACT,
    ACTT,
    GP,
    GBF,
    GA,
    GC,
    GQ,
    VS,
    PV,
    ft_own,
    bp_own,
    own_s,
    sm_s,
    sm_r,
    wz_s,
    w_s,
    w_r,
    g_s,
    g_r,
    z_r,
    o_s,
    o_r,
    h_s,
    h_r,
    l_s,
    l_r,
    lz_s,
    lz_r,
    c_s,
    c_r,
):
    dp = lax.axis_index("dp")
    z = lax.axis_index("tensor")
    T = x_ref.shape[0]
    NB = T // CB
    core = lax.rem(dp, 2)
    bx = lax.rem(dp // 2, 2)
    by = lax.rem(dp // 4, 2)
    d_core = 1 - 2 * core
    d_x = 2 * (1 - 2 * bx)
    d_y = 4 * (1 - 2 * by)
    slot = core * 4 + by * 2 + bx

    W = (WA, WB, WC)
    OWN = (a_own, b_own, c_own)
    R0 = (R0A, R0B, R0C)
    RA = (RAA, RAB, RAC)
    RB = (RBA, RBB, RBC)
    ZR = (ZRA, ZRB, ZRC)
    O = (OA, OB, OC)
    RH = (RHA, RHB, RHC)

    near = z + 1 - 2 * lax.rem(z, 2)
    mid = 2 - z // 2
    far = 3 * (1 - z // 2)
    is_outer = jnp.logical_or(z == 0, z == NT - 1)
    is_inner = jnp.logical_and(z > 0, z < NT - 1)

    def choose(j, groups):
        out = groups[-1]
        for i in range(NT - 2, -1, -1):
            out = jnp.where(j == i, groups[i], out)
        return out

    def wo(j):
        return choose(j, (z, near, mid, far))

    def ff(j):
        return choose(j, (z, far, mid, near))

    def last(t):
        return choose(t, (far, mid, near, z))

    def high(i):
        step = 8 * 2**i
        return dp + step * (1 - 2 * lax.rem(dp // step, 2))

    def rcopy(src, dst, ssem, rsem, dev):
        return pltpu.make_async_remote_copy(
            src_ref=src, dst_ref=dst, send_sem=ssem, recv_sem=rsem, device_id=dev, device_id_type=MESH
        )

    dev_x = (dp + d_x, z)
    dev_y = (dp + d_y, z)
    dev_c = (dp + d_core, z)
    slot_x = core * 4 + by * 2 + (1 - bx)
    slot_y = core * 4 + (1 - by) * 2 + bx
    slot_d = core * 4 + (1 - by) * 2 + (1 - bx)

    for i, ref in enumerate((ln1g_in, ln1b_in, bout_in, ln2g_in, ln2b_in, bproj_in)):
        PV[i] = ref[...].reshape(1, D)
    ln1g_ref, ln1b_ref, bout_ref, ln2g_ref, ln2b_ref, bproj_ref = (PV.at[i] for i in range(6))
    bp_own[...] = jnp.zeros_like(bp_own)
    bp_own[0:3, 0:HC] = bqkv_in[...]
    bp_own[3:4, :] = bfc_in[...].reshape(1, D)
    for h in range(HPG):
        ft_own[h * HD : (h + 1) * HD, :] = jnp.concatenate([fq_in[h], fk_in[h]], axis=1)

    peers = [(dp + d_core, z), (dp + d_x, z), (dp + d_y, z)]
    peers += [(high(i), z) for i in range(nh)]
    peers += [(dp, lax.rem(z + o, NT)) for o in range(1, NT)]
    barrier = pltpu.get_barrier_semaphore()
    for peer in peers:
        pl.semaphore_signal(barrier, inc=1, device_id=peer, device_id_type=MESH)
    pl.semaphore_wait(barrier, len(peers))

    def wrows(k, g, s):
        return W[k].at[g, pl.ds(mo(s * R_W, R_W), R_W), :]

    def wrows4(k, g, c):
        return W[k].at[g, pl.ds(mo(c * 4 * R_W, R_W), 4 * R_W), :]

    def whalf(k, g, s, h):
        return W[k].at[g, pl.ds(mo(s * R_W + h * HALF_W[0], 16), HALF_W[h]), :]

    def z_next(g):
        return jnp.where(g < z, z + 1, z - 1)

    def own_rows(k):
        at = pl.ds(mo(slot * R_W, R_W), R_W)
        if k:
            return ((slot >= 0, OWN[k].at[at, :]),)
        split = QKV // R_W
        low = jnp.where(slot < split, slot, 0)
        high = jnp.where(slot < split, 0, slot - split)
        return (
            (slot < split, a_own.at[pl.ds(mo(low * R_W, R_W), R_W), :]),
            (slot >= split, a_out.at[pl.ds(mo(high * R_W, R_W), R_W), :]),
        )

    def w_z(k):
        for here, src in own_rows(k):

            @pl.when(jnp.logical_and(here, z < NT - 1))
            def _():
                rcopy(src, wrows(k, z, slot), wz_s.at[k, 0], w_r.at[0, k, z], (dp, z + 1)).start()

            @pl.when(jnp.logical_and(here, z > 0))
            def _():
                rcopy(src, wrows(k, z, slot), wz_s.at[k, 1], w_r.at[0, k, z], (dp, z - 1)).start()

    def w_wait(k, g, stage, ref):
        rcopy(ref, ref, w_s.at[0, k, g], w_r.at[stage, k, g], dev_c).wait_recv()

    def w_send(k, g, s_stage, r_stage, ref, dev):
        rcopy(ref, ref, w_s.at[s_stage, k, g], w_r.at[r_stage, k, g], dev).start()

    def w_0(k, g):
        mine = wrows(k, g, slot)
        w_wait(k, g, 0, mine)

        @pl.when(is_inner)
        def _():
            w_send(k, g, 5, 0, mine, (dp, z_next(g)))

    def w_1(k, g):
        mine = wrows(k, g, slot)
        w_send(k, g, 0, 1, mine, dev_x)
        w_send(k, g, 1, 2, mine, dev_y)

    def w_2(k, g):
        w_wait(k, g, 1, wrows(k, g, slot_x))
        w_send(k, g, 2, 3, whalf(k, g, slot_x, 0), dev_y)
        w_wait(k, g, 2, wrows(k, g, slot_y))
        w_send(k, g, 3, 4, whalf(k, g, slot_y, 1), dev_x)

    def w_3(k, g):
        w_wait(k, g, 3, whalf(k, g, slot_d, 0))
        w_wait(k, g, 4, whalf(k, g, slot_d, 1))
        w_send(k, g, 4, 5, wrows4(k, g, core), dev_c)

    def w_4(k, g):
        w_wait(k, g, 5, wrows4(k, g, 1 - core))
        sent = [wrows(k, g, slot)] * 2 + [whalf(k, g, slot_x, 0), whalf(k, g, slot_y, 1), wrows4(k, g, core)]
        for st, ref in enumerate(sent):
            rcopy(ref, ref, w_s.at[st, k, g], w_r.at[0, k, g], dev_c).wait_send()

        @pl.when(is_inner)
        def _():
            mine = wrows(k, g, slot)
            rcopy(mine, mine, w_s.at[5, k, g], w_r.at[0, k, g], dev_c).wait_send()

    def w_z_done(k):
        src = own_rows(k)[0][1]

        @pl.when(z < NT - 1)
        def _():
            rcopy(src, wrows(k, z, slot), wz_s.at[k, 0], w_r.at[0, k, z], (dp, z + 1)).wait_send()

        @pl.when(z > 0)
        def _():
            rcopy(src, wrows(k, z, slot), wz_s.at[k, 1], w_r.at[0, k, z], (dp, z - 1)).wait_send()

    small = ((ft_own, FT), (bp_own, BP))

    def small_send():
        for i, (own, buf) in enumerate(small):
            for o in range(1, NT):
                rcopy(own, buf.at[z], sm_s.at[i, o - 1], sm_r.at[i, z], (dp, lax.rem(z + o, NT))).start()

    def small_wait(g):
        for i, (own, buf) in enumerate(small):
            rcopy(own, buf.at[g], sm_s.at[i, 0], sm_r.at[i, g], (dp, z)).wait_recv()

    def small_done():
        for i, (own, buf) in enumerate(small):
            for o in range(1, NT):
                rcopy(own, buf.at[z], sm_s.at[i, o - 1], sm_r.at[i, z], (dp, lax.rem(z + o, NT))).wait_send()

    local = [
        pltpu.make_async_copy(ft_own, FT.at[z], own_s.at[0]),
        pltpu.make_async_copy(bp_own, BP.at[z], own_s.at[1]),
        pltpu.make_async_copy(a_own, WA.at[z, pl.ds(0, QKV), :], own_s.at[2]),
        pltpu.make_async_copy(a_out, WA.at[z, pl.ds(QKV, HC), :], own_s.at[5]),
        pltpu.make_async_copy(b_own, WB.at[z], own_s.at[3]),
        pltpu.make_async_copy(c_own, WC.at[z], own_s.at[4]),
    ]
    small_send()
    w_z(0)

    @pl.when(is_outer)
    def _():
        w_z(1)
        w_z(2)

    for copy in local:
        copy.start()

    def grows(k, g, s, n=1):
        return W[k].at[g, pl.ds(mo(s * R_G[k], 16), n * R_G[k]), :]

    def add_rows(dst, start, src, n):
        blk = 16 if n % 32 else 32

        def body(i, _):
            at = pl.ds(mo(start + i * blk, 16), blk)
            dst[at, :] = (dst[at, :].astype(F32) + src[pl.ds(mo(i * blk, 16), blk), :].astype(F32)).astype(BF)
            return 0

        lax.fori_loop(0, n // blk, body, 0)

    def ghalf(k, g, s, h):
        return W[k].at[g, pl.ds(mo(s * R_G[k] + h * HALF_G[k][0], 16), HALF_G[k][h]), :]

    def ra(k, g, h):
        return RA[k].at[g, pl.ds(h * HALF_G[k][0], HALF_G[k][h]), :]

    def g_wait(k, g, stage, ref):
        rcopy(ref, ref, g_s.at[0, k, g], g_r.at[stage, k, g], dev_c).wait_recv()

    def g_send(k, g, stage, src, dst, dev):
        rcopy(src, dst, g_s.at[stage, k, g], g_r.at[stage, k, g], dev).start()

    def g_core(k, g):
        g_send(k, g, 0, grows(k, g, (1 - core) * 4, 4), R0[k].at[g], dev_c)

    def g_a(k, g):
        g_wait(k, g, 0, R0[k].at[g])
        add_rows(W[k].at[g], core * 4 * R_G[k], R0[k].at[g], 4 * R_G[k])
        g_send(k, g, 1, ghalf(k, g, slot_d, 0), ra(k, g, 0), dev_x)
        g_send(k, g, 2, ghalf(k, g, slot_d, 1), ra(k, g, 1), dev_y)

    def g_b(k, g):
        g_wait(k, g, 1, ra(k, g, 0))
        add_rows(W[k].at[g], slot_y * R_G[k], ra(k, g, 0), HALF_G[k][0])
        g_send(k, g, 4, grows(k, g, slot_y), RB[k].at[g, 1], dev_y)
        g_wait(k, g, 2, ra(k, g, 1))
        add_rows(W[k].at[g], slot_x * R_G[k] + HALF_G[k][0], ra(k, g, 1), HALF_G[k][1])
        g_send(k, g, 3, grows(k, g, slot_x), RB[k].at[g, 0], dev_x)

    def g_y(k, g):
        for i in range(2):
            g_wait(k, g, 3 + i, RB[k].at[g, i])
            add_rows(W[k].at[g], slot * R_G[k], RB[k].at[g, i], R_G[k])

    def z_send(k, g):
        @pl.when(z < g)
        def _():
            rcopy(grows(k, g, slot), ZR[k].at[g], g_s.at[5, k, g], z_r.at[k, g], (dp, z + 1)).start()

        @pl.when(z > g)
        def _():
            at = jnp.where(z - 1 == g, NT, g)
            rcopy(grows(k, g, slot), ZR[k].at[at], g_s.at[5, k, g], z_r.at[k, at], (dp, z - 1)).start()

    def z_add(k, g, at):
        ref = ZR[k].at[at]
        rcopy(ref, ref, g_s.at[0, k, 0], z_r.at[k, at], dev_c).wait_recv()
        add_rows(W[k].at[g], slot * R_G[k], ref, R_G[k])

    def z_out(k, g):
        @pl.when(is_outer)
        def _():
            z_send(k, g)

    def z_in(k, g):
        @pl.when(is_inner)
        def _():
            z_add(k, g, g)
            z_send(k, g)

    def g_done(k, g):
        one = grows(k, g, 0)
        sent = [grows(k, g, 0, 4), ghalf(k, g, 0, 0), ghalf(k, g, 0, 1), one, one]
        for st, ref in enumerate(sent):
            rcopy(ref, ref, g_s.at[st, k, g], g_r.at[0, k, g], dev_c).wait_send()

        @pl.when(g != z)
        def _():
            rcopy(one, one, g_s.at[5, k, g], g_r.at[0, k, g], dev_c).wait_send()

    def orows(k, s, n=1):
        return O[k].at[pl.ds(mo(s * R_G[k], 16), n * R_G[k]), :]

    def ohalf(k, s, h):
        return O[k].at[pl.ds(mo(s * R_G[k] + h * HALF_G[k][0], 16), HALF_G[k][h]), :]

    def o_wait(k, stage, ref):
        rcopy(ref, ref, o_s.at[stage, k], o_r.at[stage, k], dev_c).wait_recv()

    def o_send(k, stage, ref, dev):
        rcopy(ref, ref, o_s.at[stage, k], o_r.at[stage, k], dev).start()

    def g_sum(k):
        @pl.when(z > 0)
        def _():
            z_add(k, z, z)

        @pl.when(z < NT - 1)
        def _():
            z_add(k, z, NT)

        O[k][pl.ds(mo(slot * R_G[k], 16), R_G[k]), :] = W[k][z, pl.ds(mo(slot * R_G[k], 16), R_G[k]), :]
        for i in range(nh):
            rcopy(orows(k, slot), RH[k].at[i], h_s.at[i, k], h_r.at[i, k], (high(i), z)).start()
            rcopy(orows(k, slot), RH[k].at[i], h_s.at[i, k], h_r.at[i, k], (high(i), z)).wait()
            add_rows(O[k], slot * R_G[k], RH[k].at[i], R_G[k])
        o_send(k, 0, orows(k, slot), dev_x)
        o_send(k, 1, orows(k, slot), dev_y)

    def o_2(k):
        o_wait(k, 0, orows(k, slot_x))
        o_send(k, 2, ohalf(k, slot_x, 0), dev_y)
        o_wait(k, 1, orows(k, slot_y))
        o_send(k, 3, ohalf(k, slot_y, 1), dev_x)
        for i, s in enumerate((slot, slot_x, slot_y)):
            o_send(k, 4 + i, orows(k, s), dev_c)

    def o_3(k):
        o_wait(k, 2, ohalf(k, slot_d, 0))
        o_wait(k, 3, ohalf(k, slot_d, 1))
        o_send(k, 7, orows(k, slot_d), dev_c)

    def o_4(k):
        slots = (slot, slot_x, slot_y, slot_d)
        for i, s in enumerate(slots):
            o_wait(k, 4 + i, orows(k, s + (1 - 2 * core) * 4))
        sent = [orows(k, slot)] * 2 + [ohalf(k, slot_x, 0), ohalf(k, slot_y, 1)] + [orows(k, s) for s in slots]
        for st, ref in enumerate(sent):
            rcopy(ref, ref, o_s.at[st, k], o_r.at[0, k], dev_c).wait_send()

    def write(src, dst, sem):
        copy = pltpu.make_async_copy(src, dst, sem)
        copy.start()
        return copy

    def iota(shape, axis):
        return lax.broadcasted_iota(jnp.int32, shape, axis)

    causal = iota((CB, CB), 0) <= iota((CB, CB), 1)
    aug_tail = jnp.where(iota((16, T), 0) < 2, 1.0, 0.0).astype(BF)
    ones_rows = jnp.ones((16, T), BF)
    head_mask = (iota((HC, HC), 0) // HD) == (iota((HC, HC), 1) // HD)

    def pick(which):
        r = iota((2 * HD, HC), 0) - which * HD
        return (r == lax.rem(iota((2 * HD, HC), 1), HD)).astype(BF)

    def pick_back(which):
        r = iota((HC, 2 * HD), 1) - which * HD
        return (r == lax.rem(iota((HC, 2 * HD), 0), HD)).astype(BF)

    def block_diag(g, which):
        return jnp.where(head_mask, dot(FT[g], pick(which)), 0.0).astype(BF)

    first_end = seq_ref[0, 0]
    second_end = seq_ref[0, 0] + seq_ref[0, 1]

    def seq_id(zz):
        start = zz * T
        return (start >= first_end).astype(jnp.int32) + (start >= second_end).astype(jnp.int32)

    from_prev = jnp.logical_and(z > 0, seq_id(z) == seq_id(z - 1))
    from_next = jnp.logical_and(z < NT - 1, seq_id(z) == seq_id(z + 1))

    RB_ = 64

    def p0(i, _):
        at = pl.ds(mo(i * RB_, RB_), RB_)
        xh, _inv = norm_stats(x_ref[at, :].astype(F32))
        N1[at, :] = (xh * ln1g_ref[...] + ln1b_ref[...]).astype(BF)
        return 0

    lax.fori_loop(0, T // RB_, p0, 0)
    for g in range(NT):
        WA[g, pl.ds(D, ROWS_G[0] - D), :] = jnp.zeros((ROWS_G[0] - D, D), BF)
    GQ[pl.ds(QKV, D - QKV), :] = jnp.zeros((D - QKV, T), BF)

    @pl.when(z == 0)
    def _():
        CR[...] = jnp.zeros_like(CR)

    @pl.when(z == NT - 1)
    def _():
        GR[...] = jnp.zeros_like(GR)

    for copy in local[:4]:
        copy.wait()

    def chain_wait(buf, g, stage):
        rcopy(buf.at[g], buf.at[g], c_s.at[stage, g], c_r.at[stage, g], (dp, z)).wait_recv()

    def chain_send(g):
        rcopy(SQ.at[g], CR.at[g], c_s.at[0, g], c_r.at[0, g], (dp, z + 1)).start()

    def chain_pass(g):
        chain_wait(CR, g, 0)
        for h in range(HPG):
            carried = jnp.where(from_prev, CR[g, h].astype(F32), 0.0)
            SQ[g, h] = (ST[g * HPG + h] + carried).astype(BF)
        chain_send(g)

    def p1(j, _):
        g = wo(j)

        @pl.when(j == 1)
        def _():
            w_0(0, near)
            w_1(0, near)
            small_wait(near)

            @pl.when(is_inner)
            def _():
                w_0(0, mid)
                w_1(0, mid)
                w_0(1, near)
                w_2(0, near)
                w_0(0, far)
                w_1(0, far)
                w_0(2, near)
                w_0(1, far)
                w_2(0, mid)
                w_3(0, near)

            @pl.when(is_outer)
            def _():
                w_2(0, near)
                w_0(0, mid)
                w_1(0, mid)
                w_3(0, near)
                w_0(0, far)
                w_1(0, far)

            w_4(0, near)

        @pl.when(j == 2)
        def _():
            small_wait(mid)

            @pl.when(is_inner)
            def _():
                w_0(2, far)
                w_z(1)
                w_z(2)
                w_2(0, far)
                w_3(0, mid)
                w_1(1, far)
                w_1(2, far)

            @pl.when(is_outer)
            def _():
                w_2(0, mid)
                w_0(1, far)
                w_2(0, far)
                w_1(1, far)
                w_3(0, mid)
                w_0(2, far)
                w_1(2, far)

            w_4(0, mid)

        @pl.when(j == 3)
        def _():
            small_wait(far)
            w_3(0, far)

            @pl.when(is_inner)
            def _():
                w_0(1, mid)

            w_4(0, far)

        bias = jnp.transpose(BP[g, :, 0:256])
        bias = jnp.concatenate([bias[:HC, i : i + 1] for i in range(3)], axis=0)
        qkv = (dot(WA[g, pl.ds(0, QKV), :], N1[...], 1, 1) + bias).astype(BF)
        QK[g] = qkv[: 2 * HC]
        ql = dot(block_diag(g, 0), qkv[:HC], 0, 0)
        kl = dot(block_diag(g, 1), qkv[HC : 2 * HC], 0, 0)
        for h in range(HPG):
            hh = g * HPG + h
            rows = slice(h * HD, (h + 1) * HD)
            qf = soft_pair(ql[rows]).astype(BF)
            kf = soft_pair(kl[rows]).astype(BF)
            va = jnp.concatenate([qkv[2 * HC + h * HD : 2 * HC + (h + 1) * HD], aug_tail], axis=0)
            QF[hh] = qf
            KF[hh] = kf
            VA[hh] = va
            kn = kf.T
            ST[hh] = dot(va, kn)
            for qi in range(NB):
                qs = slice(qi * CB, (qi + 1) * CB)
                acc = None
                for ki in range(qi + 1):
                    ks = slice(ki * CB, (ki + 1) * CB)
                    s = dot(kn[ks], qf[:, qs])
                    if ki == qi:
                        s = jnp.where(causal, s, 0.0)
                    part = dot(va[:, ks], s.astype(BF))
                    acc = part if acc is None else acc + part
                NM[hh, :, qs] = acc[: HD + 8]

        @pl.when(z == 0)
        def _():
            for h in range(HPG):
                SQ[g, h] = ST[g * HPG + h].astype(BF)
            chain_send(g)

        for zz, jj, ready in ((1, 1, (0, 1)), (1, 2, (2,)), (2, 2, (1,))):

            @pl.when(jnp.logical_and(z == zz, j == jj))
            def _():
                for gg in ready:
                    chain_pass(gg)

        return 0

    lax.fori_loop(0, NT, p1, 0)
    @pl.when(is_inner)
    def _():
        w_0(2, mid)

    w_2(1, far)

    @pl.when(z == 1)
    def _():
        chain_pass(3)

    @pl.when(z == 2)
    def _():
        chain_pass(0)
        chain_pass(2)

    @pl.when(is_outer)
    def _():
        w_0(1, near)

    w_2(2, far)
    w_1(1, near)

    @pl.when(is_outer)
    def _():
        w_0(2, near)

    w_1(2, near)

    @pl.when(z == 2)
    def _():
        chain_pass(3)

    def p1b(g, _):
        @pl.when(z == NT - 1)
        def _():
            chain_wait(CR, g, 0)

        for h in range(HPG):
            CT[g * HPG + h] = jnp.where(from_prev, CR[g, h], jnp.zeros((AUG, 2 * HD), BF))
        return 0

    lax.fori_loop(0, NT, p1b, 0)

    def p1c(g, _):
        for h in range(HPG):
            hh = g * HPG + h
            num = NM[hh] + dot(CT[hh], QF[hh])[: HD + 8]
            inv = 1.0 / num[HD : HD + 1]
            DI[hh] = inv
            MX[g, pl.ds(h * HD, HD), :] = (num[:HD] * inv).astype(BF)
        return 0

    lax.fori_loop(0, NT, p1c, 0)
    w_3(1, far)
    w_3(2, far)

    def p2(n, _):
        acc = None
        for g in range(NT):
            part = dot(MX[g], WA[g, pl.ds(QKV, HC), col(n)], 0, 0)
            acc = part if acc is None else acc + part
        MID[:, col(n)] = x_ref[:, col(n)].astype(F32) + (acc + bout_ref[:, col(n)])
        return 0

    lax.fori_loop(0, D // CB, p2, 0)

    def p2b(i, _):
        at = pl.ds(mo(i * 128, 128), 128)
        xh, _inv = norm_stats(MID[at, :])
        n2 = (xh * ln2g_ref[...] + ln2b_ref[...]).astype(BF)
        N2[at, :] = n2
        N2T[:, at] = n2.T
        return 0

    lax.fori_loop(0, T // 128, p2b, 0)
    for k in (1, 2):

        @pl.when(is_outer)
        def _():
            w_0(k, mid)

        w_1(k, mid)

    w_2(1, near)
    w_2(2, near)

    @pl.when(z < NT - 1)
    def _():
        for g in range(NT):
            rcopy(SQ.at[g], SQ.at[g], c_s.at[0, g], c_r.at[0, g], (dp, z)).wait_send()

    UN[...] = jnp.zeros_like(UN)
    GN2[...] = jnp.zeros_like(GN2)
    for copy in local[4:]:
        copy.wait()

    cc = math.sqrt(2.0 / math.pi)

    def p3(j, _):
        g = ff(j)

        @pl.when(j > 0)
        def _():
            w_4(1, g)
            w_4(2, g)

        def units(u, total):
            pre = dot(N2[...], WB[g, :, col(u)]) + BP[g, pl.ds(3, 1), col(u)]
            sq = pre * pre
            t = jnp.tanh(cc * pre * (1.0 + 0.044715 * sq))
            act = (0.5 * pre * (1.0 + t)).astype(BF)
            slope = 0.5 * (1.0 + t) + (0.5 * cc) * pre * (1.0 - t * t) * (1.0 + (3 * 0.044715) * sq)
            ACT[:, col(u)] = act
            ACTT[col(u), :] = act.T
            gact = dot(cot_ref[...], WC[g, col(u), :], 1, 1)
            gpre = (gact * slope).astype(BF)
            GP[:, col(u)] = gpre
            GBF[g, :, col(u)] = jnp.sum(gpre.astype(F32), axis=0, keepdims=True)
            return total

        lax.fori_loop(0, U // CB, units, 0)

        @pl.when(j >= 1)
        def _():
            g_a(1, ff(j - 1))
            g_a(2, ff(j - 1))

        @pl.when(j == 1)
        def _():
            w_3(1, near)
            w_3(2, near)
            w_3(1, mid)
            w_3(2, mid)

        @pl.when(j == 2)
        def _():
            g_b(1, z)
            g_b(2, z)

        def outs(n, _):
            UN[:, col(n)] += dot(ACT[...], WC[g, :, col(n)])
            GN2[:, col(n)] += dot(GP[...], WB[g, col(n), :], 1, 1)
            return 0

        lax.fori_loop(0, D // CB, outs, 0)

        @pl.when(j == 0)
        def _():
            w_2(1, mid)
            w_2(2, mid)

        def grads(n, _):
            WC[g, col(n), :] = dot(ACTT[col(n), :], cot_ref[...]).astype(BF)
            WB[g, col(n), :] = dot(N2T[col(n), :], GP[...]).astype(BF)
            return 0

        lax.fori_loop(0, D // CB, grads, 0)
        g_core(1, g)
        g_core(2, g)

        return 0

    lax.fori_loop(0, NT, p3, 0)
    g_b(1, far)
    g_b(2, far)

    VS[...] = jnp.zeros_like(VS)

    def p4(i, _):
        at = pl.ds(mo(i * RB_, RB_), RB_)
        mid = MID[at, :]
        res_ref[at, :] = (mid + UN[at, :] + bproj_ref[...]).astype(BF)
        xh, inv = norm_stats(mid)
        gn = GN2[at, :]
        gh = gn * ln2g_ref[...]
        c1 = jnp.mean(gh, axis=-1, keepdims=True)
        c2 = jnp.mean(gh * xh, axis=-1, keepdims=True)
        cot = cot_ref[at, :].astype(F32)
        gm = cot + inv * (gh - c1 - xh * c2)
        GN2[at, :] = gm
        low = gm.astype(BF)
        GML[at, :] = low
        VS[0] += jnp.sum(cot, axis=0, keepdims=True)
        VS[1] += jnp.sum(low.astype(F32), axis=0, keepdims=True)
        VS[2] += jnp.sum(gn * xh, axis=0, keepdims=True)
        VS[3] += jnp.sum(gn, axis=0, keepdims=True)
        return 0

    lax.fori_loop(0, T // RB_, p4, 0)
    g_a(1, near)
    g_a(2, near)

    tail_row = iota((16, T), 0)

    def p5a(g, _):
        gmix = dot(WA[g, pl.ds(QKV, HC), :], GML[...], 1, 1).astype(BF).astype(F32)
        mix = MX[g]
        WA[g, pl.ds(QKV, HC), :] = dot(mix, GML[...]).astype(BF)
        prod = gmix * mix.astype(F32)
        for h in range(HPG):
            hh = g * HPG + h
            rows = slice(h * HD, (h + 1) * HD)
            inv = DI[hh]
            gden = -jnp.sum(prod[rows], axis=0, keepdims=True) * inv
            hi = gden.astype(BF).astype(F32)
            lo = gden - hi
            tail = jnp.where(tail_row == 0, hi, jnp.where(tail_row == 1, lo, 0.0)).astype(BF)
            ga = jnp.concatenate([(gmix[rows] * inv).astype(BF), tail], axis=0)
            GA[hh] = ga
            gc = dot(ga, QF[hh].T)
            GC[hh] = gc
            SQ[g, h] = gc.astype(BF)

        @pl.when(z == NT - 1)
        def _():
            rcopy(SQ.at[g], GR.at[g], c_s.at[1, g], c_r.at[1, g], (dp, z - 1)).start()

        return 0

    lax.fori_loop(0, NT, p5a, 0)

    def chain_back(g, _):
        @pl.when(z < NT - 1)
        def _():
            chain_wait(GR, g, 1)
            for h in range(HPG):
                hh = g * HPG + h
                later = jnp.where(from_next, GR[g, h].astype(F32), 0.0)
                SQ[g, h] = (GC[hh] + later).astype(BF)

        @pl.when(jnp.logical_and(z > 0, z < NT - 1))
        def _():
            rcopy(SQ.at[g], GR.at[g], c_s.at[1, g], c_r.at[1, g], (dp, z - 1)).start()

        return 0

    GN1 = UN
    GN1[...] = jnp.zeros_like(GN1)

    def back(feat, grads):
        out = []
        for b in range(NB):
            bs = slice(b * CB, (b + 1) * CB)
            p = feat[:HD, bs].astype(F32)
            m = feat[HD:, bs].astype(F32)
            g1 = grads[b][:HD]
            g2 = grads[b][HD:]
            s1 = jnp.sum(g1 * p, axis=0, keepdims=True)
            s2 = jnp.sum(g2 * m, axis=0, keepdims=True)
            out.append((p * (g1 - s1) - m * (g2 - s2)).astype(BF))
        return jnp.concatenate(out, axis=1)

    def p5b(t, _):
        g = last(t)
        gql = []
        gkl = []
        for h in range(HPG):
            hh = g * HPG + h
            qf = QF[hh]
            kf = KF[hh]
            va = VA[hh]
            ga = GA[hh]
            kn = kf.T
            vn = va.T
            ctt = CT[hh].T
            gq = [None] * NB
            gk = [None] * NB
            gv = [None] * NB
            for qi in range(NB):
                qs = slice(qi * CB, (qi + 1) * CB)
                gq[qi] = dot(ctt, ga[:, qs])
                for ki in range(qi + 1):
                    ks = slice(ki * CB, (ki + 1) * CB)
                    s = dot(kn[ks], qf[:, qs])
                    gs = dot(vn[ks], ga[:, qs])
                    if ki == qi:
                        s = jnp.where(causal, s, 0.0)
                        gs = jnp.where(causal, gs, 0.0)
                    s = s.astype(BF)
                    gs = gs.astype(BF)
                    gq[qi] = gq[qi] + dot(kf[:, ks], gs)
                    pk = dot(qf[:, qs], gs, 1, 1)
                    pv = dot(ga[:, qs], s, 1, 1)[:HD]
                    gk[ki] = pk if gk[ki] is None else gk[ki] + pk
                    gv[ki] = pv if gv[ki] is None else gv[ki] + pv
            for ki in range(NB):
                ks = slice(ki * CB, (ki + 1) * CB)
                NM[3 * h, :HD, ks] = gk[ki][:HD]
                NM[3 * h + 1, :HD, ks] = gk[ki][HD:]
                NM[3 * h + 2, :HD, ks] = gv[ki]
            gql.append(back(qf, gq))

        @pl.when(t == 0)
        def _():
            lax.fori_loop(0, NT, chain_back, 0)
            for k in (1, 2):
                g_b(k, mid)
                g_y(k, z)
                g_y(k, far)

        @pl.when(t >= 1)
        def _():
            g_a(0, last(t - 1))

        @pl.when(t == 1)
        def _():
            g_b(1, near)
            g_b(2, near)

        @pl.when(t >= 2)
        def _():
            g_b(0, last(t - 2))

        for k in (1, 2):

            @pl.when(t == 2)
            def _():
                z_in(k, far)

            @pl.when(t == 3)
            def _():
                z_in(k, mid)

        @pl.when(t == 3)
        def _():
            g_y(0, far)
            z_out(0, far)

        for h in range(HPG):
            hh = g * HPG + h
            kf = KF[hh]
            va = VA[hh]
            gkc = jnp.where(from_next, GR[g, h], jnp.zeros((AUG, 2 * HD), BF))
            gkt = gkc.T
            gk = [None] * NB
            for ki in range(NB):
                ks = slice(ki * CB, (ki + 1) * CB)
                gk[ki] = jnp.concatenate([NM[3 * h, :HD, ks], NM[3 * h + 1, :HD, ks]], axis=0) + dot(gkt, va[:, ks])
                gv = NM[3 * h + 2, :HD, ks] + dot(gkc[:HD], kf[:, ks])
                GQ[pl.ds(2 * HC + h * HD, HD), ks] = gv.astype(BF)
            gkl.append(back(kf, gk))

        comp = None
        for which, parts in ((0, gql), (1, gkl)):
            glog = jnp.concatenate(parts, axis=0)
            own = QK[g, pl.ds(which * HC, HC), :]
            GQ[pl.ds(which * HC, HC), :] = dot(block_diag(g, which), glog).astype(BF)
            gfeat = jnp.where(head_mask, dot(own, glog, 1, 1), 0.0).astype(BF)
            part = dot(gfeat, pick_back(which))
            comp = part if comp is None else comp + part
        comp = comp.astype(BF)
        gq_all = GQ[...]
        gqn = gq_all[:QKV].T
        for n in range(D // CB):
            GN1[:, n * CB : (n + 1) * CB] += dot(gqn, WA[g, pl.ds(0, QKV), n * CB : (n + 1) * CB])
        WA[g, pl.ds(0, QKV), :] = dot(gq_all[:QKV], N1[...]).astype(BF)
        for b in range(HC // 32):
            WA[g, pl.ds(D, 32), b * 128 : (b + 1) * 128] = comp[b * 32 : (b + 1) * 32]
        vec = dot(ones_rows, gq_all, 1, 1)
        row = iota((16, D), 0)
        vec = jnp.where(row == 1, GBF[g], vec)
        for i in range(4):
            vec = jnp.where(row == 2 + i, VS[i], vec)
        WA[g, pl.ds(D + 32, 16), :] = vec.astype(BF)
        g_core(0, g)

        for k in (1, 2):

            @pl.when(t == 0)
            def _():
                z_out(k, far)

            @pl.when(t == 1)
            def _():
                g_y(k, mid)
                z_out(k, mid)

            @pl.when(t == 2)
            def _():
                g_y(k, near)
                z_out(k, near)

            @pl.when(t == 3)
            def _():
                z_in(k, near)

        return 0

    lax.fori_loop(0, NT, p5b, 0)

    LS[...] = jnp.zeros_like(LS)

    def p6(i, _):
        at = pl.ds(mo(i * RB_, RB_), RB_)
        xh, inv = norm_stats(x_ref[at, :].astype(F32))
        gn = GN1[at, :]
        gh = gn * ln1g_ref[...]
        c1 = jnp.mean(gh, axis=-1, keepdims=True)
        c2 = jnp.mean(gh * xh, axis=-1, keepdims=True)
        gin_ref[at, :] = (GN2[at, :] + inv * (gh - c1 - xh * c2)).astype(BF)
        LS[0, 0:1, :] += jnp.sum(gn * xh, axis=0, keepdims=True)
        LS[0, 1:2, :] += jnp.sum(gn, axis=0, keepdims=True)
        return 0

    lax.fori_loop(0, T // RB_, p6, 0)

    partners = [dp + d_core, dp + d_x, dp + d_y] + [high(i) for i in range(nh)]

    steps = len(partners)

    def small_start(i):
        rcopy(LS.at[i], LR.at[i], l_s.at[i], l_r.at[i], (partners[i], z)).start()

    def small_end(i):
        rcopy(LS.at[i], LR.at[i], l_s.at[i], l_r.at[i], (partners[i], z)).wait()
        LS[i + 1] = LS[i] + LR[i]

    small_start(0)
    g_a(0, z)
    g_b(0, near)
    g_y(0, mid)
    z_out(0, mid)
    z_in(0, far)
    small_end(0)
    small_start(1)
    g_b(0, z)
    z_in(0, mid)
    g_y(0, near)
    z_out(0, near)
    z_in(0, near)
    small_end(1)
    small_start(2)
    g_sum(1)
    g_sum(2)
    small_end(2)
    for i in range(3, steps):
        small_start(i)
        small_end(i)
    LZ[z] = LS[steps]
    for o in range(1, NT):
        rcopy(LS.at[steps], LZ.at[z], lz_s.at[o - 1], lz_r.at[z], (dp, lax.rem(z + o, NT))).start()
    o_2(1)
    o_2(2)
    g_y(0, z)
    g_sum(0)
    o_3(1)
    o_3(2)
    o_2(0)
    o_4(1)
    outs = [write(OB, ob_ref, own_s.at[0])]
    o_4(2)
    outs.append(write(OC, oc_ref, own_s.at[1]))
    for o in range(1, NT):
        zz = lax.rem(z + o, NT)
        rcopy(LZ.at[zz], LZ.at[zz], lz_s.at[o - 1], lz_r.at[zz], (dp, z)).wait_recv()
    total = LZ[0]
    for zz in range(1, NT):
        total = total + LZ[zz]
    gln1g_ref[...] = total[0:1].reshape(D)
    gln1b_ref[...] = total[1:2].reshape(D)
    o_3(0)
    o_4(0)
    outs.append(write(OA.at[pl.ds(0, QKV), :], oa_ref, own_s.at[4]))
    outs.append(write(OA.at[pl.ds(QKV, HC), :], oo_ref, own_s.at[5]))
    for b in range(HC // 32):
        block = OA[D : D + 32, b * 128 : (b + 1) * 128].astype(F32)
        rows = slice(b % 2 * 32, b % 2 * 32 + 32)
        gfq_ref[b // 2, rows, :] = block[:, :HD]
        gfk_ref[b // 2, rows, :] = block[:, HD:]
    vec = OA[D + 32 : D + 48, :].astype(F32)
    for i in range(3):
        gbqkv_ref[i : i + 1, :] = vec[0:1, i * HC : (i + 1) * HC]
    for i, ref in enumerate((gbfc_ref, gbproj_ref, gbout_ref, gln2g_ref, gln2b_ref)):
        ref[...] = vec[i + 1 : i + 2].reshape(D)
    for copy in outs:
        copy.wait()

    for o in range(1, NT):
        rcopy(LS.at[steps], LZ.at[z], lz_s.at[o - 1], lz_r.at[z], (dp, lax.rem(z + o, NT))).wait_send()
    small_done()
    for k in range(KINDS):
        w_z_done(k)
        for g in range(NT):
            g_done(k, g)

    @pl.when(z > 0)
    def _():
        for g in range(NT):
            rcopy(SQ.at[g], SQ.at[g], c_s.at[1, g], c_r.at[1, g], (dp, z)).wait_send()


def layer_call(nh, T, *args):
    def vm(shape, dtype=BF):
        return pltpu.VMEM(shape, dtype)

    dma = pltpu.SemaphoreType.DMA
    nhb = max(nh, 1)
    nst = 3 + nh
    scratch = [
        vm((NT, ROWS_G[0], D)),
        vm((NT, D, U)),
        vm((NT, U, D)),
        vm((NT, HC, 2 * HD)),
        vm((NT, 8, D), F32),
    ]
    scratch += [vm((NT, 4 * r, D)) for r in R_G]
    scratch += [vm((NT, r, D)) for r in R_G]
    scratch += [vm((NT, 2, r, D)) for r in R_G]
    scratch += [vm((NT + 1, r, D)) for r in R_G]
    scratch += [vm((rows, D)) for rows in ROWS_G]
    scratch += [vm((nhb, r if nh else 16, D)) for r in R_G]
    scratch += [vm((nst + 1, 8, D), F32), vm((nst, 8, D), F32), vm((NT, 8, D), F32)]
    scratch += [
        vm((T, D)),
        vm((NT, 2 * HC, T)),
        vm((NH, AUG, T)),
        vm((NH, 2 * HD, T)),
        vm((NH, 2 * HD, T)),
        vm((NH, HD + 8, T), F32),
        vm((NH, AUG, 2 * HD), F32),
        vm((NH, AUG, 2 * HD)),
        vm((NT, HPG, AUG, 2 * HD)),
        vm((NT, HPG, AUG, 2 * HD)),
        vm((NT, HPG, AUG, 2 * HD)),
        vm((NT, HC, T)),
        vm((NH, 1, T), F32),
        vm((T, D), F32),
        vm((T, D)),
        vm((D, T)),
        vm((T, D), F32),
        vm((T, D), F32),
        vm((T, D)),
        vm((T, U)),
        vm((U, T)),
        vm((T, U)),
        vm((NT, 1, U), F32),
        vm((NH, AUG, T)),
        vm((NH, AUG, 2 * HD), F32),
        vm((D, T)),
        vm((4, 1, D), F32),
        vm((6, 1, D), F32),
        vm((HC, 2 * HD)),
        vm((8, D), F32),
    ]
    scratch += [
        dma((6,)),
        dma((2, NT - 1)),
        dma((2, NT)),
        dma((KINDS, 2)),
        dma((6, KINDS, NT)),
        dma((6, KINDS, NT)),
        dma((6, KINDS, NT)),
        dma((5, KINDS, NT)),
        dma((KINDS, NT + 1)),
        dma((8, KINDS)),
        dma((8, KINDS)),
        dma((nhb, KINDS)),
        dma((nhb, KINDS)),
        dma((nst,)),
        dma((nst,)),
        dma((NT - 1,)),
        dma((NT,)),
        dma((2, NT)),
        dma((2, NT)),
    ]
    vmem = pl.BlockSpec(memory_space=pltpu.VMEM)
    hbm = pl.BlockSpec(memory_space=pl.ANY)
    return pl.pallas_call(
        functools.partial(layer_kernel, nh),
        out_shape=(
            jax.ShapeDtypeStruct((T, D), BF),
            jax.ShapeDtypeStruct((T, D), BF),
            jax.ShapeDtypeStruct((QKV, D), BF),
            jax.ShapeDtypeStruct((HC, D), BF),
            jax.ShapeDtypeStruct((D, U), BF),
            jax.ShapeDtypeStruct((U, D), BF),
            jax.ShapeDtypeStruct((HPG, HD, HD), F32),
            jax.ShapeDtypeStruct((HPG, HD, HD), F32),
            jax.ShapeDtypeStruct((3, HC), F32),
            *[jax.ShapeDtypeStruct((D,), F32)] * 7,
        ),
        in_specs=[pl.BlockSpec(memory_space=pltpu.SMEM)] + [vmem] * 12 + [hbm] * 4,
        out_specs=(vmem, vmem, hbm, hbm, hbm, hbm, *[vmem] * 10),
        scratch_shapes=scratch,
        compiler_params=pltpu.CompilerParams(
            collective_id=0, has_side_effects=True, vmem_limit_bytes=67043328
        ),
    )(*args)


def hand_over(arrays):
    n = len(arrays)
    wide = (2, 3, 4, 5)
    order = (4, 5, *(i for i in range(n) if i not in wide), 2, 3)
    kinds = [F32 if i in wide else a.dtype for i, a in enumerate(arrays)]

    def body(*refs):
        taken, given, low = refs[:n], refs[n : 2 * n], refs[2 * n : 3 * n]
        high = dict(zip(wide, refs[3 * n : 3 * n + len(wide)]))
        sems = refs[3 * n + len(wide)]

        def widen(src, dst):
            def step(i, _):
                at = pl.ds(mo(i * 64, 64), 64)
                dst[at, :] = src[at, :].astype(F32)
                return 0

            lax.fori_loop(0, src.shape[0] // 64, step, 0)

        reads = [pltpu.make_async_copy(taken[i], low[i], sems.at[0, i]) for i in range(n)]
        writes = [pltpu.make_async_copy(high.get(i, low[i]), given[i], sems.at[1, i]) for i in range(n)]
        for i in order:
            reads[i].start()
        for i in order:
            reads[i].wait()
            if i in wide:
                widen(low[i], high[i])
            writes[i].start()
        for i in order:
            writes[i].wait()

    hbm = pl.BlockSpec(memory_space=pl.ANY)
    scratch = [pltpu.VMEM(a.shape, a.dtype) for a in arrays] + [pltpu.VMEM(arrays[i].shape, F32) for i in wide]
    return pl.pallas_call(
        body,
        out_shape=tuple(jax.ShapeDtypeStruct(a.shape, kind) for a, kind in zip(arrays, kinds)),
        in_specs=[hbm] * n,
        out_specs=(hbm,) * n,
        scratch_shapes=[*scratch, pltpu.SemaphoreType.DMA((2, n))],
    )(*arrays)


def local(
    nh,
    tokens_in,
    ln1_gain,
    ln1_bias,
    w_qkv,
    b_qkv,
    feat_q,
    feat_k,
    w_out,
    b_out,
    ln2_gain,
    ln2_bias,
    w_fc,
    b_fc,
    w_proj,
    b_proj,
    seq_lengths,
    cotangent,
):
    T = tokens_in.shape[0]
    w_qkv_t = jnp.transpose(w_qkv, (1, 2, 0)).reshape(QKV, D)
    out = layer_call(
        nh,
        T,
        seq_lengths,
        tokens_in,
        cotangent,
        ln1_gain,
        ln1_bias,
        b_out,
        ln2_gain,
        ln2_bias,
        b_proj,
        b_fc,
        b_qkv,
        feat_q,
        feat_k,
        w_qkv_t,
        w_out,
        w_fc,
        w_proj,
    )
    res, gin, g_w_qkv, g_w_out, g_w_fc, g_w_proj, g_fq, g_fk, g_bqkv, g_bfc, g_bproj, g_bout, *g_ln = hand_over(out)
    g_w_qkv = jnp.transpose(g_w_qkv.reshape(3, HC, D), (2, 0, 1))
    g_ln2g, g_ln2b, g_ln1g, g_ln1b = g_ln
    return (
        res,
        gin,
        g_ln1g,
        g_ln1b,
        g_w_qkv,
        g_bqkv,
        g_fq,
        g_fk,
        g_w_out,
        g_bout,
        g_ln2g,
        g_ln2b,
        g_w_fc,
        g_bfc,
        g_w_proj,
        g_bproj,
    )


def solution(mesh):
    n_dp = mesh.shape["dp"]
    nh = max(0, (n_dp // 8).bit_length() - 1)
    return jax.shard_map(
        functools.partial(local, nh),
        mesh=mesh,
        in_specs=(
            P(("dp", "tensor"), None),
            P(),
            P(),
            P(None, None, "tensor"),
            P(None, "tensor"),
            P("tensor", None, None),
            P("tensor", None, None),
            P("tensor", None),
            P(),
            P(),
            P(),
            P(None, "tensor"),
            P("tensor"),
            P("tensor", None),
            P(),
            P("dp", None),
            P(("dp", "tensor"), None),
        ),
        out_specs=(
            P(("dp", "tensor"), None),
            P(("dp", "tensor"), None),
            P(),
            P(),
            P(None, None, "tensor"),
            P(None, "tensor"),
            P("tensor", None, None),
            P("tensor", None, None),
            P("tensor", None),
            P(),
            P(),
            P(),
            P(None, "tensor"),
            P("tensor"),
            P("tensor", None),
            P(),
        ),
        check_vma=False,
    )
```

```python
import functools
import math

import jax
import jax.numpy as jnp
from jax import lax
from jax.experimental import pallas as pl
from jax.experimental.pallas import tpu as pltpu
from jax.sharding import PartitionSpec as P

NORM_EPS = 1e-05
BF = jnp.bfloat16
F32 = jnp.float32
MESH = pl.DeviceIdType.MESH
NT = 4
D = 768
HD = 64
HPG = 3
HC = HPG * HD
NH = NT * HPG
U = 768
AUG = 80
QKV = 3 * HC
KINDS = 3
R_W = 96
R_G = (112, 96, 96)
ROWS_G = (896, 768, 768)
CB = 256
HALF_W = (48, 48)
HALF_G = ((64, 48), (48, 48), (48, 48))


def dot(a, b, ca=1, cb=0):
    return lax.dot_general(a, b, (((ca,), (cb,)), ((), ())), preferred_element_type=F32)


def mo(value, multiple):
    return pl.multiple_of(value, multiple)


def soft_pair(logits):
    top = jnp.max(logits, axis=0, keepdims=True)
    low = jnp.min(logits, axis=0, keepdims=True)
    e_pos = jnp.exp(logits - top)
    e_neg = jnp.exp(low - logits)
    p = e_pos * (1.0 / jnp.sum(e_pos, axis=0, keepdims=True))
    m = e_neg * (1.0 / jnp.sum(e_neg, axis=0, keepdims=True))
    return jnp.concatenate([p, m], axis=0)


def norm_stats(rows):
    mean = jnp.mean(rows, axis=-1, keepdims=True)
    centred = rows - mean
    var = jnp.mean(centred * centred, axis=-1, keepdims=True)
    inv = lax.rsqrt(var + NORM_EPS)
    return centred * inv, inv


def col(n):
    return pl.ds(mo(n * CB, CB), CB)


def layer_kernel(
    nh,
    seq_ref,
    x_ref,
    cot_ref,
    ln1g_in,
    ln1b_in,
    bout_in,
    ln2g_in,
    ln2b_in,
    bproj_in,
    bfc_in,
    bqkv_in,
    fq_in,
    fk_in,
    a_own,
    a_out,
    b_own,
    c_own,
    res_ref,
    gin_ref,
    oa_ref,
    oo_ref,
    ob_ref,
    oc_ref,
    gfq_ref,
    gfk_ref,
    gbqkv_ref,
    gbfc_ref,
    gbproj_ref,
    gbout_ref,
    gln2g_ref,
    gln2b_ref,
    gln1g_ref,
    gln1b_ref,
    WA,
    WB,
    WC,
    FT,
    BP,
    R0A,
    R0B,
    R0C,
    RAA,
    RAB,
    RAC,
    RBA,
    RBB,
    RBC,
    ZRA,
    ZRB,
    ZRC,
    OA,
    OB,
    OC,
    RHA,
    RHB,
    RHC,
    LS,
    LR,
    LZ,
    N1,
    QK,
    VA,
    QF,
    KF,
    NM,
    ST,
    CT,
    CR,
    SQ,
    GR,
    MX,
    DI,
    MID,
    N2,
    N2T,
    UN,
    GN2,
    GML,
    ACT,
    ACTT,
    GP,
    GBF,
    GA,
    GC,
    GQ,
    VS,
    PV,
    ft_own,
    bp_own,
    own_s,
    sm_s,
    sm_r,
    wz_s,
    w_s,
    w_r,
    g_s,
    g_r,
    z_r,
    o_s,
    o_r,
    h_s,
    h_r,
    l_s,
    l_r,
    lz_s,
    lz_r,
    c_s,
    c_r,
):
    dp = lax.axis_index("dp")
    z = lax.axis_index("tensor")
    T = x_ref.shape[0]
    NB = T // CB
    core = lax.rem(dp, 2)
    bx = lax.rem(dp // 2, 2)
    by = lax.rem(dp // 4, 2)
    d_core = 1 - 2 * core
    d_x = 2 * (1 - 2 * bx)
    d_y = 4 * (1 - 2 * by)
    slot = core * 4 + by * 2 + bx

    W = (WA, WB, WC)
    OWN = (a_own, b_own, c_own)
    R0 = (R0A, R0B, R0C)
    RA = (RAA, RAB, RAC)
    RB = (RBA, RBB, RBC)
    ZR = (ZRA, ZRB, ZRC)
    O = (OA, OB, OC)
    RH = (RHA, RHB, RHC)

    near = z + 1 - 2 * lax.rem(z, 2)
    mid = 2 - z // 2
    far = 3 * (1 - z // 2)
    is_outer = jnp.logical_or(z == 0, z == NT - 1)
    is_inner = jnp.logical_and(z > 0, z < NT - 1)

    def choose(j, groups):
        out = groups[-1]
        for i in range(NT - 2, -1, -1):
            out = jnp.where(j == i, groups[i], out)
        return out

    def wo(j):
        return choose(j, (z, near, mid, far))

    def ff(j):
        return choose(j, (z, far, mid, near))

    def last(t):
        return choose(t, (far, mid, near, z))

    def high(i):
        step = 8 * 2**i
        return dp + step * (1 - 2 * lax.rem(dp // step, 2))

    def rcopy(src, dst, ssem, rsem, dev):
        return pltpu.make_async_remote_copy(
            src_ref=src, dst_ref=dst, send_sem=ssem, recv_sem=rsem, device_id=dev, device_id_type=MESH
        )

    dev_x = (dp + d_x, z)
    dev_y = (dp + d_y, z)
    dev_c = (dp + d_core, z)
    slot_x = core * 4 + by * 2 + (1 - bx)
    slot_y = core * 4 + (1 - by) * 2 + bx
    slot_d = core * 4 + (1 - by) * 2 + (1 - bx)

    for i, ref in enumerate((ln1g_in, ln1b_in, bout_in, ln2g_in, ln2b_in, bproj_in)):
        PV[i] = ref[...].reshape(1, D)
    ln1g_ref, ln1b_ref, bout_ref, ln2g_ref, ln2b_ref, bproj_ref = (PV.at[i] for i in range(6))
    bp_own[...] = jnp.zeros_like(bp_own)
    bp_own[0:3, 0:HC] = bqkv_in[...]
    bp_own[3:4, :] = bfc_in[...].reshape(1, D)
    for h in range(HPG):
        ft_own[h * HD : (h + 1) * HD, :] = jnp.concatenate([fq_in[h], fk_in[h]], axis=1)

    peers = [(dp + d_core, z), (dp + d_x, z), (dp + d_y, z)]
    peers += [(high(i), z) for i in range(nh)]
    peers += [(dp, lax.rem(z + o, NT)) for o in range(1, NT)]
    barrier = pltpu.get_barrier_semaphore()
    for peer in peers:
        pl.semaphore_signal(barrier, inc=1, device_id=peer, device_id_type=MESH)
    pl.semaphore_wait(barrier, len(peers))

    def wrows(k, g, s):
        return W[k].at[g, pl.ds(mo(s * R_W, R_W), R_W), :]

    def wrows4(k, g, c):
        return W[k].at[g, pl.ds(mo(c * 4 * R_W, R_W), 4 * R_W), :]

    def whalf(k, g, s, h):
        return W[k].at[g, pl.ds(mo(s * R_W + h * HALF_W[0], 16), HALF_W[h]), :]

    def z_next(g):
        return jnp.where(g < z, z + 1, z - 1)

    def own_rows(k):
        at = pl.ds(mo(slot * R_W, R_W), R_W)
        if k:
            return ((slot >= 0, OWN[k].at[at, :]),)
        split = QKV // R_W
        low = jnp.where(slot < split, slot, 0)
        high = jnp.where(slot < split, 0, slot - split)
        return (
            (slot < split, a_own.at[pl.ds(mo(low * R_W, R_W), R_W), :]),
            (slot >= split, a_out.at[pl.ds(mo(high * R_W, R_W), R_W), :]),
        )

    def w_z(k):
        for here, src in own_rows(k):

            @pl.when(jnp.logical_and(here, z < NT - 1))
            def _():
                rcopy(src, wrows(k, z, slot), wz_s.at[k, 0], w_r.at[0, k, z], (dp, z + 1)).start()

            @pl.when(jnp.logical_and(here, z > 0))
            def _():
                rcopy(src, wrows(k, z, slot), wz_s.at[k, 1], w_r.at[0, k, z], (dp, z - 1)).start()

    def w_wait(k, g, stage, ref):
        rcopy(ref, ref, w_s.at[0, k, g], w_r.at[stage, k, g], dev_c).wait_recv()

    def w_send(k, g, s_stage, r_stage, ref, dev):
        rcopy(ref, ref, w_s.at[s_stage, k, g], w_r.at[r_stage, k, g], dev).start()

    def w_0(k, g):
        mine = wrows(k, g, slot)
        w_wait(k, g, 0, mine)

        @pl.when(is_inner)
        def _():
            w_send(k, g, 5, 0, mine, (dp, z_next(g)))

    def w_1(k, g):
        mine = wrows(k, g, slot)
        w_send(k, g, 0, 1, mine, dev_x)
        w_send(k, g, 1, 2, mine, dev_y)

    def w_2(k, g):
        w_wait(k, g, 1, wrows(k, g, slot_x))
        w_send(k, g, 2, 3, whalf(k, g, slot_x, 0), dev_y)
        w_wait(k, g, 2, wrows(k, g, slot_y))
        w_send(k, g, 3, 4, whalf(k, g, slot_y, 1), dev_x)
        for i, s in enumerate((slot, slot_x, slot_y)):
            w_send(k, g, 6 + i, 5 + i, wrows(k, g, s), dev_c)

    def w_3(k, g):
        w_wait(k, g, 3, whalf(k, g, slot_d, 0))
        w_wait(k, g, 4, whalf(k, g, slot_d, 1))
        w_send(k, g, 4, 8, wrows(k, g, slot_d), dev_c)

    def w_4(k, g):
        for i, s in enumerate((slot, slot_x, slot_y, slot_d)):
            w_wait(k, g, 5 + i, wrows(k, g, s + (1 - 2 * core) * 4))
        for i in range(3):
            rcopy(wrows(k, g, slot), wrows(k, g, slot), w_s.at[6 + i, k, g], w_r.at[0, k, g], dev_c).wait_send()
        sent = [wrows(k, g, slot)] * 2 + [whalf(k, g, slot_x, 0), whalf(k, g, slot_y, 1), wrows(k, g, slot_d)]
        for st, ref in enumerate(sent):
            rcopy(ref, ref, w_s.at[st, k, g], w_r.at[0, k, g], dev_c).wait_send()

        @pl.when(is_inner)
        def _():
            mine = wrows(k, g, slot)
            rcopy(mine, mine, w_s.at[5, k, g], w_r.at[0, k, g], dev_c).wait_send()

    def w_z_done(k):
        src = own_rows(k)[0][1]

        @pl.when(z < NT - 1)
        def _():
            rcopy(src, wrows(k, z, slot), wz_s.at[k, 0], w_r.at[0, k, z], (dp, z + 1)).wait_send()

        @pl.when(z > 0)
        def _():
            rcopy(src, wrows(k, z, slot), wz_s.at[k, 1], w_r.at[0, k, z], (dp, z - 1)).wait_send()

    small = ((ft_own, FT), (bp_own, BP))

    def small_send():
        for i, (own, buf) in enumerate(small):
            for o in range(1, NT):
                rcopy(own, buf.at[z], sm_s.at[i, o - 1], sm_r.at[i, z], (dp, lax.rem(z + o, NT))).start()

    def small_wait(g):
        for i, (own, buf) in enumerate(small):
            rcopy(own, buf.at[g], sm_s.at[i, 0], sm_r.at[i, g], (dp, z)).wait_recv()

    def small_done():
        for i, (own, buf) in enumerate(small):
            for o in range(1, NT):
                rcopy(own, buf.at[z], sm_s.at[i, o - 1], sm_r.at[i, z], (dp, lax.rem(z + o, NT))).wait_send()

    local = [
        pltpu.make_async_copy(ft_own, FT.at[z], own_s.at[0]),
        pltpu.make_async_copy(bp_own, BP.at[z], own_s.at[1]),
        pltpu.make_async_copy(a_own, WA.at[z, pl.ds(0, QKV), :], own_s.at[2]),
        pltpu.make_async_copy(a_out, WA.at[z, pl.ds(QKV, HC), :], own_s.at[5]),
        pltpu.make_async_copy(b_own, WB.at[z], own_s.at[3]),
        pltpu.make_async_copy(c_own, WC.at[z], own_s.at[4]),
    ]
    small_send()
    w_z(0)

    @pl.when(is_outer)
    def _():
        w_z(1)
        w_z(2)

    for copy in local:
        copy.start()

    def grows(k, g, s, n=1):
        return W[k].at[g, pl.ds(mo(s * R_G[k], 16), n * R_G[k]), :]

    def add_rows(dst, start, src, n):
        blk = 16 if n % 32 else 32

        def body(i, _):
            at = pl.ds(mo(start + i * blk, 16), blk)
            dst[at, :] = (dst[at, :].astype(F32) + src[pl.ds(mo(i * blk, 16), blk), :].astype(F32)).astype(BF)
            return 0

        lax.fori_loop(0, n // blk, body, 0)

    def ghalf(k, g, s, h):
        return W[k].at[g, pl.ds(mo(s * R_G[k] + h * HALF_G[k][0], 16), HALF_G[k][h]), :]

    def ra(k, g, h):
        return RA[k].at[g, pl.ds(h * HALF_G[k][0], HALF_G[k][h]), :]

    def g_wait(k, g, stage, ref):
        rcopy(ref, ref, g_s.at[0, k, g], g_r.at[stage, k, g], dev_c).wait_recv()

    def g_send(k, g, stage, src, dst, dev):
        rcopy(src, dst, g_s.at[stage, k, g], g_r.at[stage, k, g], dev).start()

    def g_core(k, g):
        g_send(k, g, 0, grows(k, g, (1 - core) * 4, 4), R0[k].at[g], dev_c)

    def g_a(k, g):
        g_wait(k, g, 0, R0[k].at[g])
        add_rows(W[k].at[g], core * 4 * R_G[k], R0[k].at[g], 4 * R_G[k])
        g_send(k, g, 1, ghalf(k, g, slot_d, 0), ra(k, g, 0), dev_x)
        g_send(k, g, 2, ghalf(k, g, slot_d, 1), ra(k, g, 1), dev_y)

    def g_b(k, g):
        g_wait(k, g, 1, ra(k, g, 0))
        add_rows(W[k].at[g], slot_y * R_G[k], ra(k, g, 0), HALF_G[k][0])
        g_send(k, g, 4, grows(k, g, slot_y), RB[k].at[g, 1], dev_y)
        g_wait(k, g, 2, ra(k, g, 1))
        add_rows(W[k].at[g], slot_x * R_G[k] + HALF_G[k][0], ra(k, g, 1), HALF_G[k][1])
        g_send(k, g, 3, grows(k, g, slot_x), RB[k].at[g, 0], dev_x)

    def g_y(k, g):
        for i in range(2):
            g_wait(k, g, 3 + i, RB[k].at[g, i])
            add_rows(W[k].at[g], slot * R_G[k], RB[k].at[g, i], R_G[k])

    def z_send(k, g):
        @pl.when(z < g)
        def _():
            rcopy(grows(k, g, slot), ZR[k].at[g], g_s.at[5, k, g], z_r.at[k, g], (dp, z + 1)).start()

        @pl.when(z > g)
        def _():
            at = jnp.where(z - 1 == g, NT, g)
            rcopy(grows(k, g, slot), ZR[k].at[at], g_s.at[5, k, g], z_r.at[k, at], (dp, z - 1)).start()

    def z_add(k, g, at):
        ref = ZR[k].at[at]
        rcopy(ref, ref, g_s.at[0, k, 0], z_r.at[k, at], dev_c).wait_recv()
        add_rows(W[k].at[g], slot * R_G[k], ref, R_G[k])

    def z_out(k, g):
        @pl.when(is_outer)
        def _():
            z_send(k, g)

    def z_in(k, g):
        @pl.when(is_inner)
        def _():
            z_add(k, g, g)
            z_send(k, g)

    def g_done(k, g):
        one = grows(k, g, 0)
        sent = [grows(k, g, 0, 4), ghalf(k, g, 0, 0), ghalf(k, g, 0, 1), one, one]
        for st, ref in enumerate(sent):
            rcopy(ref, ref, g_s.at[st, k, g], g_r.at[0, k, g], dev_c).wait_send()

        @pl.when(g != z)
        def _():
            rcopy(one, one, g_s.at[5, k, g], g_r.at[0, k, g], dev_c).wait_send()

    def orows(k, s, n=1):
        return O[k].at[pl.ds(mo(s * R_G[k], 16), n * R_G[k]), :]

    def ohalf(k, s, h):
        return O[k].at[pl.ds(mo(s * R_G[k] + h * HALF_G[k][0], 16), HALF_G[k][h]), :]

    def o_wait(k, stage, ref):
        rcopy(ref, ref, o_s.at[stage, k], o_r.at[stage, k], dev_c).wait_recv()

    def o_send(k, stage, ref, dev):
        rcopy(ref, ref, o_s.at[stage, k], o_r.at[stage, k], dev).start()

    def g_sum(k):
        @pl.when(z > 0)
        def _():
            z_add(k, z, z)

        @pl.when(z < NT - 1)
        def _():
            z_add(k, z, NT)

        O[k][pl.ds(mo(slot * R_G[k], 16), R_G[k]), :] = W[k][z, pl.ds(mo(slot * R_G[k], 16), R_G[k]), :]
        for i in range(nh):
            rcopy(orows(k, slot), RH[k].at[i], h_s.at[i, k], h_r.at[i, k], (high(i), z)).start()
            rcopy(orows(k, slot), RH[k].at[i], h_s.at[i, k], h_r.at[i, k], (high(i), z)).wait()
            add_rows(O[k], slot * R_G[k], RH[k].at[i], R_G[k])
        o_send(k, 0, orows(k, slot), dev_x)
        o_send(k, 1, orows(k, slot), dev_y)

    def o_2(k):
        o_wait(k, 0, orows(k, slot_x))
        o_send(k, 2, ohalf(k, slot_x, 0), dev_y)
        o_wait(k, 1, orows(k, slot_y))
        o_send(k, 3, ohalf(k, slot_y, 1), dev_x)
        for i, s in enumerate((slot, slot_x, slot_y)):
            o_send(k, 4 + i, orows(k, s), dev_c)

    def o_3(k):
        o_wait(k, 2, ohalf(k, slot_d, 0))
        o_wait(k, 3, ohalf(k, slot_d, 1))
        o_send(k, 7, orows(k, slot_d), dev_c)

    def o_4(k):
        slots = (slot, slot_x, slot_y, slot_d)
        for i, s in enumerate(slots):
            o_wait(k, 4 + i, orows(k, s + (1 - 2 * core) * 4))
        sent = [orows(k, slot)] * 2 + [ohalf(k, slot_x, 0), ohalf(k, slot_y, 1)] + [orows(k, s) for s in slots]
        for st, ref in enumerate(sent):
            rcopy(ref, ref, o_s.at[st, k], o_r.at[0, k], dev_c).wait_send()

    def write(src, dst, sem):
        copy = pltpu.make_async_copy(src, dst, sem)
        copy.start()
        return copy

    def iota(shape, axis):
        return lax.broadcasted_iota(jnp.int32, shape, axis)

    causal = iota((CB, CB), 0) <= iota((CB, CB), 1)
    aug_tail = jnp.where(iota((16, T), 0) < 2, 1.0, 0.0).astype(BF)
    ones_rows = jnp.ones((16, T), BF)
    head_mask = (iota((HC, HC), 0) // HD) == (iota((HC, HC), 1) // HD)

    def pick(which):
        r = iota((2 * HD, HC), 0) - which * HD
        return (r == lax.rem(iota((2 * HD, HC), 1), HD)).astype(BF)

    def pick_back(which):
        r = iota((HC, 2 * HD), 1) - which * HD
        return (r == lax.rem(iota((HC, 2 * HD), 0), HD)).astype(BF)

    def block_diag(g, which):
        return jnp.where(head_mask, dot(FT[g], pick(which)), 0.0).astype(BF)

    first_end = seq_ref[0, 0]
    second_end = seq_ref[0, 0] + seq_ref[0, 1]

    def seq_id(zz):
        start = zz * T
        return (start >= first_end).astype(jnp.int32) + (start >= second_end).astype(jnp.int32)

    from_prev = jnp.logical_and(z > 0, seq_id(z) == seq_id(z - 1))
    from_next = jnp.logical_and(z < NT - 1, seq_id(z) == seq_id(z + 1))

    RB_ = 64

    def p0(i, _):
        at = pl.ds(mo(i * RB_, RB_), RB_)
        xh, _inv = norm_stats(x_ref[at, :].astype(F32))
        N1[at, :] = (xh * ln1g_ref[...] + ln1b_ref[...]).astype(BF)
        return 0

    lax.fori_loop(0, T // RB_, p0, 0)
    for g in range(NT):
        WA[g, pl.ds(D, ROWS_G[0] - D), :] = jnp.zeros((ROWS_G[0] - D, D), BF)
    GQ[pl.ds(QKV, D - QKV), :] = jnp.zeros((D - QKV, T), BF)

    @pl.when(z == 0)
    def _():
        CR[...] = jnp.zeros_like(CR)

    @pl.when(z == NT - 1)
    def _():
        GR[...] = jnp.zeros_like(GR)

    for copy in local[:4]:
        copy.wait()

    def chain_wait(buf, g, stage):
        rcopy(buf.at[g], buf.at[g], c_s.at[stage, g], c_r.at[stage, g], (dp, z)).wait_recv()

    def chain_send(g):
        rcopy(SQ.at[g], CR.at[g], c_s.at[0, g], c_r.at[0, g], (dp, z + 1)).start()

    def chain_pass(g):
        chain_wait(CR, g, 0)
        for h in range(HPG):
            carried = jnp.where(from_prev, CR[g, h].astype(F32), 0.0)
            SQ[g, h] = (ST[g * HPG + h] + carried).astype(BF)
        chain_send(g)

    def p1(j, _):
        g = wo(j)

        @pl.when(j == 1)
        def _():
            w_0(0, near)
            w_1(0, near)
            small_wait(near)

            @pl.when(is_inner)
            def _():
                w_0(0, mid)
                w_1(0, mid)
                w_0(1, near)
                w_2(0, near)
                w_0(0, far)
                w_1(0, far)
                w_0(2, near)
                w_0(1, far)
                w_2(0, mid)
                w_3(0, near)

            @pl.when(is_outer)
            def _():
                w_2(0, near)
                w_0(0, mid)
                w_1(0, mid)
                w_3(0, near)
                w_0(0, far)
                w_1(0, far)

            w_4(0, near)

        @pl.when(j == 2)
        def _():
            small_wait(mid)

            @pl.when(is_inner)
            def _():
                w_0(2, far)
                w_z(1)
                w_z(2)
                w_2(0, far)
                w_3(0, mid)
                w_1(1, far)
                w_1(2, far)

            @pl.when(is_outer)
            def _():
                w_2(0, mid)
                w_0(1, far)
                w_2(0, far)
                w_1(1, far)
                w_3(0, mid)
                w_0(2, far)
                w_1(2, far)

            w_4(0, mid)

        @pl.when(j == 3)
        def _():
            small_wait(far)
            w_3(0, far)

            @pl.when(is_inner)
            def _():
                w_0(1, mid)

            w_4(0, far)

        bias = jnp.transpose(BP[g, :, 0:256])
        bias = jnp.concatenate([bias[:HC, i : i + 1] for i in range(3)], axis=0)
        qkv = (dot(WA[g, pl.ds(0, QKV), :], N1[...], 1, 1) + bias).astype(BF)
        QK[g] = qkv[: 2 * HC]
        ql = dot(block_diag(g, 0), qkv[:HC], 0, 0)
        kl = dot(block_diag(g, 1), qkv[HC : 2 * HC], 0, 0)
        for h in range(HPG):
            hh = g * HPG + h
            rows = slice(h * HD, (h + 1) * HD)
            qf = soft_pair(ql[rows]).astype(BF)
            kf = soft_pair(kl[rows]).astype(BF)
            va = jnp.concatenate([qkv[2 * HC + h * HD : 2 * HC + (h + 1) * HD], aug_tail], axis=0)
            QF[hh] = qf
            KF[hh] = kf
            VA[hh] = va
            kn = kf.T
            ST[hh] = dot(va, kn)
            for qi in range(NB):
                qs = slice(qi * CB, (qi + 1) * CB)
                acc = None
                for ki in range(qi + 1):
                    ks = slice(ki * CB, (ki + 1) * CB)
                    s = dot(kn[ks], qf[:, qs])
                    if ki == qi:
                        s = jnp.where(causal, s, 0.0)
                    part = dot(va[:, ks], s.astype(BF))
                    acc = part if acc is None else acc + part
                NM[hh, :, qs] = acc[: HD + 8]

        @pl.when(z == 0)
        def _():
            for h in range(HPG):
                SQ[g, h] = ST[g * HPG + h].astype(BF)
            chain_send(g)

        for zz, jj, ready in ((1, 1, (0, 1)), (1, 2, (2,)), (2, 2, (1,))):

            @pl.when(jnp.logical_and(z == zz, j == jj))
            def _():
                for gg in ready:
                    chain_pass(gg)

        return 0

    lax.fori_loop(0, NT, p1, 0)
    @pl.when(is_inner)
    def _():
        w_0(2, mid)

    w_2(1, far)

    @pl.when(z == 1)
    def _():
        chain_pass(3)

    @pl.when(z == 2)
    def _():
        chain_pass(0)
        chain_pass(2)

    @pl.when(is_outer)
    def _():
        w_0(1, near)

    w_2(2, far)
    w_1(1, near)

    @pl.when(is_outer)
    def _():
        w_0(2, near)

    w_1(2, near)

    @pl.when(z == 2)
    def _():
        chain_pass(3)

    def p1b(g, _):
        @pl.when(z == NT - 1)
        def _():
            chain_wait(CR, g, 0)

        for h in range(HPG):
            CT[g * HPG + h] = jnp.where(from_prev, CR[g, h], jnp.zeros((AUG, 2 * HD), BF))
        return 0

    lax.fori_loop(0, NT, p1b, 0)

    def p1c(g, _):
        for h in range(HPG):
            hh = g * HPG + h
            num = NM[hh] + dot(CT[hh], QF[hh])[: HD + 8]
            inv = 1.0 / num[HD : HD + 1]
            DI[hh] = inv
            MX[g, pl.ds(h * HD, HD), :] = (num[:HD] * inv).astype(BF)
        return 0

    lax.fori_loop(0, NT, p1c, 0)
    w_3(1, far)
    w_3(2, far)

    def p2(n, _):
        acc = None
        for g in range(NT):
            part = dot(MX[g], WA[g, pl.ds(QKV, HC), col(n)], 0, 0)
            acc = part if acc is None else acc + part
        MID[:, col(n)] = x_ref[:, col(n)].astype(F32) + (acc + bout_ref[:, col(n)])
        return 0

    lax.fori_loop(0, D // CB, p2, 0)

    def p2b(i, _):
        at = pl.ds(mo(i * 128, 128), 128)
        xh, _inv = norm_stats(MID[at, :])
        n2 = (xh * ln2g_ref[...] + ln2b_ref[...]).astype(BF)
        N2[at, :] = n2
        N2T[:, at] = n2.T
        return 0

    lax.fori_loop(0, T // 128, p2b, 0)
    for k in (1, 2):

        @pl.when(is_outer)
        def _():
            w_0(k, mid)

        w_1(k, mid)

    w_2(1, near)
    w_2(2, near)

    @pl.when(z < NT - 1)
    def _():
        for g in range(NT):
            rcopy(SQ.at[g], SQ.at[g], c_s.at[0, g], c_r.at[0, g], (dp, z)).wait_send()

    UN[...] = jnp.zeros_like(UN)
    GN2[...] = jnp.zeros_like(GN2)
    for copy in local[4:]:
        copy.wait()

    cc = math.sqrt(2.0 / math.pi)

    def p3(j, _):
        g = ff(j)

        @pl.when(j > 0)
        def _():
            w_4(1, g)
            w_4(2, g)

        def units(u, total):
            pre = dot(N2[...], WB[g, :, col(u)]) + BP[g, pl.ds(3, 1), col(u)]
            sq = pre * pre
            t = jnp.tanh(cc * pre * (1.0 + 0.044715 * sq))
            act = (0.5 * pre * (1.0 + t)).astype(BF)
            slope = 0.5 * (1.0 + t) + (0.5 * cc) * pre * (1.0 - t * t) * (1.0 + (3 * 0.044715) * sq)
            ACT[:, col(u)] = act
            ACTT[col(u), :] = act.T
            gact = dot(cot_ref[...], WC[g, col(u), :], 1, 1)
            gpre = (gact * slope).astype(BF)
            GP[:, col(u)] = gpre
            GBF[g, :, col(u)] = jnp.sum(gpre.astype(F32), axis=0, keepdims=True)
            return total

        lax.fori_loop(0, U // CB, units, 0)

        @pl.when(j >= 1)
        def _():
            g_a(1, ff(j - 1))
            g_a(2, ff(j - 1))

        @pl.when(j == 1)
        def _():
            w_3(1, near)
            w_3(2, near)
            w_3(1, mid)
            w_3(2, mid)

        @pl.when(j == 2)
        def _():
            g_b(1, z)
            g_b(2, z)

        def outs(n, _):
            UN[:, col(n)] += dot(ACT[...], WC[g, :, col(n)])
            GN2[:, col(n)] += dot(GP[...], WB[g, col(n), :], 1, 1)
            return 0

        lax.fori_loop(0, D // CB, outs, 0)

        @pl.when(j == 0)
        def _():
            w_2(1, mid)
            w_2(2, mid)

        def grads(n, _):
            WC[g, col(n), :] = dot(ACTT[col(n), :], cot_ref[...]).astype(BF)
            WB[g, col(n), :] = dot(N2T[col(n), :], GP[...]).astype(BF)
            return 0

        lax.fori_loop(0, D // CB, grads, 0)
        g_core(1, g)
        g_core(2, g)

        return 0

    lax.fori_loop(0, NT, p3, 0)
    g_b(1, far)
    g_b(2, far)

    VS[...] = jnp.zeros_like(VS)

    def p4(i, _):
        at = pl.ds(mo(i * RB_, RB_), RB_)
        mid = MID[at, :]
        res_ref[at, :] = (mid + UN[at, :] + bproj_ref[...]).astype(BF)
        xh, inv = norm_stats(mid)
        gn = GN2[at, :]
        gh = gn * ln2g_ref[...]
        c1 = jnp.mean(gh, axis=-1, keepdims=True)
        c2 = jnp.mean(gh * xh, axis=-1, keepdims=True)
        cot = cot_ref[at, :].astype(F32)
        gm = cot + inv * (gh - c1 - xh * c2)
        GN2[at, :] = gm
        low = gm.astype(BF)
        GML[at, :] = low
        VS[0] += jnp.sum(cot, axis=0, keepdims=True)
        VS[1] += jnp.sum(low.astype(F32), axis=0, keepdims=True)
        VS[2] += jnp.sum(gn * xh, axis=0, keepdims=True)
        VS[3] += jnp.sum(gn, axis=0, keepdims=True)
        return 0

    lax.fori_loop(0, T // RB_, p4, 0)
    g_a(1, near)
    g_a(2, near)

    tail_row = iota((16, T), 0)

    def p5a(g, _):
        gmix = dot(WA[g, pl.ds(QKV, HC), :], GML[...], 1, 1).astype(BF).astype(F32)
        mix = MX[g]
        WA[g, pl.ds(QKV, HC), :] = dot(mix, GML[...]).astype(BF)
        prod = gmix * mix.astype(F32)
        for h in range(HPG):
            hh = g * HPG + h
            rows = slice(h * HD, (h + 1) * HD)
            inv = DI[hh]
            gden = -jnp.sum(prod[rows], axis=0, keepdims=True) * inv
            hi = gden.astype(BF).astype(F32)
            lo = gden - hi
            tail = jnp.where(tail_row == 0, hi, jnp.where(tail_row == 1, lo, 0.0)).astype(BF)
            ga = jnp.concatenate([(gmix[rows] * inv).astype(BF), tail], axis=0)
            GA[hh] = ga
            gc = dot(ga, QF[hh].T)
            GC[hh] = gc
            SQ[g, h] = gc.astype(BF)

        @pl.when(z == NT - 1)
        def _():
            rcopy(SQ.at[g], GR.at[g], c_s.at[1, g], c_r.at[1, g], (dp, z - 1)).start()

        return 0

    lax.fori_loop(0, NT, p5a, 0)

    def chain_back(g, _):
        @pl.when(z < NT - 1)
        def _():
            chain_wait(GR, g, 1)
            for h in range(HPG):
                hh = g * HPG + h
                later = jnp.where(from_next, GR[g, h].astype(F32), 0.0)
                SQ[g, h] = (GC[hh] + later).astype(BF)

        @pl.when(jnp.logical_and(z > 0, z < NT - 1))
        def _():
            rcopy(SQ.at[g], GR.at[g], c_s.at[1, g], c_r.at[1, g], (dp, z - 1)).start()

        return 0

    GN1 = UN
    GN1[...] = jnp.zeros_like(GN1)

    def back(feat, grads):
        out = []
        for b in range(NB):
            bs = slice(b * CB, (b + 1) * CB)
            p = feat[:HD, bs].astype(F32)
            m = feat[HD:, bs].astype(F32)
            g1 = grads[b][:HD]
            g2 = grads[b][HD:]
            s1 = jnp.sum(g1 * p, axis=0, keepdims=True)
            s2 = jnp.sum(g2 * m, axis=0, keepdims=True)
            out.append((p * (g1 - s1) - m * (g2 - s2)).astype(BF))
        return jnp.concatenate(out, axis=1)

    def p5b(t, _):
        g = last(t)
        gql = []
        gkl = []
        for h in range(HPG):
            hh = g * HPG + h
            qf = QF[hh]
            kf = KF[hh]
            va = VA[hh]
            ga = GA[hh]
            kn = kf.T
            vn = va.T
            ctt = CT[hh].T
            gq = [None] * NB
            gk = [None] * NB
            gv = [None] * NB
            for qi in range(NB):
                qs = slice(qi * CB, (qi + 1) * CB)
                gq[qi] = dot(ctt, ga[:, qs])
                for ki in range(qi + 1):
                    ks = slice(ki * CB, (ki + 1) * CB)
                    s = dot(kn[ks], qf[:, qs])
                    gs = dot(vn[ks], ga[:, qs])
                    if ki == qi:
                        s = jnp.where(causal, s, 0.0)
                        gs = jnp.where(causal, gs, 0.0)
                    s = s.astype(BF)
                    gs = gs.astype(BF)
                    gq[qi] = gq[qi] + dot(kf[:, ks], gs)
                    pk = dot(qf[:, qs], gs, 1, 1)
                    pv = dot(ga[:, qs], s, 1, 1)[:HD]
                    gk[ki] = pk if gk[ki] is None else gk[ki] + pk
                    gv[ki] = pv if gv[ki] is None else gv[ki] + pv
            for ki in range(NB):
                ks = slice(ki * CB, (ki + 1) * CB)
                NM[3 * h, :HD, ks] = gk[ki][:HD]
                NM[3 * h + 1, :HD, ks] = gk[ki][HD:]
                NM[3 * h + 2, :HD, ks] = gv[ki]
            gql.append(back(qf, gq))

        @pl.when(t == 0)
        def _():
            lax.fori_loop(0, NT, chain_back, 0)
            for k in (1, 2):
                g_b(k, mid)
                g_y(k, z)
                g_y(k, far)

        @pl.when(t >= 1)
        def _():
            g_a(0, last(t - 1))

        @pl.when(t == 1)
        def _():
            g_b(1, near)
            g_b(2, near)

        @pl.when(t >= 2)
        def _():
            g_b(0, last(t - 2))

        for k in (1, 2):

            @pl.when(t == 2)
            def _():
                z_in(k, far)

            @pl.when(t == 3)
            def _():
                z_in(k, mid)

        @pl.when(t == 3)
        def _():
            g_y(0, far)
            z_out(0, far)

        for h in range(HPG):
            hh = g * HPG + h
            kf = KF[hh]
            va = VA[hh]
            gkc = jnp.where(from_next, GR[g, h], jnp.zeros((AUG, 2 * HD), BF))
            gkt = gkc.T
            gk = [None] * NB
            for ki in range(NB):
                ks = slice(ki * CB, (ki + 1) * CB)
                gk[ki] = jnp.concatenate([NM[3 * h, :HD, ks], NM[3 * h + 1, :HD, ks]], axis=0) + dot(gkt, va[:, ks])
                gv = NM[3 * h + 2, :HD, ks] + dot(gkc[:HD], kf[:, ks])
                GQ[pl.ds(2 * HC + h * HD, HD), ks] = gv.astype(BF)
            gkl.append(back(kf, gk))

        comp = None
        for which, parts in ((0, gql), (1, gkl)):
            glog = jnp.concatenate(parts, axis=0)
            own = QK[g, pl.ds(which * HC, HC), :]
            GQ[pl.ds(which * HC, HC), :] = dot(block_diag(g, which), glog).astype(BF)
            gfeat = jnp.where(head_mask, dot(own, glog, 1, 1), 0.0).astype(BF)
            part = dot(gfeat, pick_back(which))
            comp = part if comp is None else comp + part
        comp = comp.astype(BF)
        gq_all = GQ[...]
        gqn = gq_all[:QKV].T
        for n in range(D // CB):
            GN1[:, n * CB : (n + 1) * CB] += dot(gqn, WA[g, pl.ds(0, QKV), n * CB : (n + 1) * CB])
        WA[g, pl.ds(0, QKV), :] = dot(gq_all[:QKV], N1[...]).astype(BF)
        for b in range(HC // 32):
            WA[g, pl.ds(D, 32), b * 128 : (b + 1) * 128] = comp[b * 32 : (b + 1) * 32]
        vec = dot(ones_rows, gq_all, 1, 1)
        row = iota((16, D), 0)
        vec = jnp.where(row == 1, GBF[g], vec)
        for i in range(4):
            vec = jnp.where(row == 2 + i, VS[i], vec)
        WA[g, pl.ds(D + 32, 16), :] = vec.astype(BF)
        g_core(0, g)

        for k in (1, 2):

            @pl.when(t == 0)
            def _():
                z_out(k, far)

            @pl.when(t == 1)
            def _():
                g_y(k, mid)
                z_out(k, mid)

            @pl.when(t == 2)
            def _():
                g_y(k, near)
                z_out(k, near)

            @pl.when(t == 3)
            def _():
                z_in(k, near)

        return 0

    lax.fori_loop(0, NT, p5b, 0)

    LS[...] = jnp.zeros_like(LS)

    def p6(i, _):
        at = pl.ds(mo(i * RB_, RB_), RB_)
        xh, inv = norm_stats(x_ref[at, :].astype(F32))
        gn = GN1[at, :]
        gh = gn * ln1g_ref[...]
        c1 = jnp.mean(gh, axis=-1, keepdims=True)
        c2 = jnp.mean(gh * xh, axis=-1, keepdims=True)
        gin_ref[at, :] = (GN2[at, :] + inv * (gh - c1 - xh * c2)).astype(BF)
        LS[0, 0:1, :] += jnp.sum(gn * xh, axis=0, keepdims=True)
        LS[0, 1:2, :] += jnp.sum(gn, axis=0, keepdims=True)
        return 0

    lax.fori_loop(0, T // RB_, p6, 0)

    partners = [dp + d_core, dp + d_x, dp + d_y] + [high(i) for i in range(nh)]

    steps = len(partners)

    def small_start(i):
        rcopy(LS.at[i], LR.at[i], l_s.at[i], l_r.at[i], (partners[i], z)).start()

    def small_end(i):
        rcopy(LS.at[i], LR.at[i], l_s.at[i], l_r.at[i], (partners[i], z)).wait()
        LS[i + 1] = LS[i] + LR[i]

    small_start(0)
    g_a(0, z)
    g_b(0, near)
    g_y(0, mid)
    z_out(0, mid)
    z_in(0, far)
    small_end(0)
    small_start(1)
    g_b(0, z)
    z_in(0, mid)
    g_y(0, near)
    z_out(0, near)
    z_in(0, near)
    small_end(1)
    small_start(2)
    g_sum(1)
    g_sum(2)
    small_end(2)
    for i in range(3, steps):
        small_start(i)
        small_end(i)
    LZ[z] = LS[steps]
    for o in range(1, NT):
        rcopy(LS.at[steps], LZ.at[z], lz_s.at[o - 1], lz_r.at[z], (dp, lax.rem(z + o, NT))).start()
    o_2(1)
    o_2(2)
    g_y(0, z)
    g_sum(0)
    o_3(1)
    o_3(2)
    o_2(0)
    o_4(1)
    outs = [write(OB, ob_ref, own_s.at[0])]
    o_4(2)
    outs.append(write(OC, oc_ref, own_s.at[1]))
    for o in range(1, NT):
        zz = lax.rem(z + o, NT)
        rcopy(LZ.at[zz], LZ.at[zz], lz_s.at[o - 1], lz_r.at[zz], (dp, z)).wait_recv()
    total = LZ[0]
    for zz in range(1, NT):
        total = total + LZ[zz]
    gln1g_ref[...] = total[0:1].reshape(D)
    gln1b_ref[...] = total[1:2].reshape(D)
    o_3(0)
    o_4(0)
    outs.append(write(OA.at[pl.ds(0, QKV), :], oa_ref, own_s.at[4]))
    outs.append(write(OA.at[pl.ds(QKV, HC), :], oo_ref, own_s.at[5]))
    for b in range(HC // 32):
        block = OA[D : D + 32, b * 128 : (b + 1) * 128].astype(F32)
        rows = slice(b % 2 * 32, b % 2 * 32 + 32)
        gfq_ref[b // 2, rows, :] = block[:, :HD]
        gfk_ref[b // 2, rows, :] = block[:, HD:]
    vec = OA[D + 32 : D + 48, :].astype(F32)
    for i in range(3):
        gbqkv_ref[i : i + 1, :] = vec[0:1, i * HC : (i + 1) * HC]
    for i, ref in enumerate((gbfc_ref, gbproj_ref, gbout_ref, gln2g_ref, gln2b_ref)):
        ref[...] = vec[i + 1 : i + 2].reshape(D)
    for copy in outs:
        copy.wait()

    for o in range(1, NT):
        rcopy(LS.at[steps], LZ.at[z], lz_s.at[o - 1], lz_r.at[z], (dp, lax.rem(z + o, NT))).wait_send()
    small_done()
    for k in range(KINDS):
        w_z_done(k)
        for g in range(NT):
            g_done(k, g)

    @pl.when(z > 0)
    def _():
        for g in range(NT):
            rcopy(SQ.at[g], SQ.at[g], c_s.at[1, g], c_r.at[1, g], (dp, z)).wait_send()


def layer_call(nh, T, *args):
    def vm(shape, dtype=BF):
        return pltpu.VMEM(shape, dtype)

    dma = pltpu.SemaphoreType.DMA
    nhb = max(nh, 1)
    nst = 3 + nh
    scratch = [
        vm((NT, ROWS_G[0], D)),
        vm((NT, D, U)),
        vm((NT, U, D)),
        vm((NT, HC, 2 * HD)),
        vm((NT, 8, D), F32),
    ]
    scratch += [vm((NT, 4 * r, D)) for r in R_G]
    scratch += [vm((NT, r, D)) for r in R_G]
    scratch += [vm((NT, 2, r, D)) for r in R_G]
    scratch += [vm((NT + 1, r, D)) for r in R_G]
    scratch += [vm((rows, D)) for rows in ROWS_G]
    scratch += [vm((nhb, r if nh else 16, D)) for r in R_G]
    scratch += [vm((nst + 1, 8, D), F32), vm((nst, 8, D), F32), vm((NT, 8, D), F32)]
    scratch += [
        vm((T, D)),
        vm((NT, 2 * HC, T)),
        vm((NH, AUG, T)),
        vm((NH, 2 * HD, T)),
        vm((NH, 2 * HD, T)),
        vm((NH, HD + 8, T), F32),
        vm((NH, AUG, 2 * HD), F32),
        vm((NH, AUG, 2 * HD)),
        vm((NT, HPG, AUG, 2 * HD)),
        vm((NT, HPG, AUG, 2 * HD)),
        vm((NT, HPG, AUG, 2 * HD)),
        vm((NT, HC, T)),
        vm((NH, 1, T), F32),
        vm((T, D), F32),
        vm((T, D)),
        vm((D, T)),
        vm((T, D), F32),
        vm((T, D), F32),
        vm((T, D)),
        vm((T, U)),
        vm((U, T)),
        vm((T, U)),
        vm((NT, 1, U), F32),
        vm((NH, AUG, T)),
        vm((NH, AUG, 2 * HD), F32),
        vm((D, T)),
        vm((4, 1, D), F32),
        vm((6, 1, D), F32),
        vm((HC, 2 * HD)),
        vm((8, D), F32),
    ]
    scratch += [
        dma((6,)),
        dma((2, NT - 1)),
        dma((2, NT)),
        dma((KINDS, 2)),
        dma((9, KINDS, NT)),
        dma((9, KINDS, NT)),
        dma((6, KINDS, NT)),
        dma((5, KINDS, NT)),
        dma((KINDS, NT + 1)),
        dma((8, KINDS)),
        dma((8, KINDS)),
        dma((nhb, KINDS)),
        dma((nhb, KINDS)),
        dma((nst,)),
        dma((nst,)),
        dma((NT - 1,)),
        dma((NT,)),
        dma((2, NT)),
        dma((2, NT)),
    ]
    vmem = pl.BlockSpec(memory_space=pltpu.VMEM)
    hbm = pl.BlockSpec(memory_space=pl.ANY)
    return pl.pallas_call(
        functools.partial(layer_kernel, nh),
        out_shape=(
            jax.ShapeDtypeStruct((T, D), BF),
            jax.ShapeDtypeStruct((T, D), BF),
            jax.ShapeDtypeStruct((QKV, D), BF),
            jax.ShapeDtypeStruct((HC, D), BF),
            jax.ShapeDtypeStruct((D, U), BF),
            jax.ShapeDtypeStruct((U, D), BF),
            jax.ShapeDtypeStruct((HPG, HD, HD), F32),
            jax.ShapeDtypeStruct((HPG, HD, HD), F32),
            jax.ShapeDtypeStruct((3, HC), F32),
            *[jax.ShapeDtypeStruct((D,), F32)] * 7,
        ),
        in_specs=[pl.BlockSpec(memory_space=pltpu.SMEM)] + [vmem] * 12 + [hbm] * 4,
        out_specs=(vmem, vmem, hbm, hbm, hbm, hbm, *[vmem] * 10),
        scratch_shapes=scratch,
        compiler_params=pltpu.CompilerParams(
            collective_id=0, has_side_effects=True, vmem_limit_bytes=67043328
        ),
    )(*args)


def hand_over(arrays):
    n = len(arrays)
    wide = (2, 3, 4, 5)
    order = (4, 5, *(i for i in range(n) if i not in wide), 2, 3)
    kinds = [F32 if i in wide else a.dtype for i, a in enumerate(arrays)]

    def body(*refs):
        taken, given, low = refs[:n], refs[n : 2 * n], refs[2 * n : 3 * n]
        high = dict(zip(wide, refs[3 * n : 3 * n + len(wide)]))
        sems = refs[3 * n + len(wide)]

        def widen(src, dst):
            def step(i, _):
                at = pl.ds(mo(i * 64, 64), 64)
                dst[at, :] = src[at, :].astype(F32)
                return 0

            lax.fori_loop(0, src.shape[0] // 64, step, 0)

        reads = [pltpu.make_async_copy(taken[i], low[i], sems.at[0, i]) for i in range(n)]
        writes = [pltpu.make_async_copy(high.get(i, low[i]), given[i], sems.at[1, i]) for i in range(n)]
        for i in order:
            reads[i].start()
        for i in order:
            reads[i].wait()
            if i in wide:
                widen(low[i], high[i])
            writes[i].start()
        for i in order:
            writes[i].wait()

    hbm = pl.BlockSpec(memory_space=pl.ANY)
    scratch = [pltpu.VMEM(a.shape, a.dtype) for a in arrays] + [pltpu.VMEM(arrays[i].shape, F32) for i in wide]
    return pl.pallas_call(
        body,
        out_shape=tuple(jax.ShapeDtypeStruct(a.shape, kind) for a, kind in zip(arrays, kinds)),
        in_specs=[hbm] * n,
        out_specs=(hbm,) * n,
        scratch_shapes=[*scratch, pltpu.SemaphoreType.DMA((2, n))],
    )(*arrays)


def local(
    nh,
    tokens_in,
    ln1_gain,
    ln1_bias,
    w_qkv,
    b_qkv,
    feat_q,
    feat_k,
    w_out,
    b_out,
    ln2_gain,
    ln2_bias,
    w_fc,
    b_fc,
    w_proj,
    b_proj,
    seq_lengths,
    cotangent,
):
    T = tokens_in.shape[0]
    w_qkv_t = jnp.transpose(w_qkv, (1, 2, 0)).reshape(QKV, D)
    out = layer_call(
        nh,
        T,
        seq_lengths,
        tokens_in,
        cotangent,
        ln1_gain,
        ln1_bias,
        b_out,
        ln2_gain,
        ln2_bias,
        b_proj,
        b_fc,
        b_qkv,
        feat_q,
        feat_k,
        w_qkv_t,
        w_out,
        w_fc,
        w_proj,
    )
    res, gin, g_w_qkv, g_w_out, g_w_fc, g_w_proj, g_fq, g_fk, g_bqkv, g_bfc, g_bproj, g_bout, *g_ln = hand_over(out)
    g_w_qkv = jnp.transpose(g_w_qkv.reshape(3, HC, D), (2, 0, 1))
    g_ln2g, g_ln2b, g_ln1g, g_ln1b = g_ln
    return (
        res,
        gin,
        g_ln1g,
        g_ln1b,
        g_w_qkv,
        g_bqkv,
        g_fq,
        g_fk,
        g_w_out,
        g_bout,
        g_ln2g,
        g_ln2b,
        g_w_fc,
        g_bfc,
        g_w_proj,
        g_bproj,
    )


def solution(mesh):
    n_dp = mesh.shape["dp"]
    nh = max(0, (n_dp // 8).bit_length() - 1)
    return jax.shard_map(
        functools.partial(local, nh),
        mesh=mesh,
        in_specs=(
            P(("dp", "tensor"), None),
            P(),
            P(),
            P(None, None, "tensor"),
            P(None, "tensor"),
            P("tensor", None, None),
            P("tensor", None, None),
            P("tensor", None),
            P(),
            P(),
            P(),
            P(None, "tensor"),
            P("tensor"),
            P("tensor", None),
            P(),
            P("dp", None),
            P(("dp", "tensor"), None),
        ),
        out_specs=(
            P(("dp", "tensor"), None),
            P(("dp", "tensor"), None),
            P(),
            P(),
            P(None, None, "tensor"),
            P(None, "tensor"),
            P("tensor", None, None),
            P("tensor", None, None),
            P("tensor", None),
            P(),
            P(),
            P(),
            P(None, "tensor"),
            P("tensor"),
            P("tensor", None),
            P(),
        ),
        check_vma=False,
    )
```
